32 devices in a mesh: dp: 8 (over z, core), fsdp: 4 (over y, x).
Axes of the slice: x: 2, y: 2, z: 4, core: 2. Of those that a mesh axis runs over, the one named last changes fastest.
Arguments:
- tokens: bfloat16 [32768, 768], P(('dp', 'fsdp')), may hold values from -6 to 6
- segments: int32 [32768], P(('dp', 'fsdp')), may hold values from -1 to 15, as said below
- cotangent: bfloat16 [32768, 768], P(('dp', 'fsdp')), may hold values from -6 to 6
- qkv_weight: bfloat16 [768, 2304], P('fsdp'), may hold values from -0.21875 to 0.21875
- qkv_bias: bfloat16 [2304], P('fsdp'), may hold values from -1.796875 to 1.796875
- out_weight: bfloat16 [768, 768], P('fsdp'), may hold values from -0.875 to 0.875
- out_bias: bfloat16 [768], P('fsdp'), may hold values from -1.796875 to 1.796875
- up_weight: bfloat16 [768, 3072], P('fsdp'), may hold values from -0.21875 to 0.21875
- up_bias: bfloat16 [3072], P('fsdp'), may hold values from -1.796875 to 1.796875
- down_weight: bfloat16 [3072, 768], P('fsdp'), may hold values from -0.109375 to 0.109375
- down_bias: bfloat16 [768], P('fsdp'), may hold values from -1.796875 to 1.796875
- first_gain: bfloat16 [768], P('fsdp'), may hold values from 0.5 to 1.5
- first_shift: bfloat16 [768], P('fsdp'), may hold values from -1.796875 to 1.796875
- second_gain: bfloat16 [768], P('fsdp'), may hold values from 0.5 to 1.5
- second_shift: bfloat16 [768], P('fsdp'), may hold values from -1.796875 to 1.796875
- query_gain: bfloat16 [64], P('fsdp'), may hold values from 0.099609375 to 1.8984375
- key_gain: bfloat16 [64], P('fsdp'), may hold values from 0.099609375 to 1.8984375
Outputs:
- out_tokens: bfloat16 [32768, 768], P(('dp', 'fsdp'))
- tokens_grad: bfloat16 [32768, 768], P(('dp', 'fsdp'))
- qkv_weight_grad: float32 [768, 2304], P('fsdp')
- qkv_bias_grad: float32 [2304], P('fsdp')
- out_weight_grad: float32 [768, 768], P('fsdp')
- out_bias_grad: float32 [768], P('fsdp')
- up_weight_grad: float32 [768, 3072], P('fsdp')
- up_bias_grad: float32 [3072], P('fsdp')
- down_weight_grad: float32 [3072, 768], P('fsdp')
- down_bias_grad: float32 [768], P('fsdp')
- first_gain_grad: float32 [768], P('fsdp')
- first_shift_grad: float32 [768], P('fsdp')
- second_gain_grad: float32 [768], P('fsdp')
- second_shift_grad: float32 [768], P('fsdp')
- query_gain_grad: float32 [64], P('fsdp')
- key_gain_grad: float32 [64], P('fsdp')
The draws below stay inside these ranges and needn't reach their ends.
Inputs may be any that keep to these rules, and one draw needn't show every extreme that they name: `segments`: within each device's block of 1024 patches, equal ids mark one image; -1 marks padding, whose output and gradient vanish. Half of all blocks hold 4 sequences of four small images of 64 patches each; the others hold one sequence: an image of 576 patches, a second image, then padding.
All inputs are finite; a program needn't handle non-finite values.
Results may differ from the reference program's by a relative error of at most 0.024.
Values may be sent and summed in bfloat16 or wider, within the bound.
A program may use at most 256 MiB of HBM per device.

```python
import jax
import jax.numpy as jnp
from jax import lax

D = 768
HEAD = 64
FF = 3072
LONG = 1024
IMG = 64
TOKENS = 32768


def draw_segments(key, part):
    blocks = TOKENS // LONG
    position = jnp.arange(LONG, dtype=jnp.int32)
    small_ids = position // IMG
    large_size = 9 * LONG // 16
    remain = LONG - large_size
    second = jax.random.randint(key, (blocks, 1), remain // 8, remain).astype(jnp.int32)
    large_ids = jnp.where(position[None, :] < large_size, 0, jnp.where(position[None, :] < large_size + second, 1, -1))
    is_small = jnp.arange(blocks, dtype=jnp.int32)[:, None] < blocks // 2
    ids = jnp.where(is_small, small_ids[None, :], large_ids)
    return ids.reshape(-1).astype(jnp.int32)


def block_levels(stream_key, dims, pieces, low, top_value):
    level = 1.0
    for dim, blocks in pieces:
        steps = jax.random.uniform(jax.random.fold_in(jax.random.fold_in(stream_key, 6), dim), (blocks,), jnp.float32, low / len(pieces), top_value / len(pieces))
        level = level * jnp.repeat(jnp.exp(steps), dims[dim] // blocks).reshape((-1,) + (1,) * (len(dims) - 1 - dim))
    return level


def gaussian(own_key, extent, deviation, bound, split=(), kind=jnp.bfloat16):
    array = jax.random.normal(own_key, extent, jnp.float32) * deviation
    if len(split) > 0:
        array = block_levels(own_key, extent, split, -0.22, 0.18) * array
    return jnp.clip(array, min=-bound, max=bound).astype(kind)


def setup_inputs(seed: int = 0) -> dict:
    seeds = jax.random.split(jax.random.key(seed), 18)
    tokens = gaussian(seeds[0], (TOKENS, D), 1.0, 6.0, ((0, 32),))
    segments = draw_segments(jax.random.fold_in(seeds[17], 71), 0)
    cotangent = gaussian(seeds[2], (TOKENS, D), 1.0, 6.0, ((0, 32),))
    qkv_weight = gaussian(seeds[3], (D, 3 * D), D ** -0.5, 0.21875, ((0, 4),))
    qkv_bias = gaussian(seeds[4], (3 * D,), 0.3, 1.796875, ((0, 4),))
    out_weight = gaussian(seeds[5], (D, D), (D // 16) ** -0.5, 0.875, ((0, 4),))
    out_bias = gaussian(seeds[6], (D,), 0.3, 1.796875, ((0, 4),))
    up_weight = gaussian(seeds[7], (D, FF), D ** -0.5, 0.21875, ((0, 4),))
    up_bias = gaussian(seeds[8], (FF,), 0.3, 1.796875, ((0, 4),))
    down_weight = gaussian(seeds[9], (FF, D), FF ** -0.5, 0.109375, ((0, 4),))
    down_bias = gaussian(seeds[10], (D,), 0.3, 1.796875, ((0, 4),))
    first_gain = jnp.clip(1.0 + 0.1 * jax.random.normal(seeds[11], (D,), jnp.float32), 0.5, 1.5).astype(jnp.bfloat16)
    first_shift = gaussian(seeds[12], (D,), 0.3, 1.796875, ((0, 4),))
    second_gain = jnp.clip(1.0 + 0.1 * jax.random.normal(seeds[13], (D,), jnp.float32), 0.5, 1.5).astype(jnp.bfloat16)
    second_shift = gaussian(seeds[14], (D,), 0.3, 1.796875, ((0, 4),))
    query_gain = jnp.clip(1.0 + 0.18 * jax.random.normal(seeds[15], (HEAD,), jnp.float32), 0.099609375, 1.8984375).astype(jnp.bfloat16)
    key_gain = jnp.clip(1.0 + 0.18 * jax.random.normal(seeds[16], (HEAD,), jnp.float32), 0.099609375, 1.8984375).astype(jnp.bfloat16)
    return {"tokens": tokens, "segments": segments, "cotangent": cotangent, "qkv_weight": qkv_weight, "qkv_bias": qkv_bias, "out_weight": out_weight, "out_bias": out_bias, "up_weight": up_weight, "up_bias": up_bias, "down_weight": down_weight, "down_bias": down_bias, "first_gain": first_gain, "first_shift": first_shift, "second_gain": second_gain, "second_shift": second_shift, "query_gain": query_gain, "key_gain": key_gain}


norm_eps = 1e-06
highest = lax.Precision.HIGHEST

@jax.custom_vjp
def low(v):
    return lax.optimization_barrier(v.astype(jnp.bfloat16)).astype(jnp.float32)

@jax.custom_vjp
def low_back(v):
    return v

def low_keep(v):
    return (low(v), None)

def low_pass(kept, grad):
    return (grad,)

def back_keep(v):
    return (v, None)

def back_low(kept, grad):
    return (low(grad),)
low.defvjp(low_keep, low_pass)
low_back.defvjp(back_keep, back_low)

def layer_norm(value, gain, shift):
    centred = value - lax.optimization_barrier(jnp.mean(value, axis=-1, keepdims=True))
    scaled = centred * lax.rsqrt(lax.optimization_barrier(jnp.mean(centred * centred, axis=-1, keepdims=True)) + norm_eps)
    return scaled * gain + shift

def head_scale(value, gain):
    centred = value - lax.optimization_barrier(jnp.mean(value, axis=-1, keepdims=True))
    return centred * lax.rsqrt(lax.optimization_barrier(jnp.mean(centred * centred, axis=-1, keepdims=True)) + norm_eps) * gain

def forward(tokens, segments, params):
    qkv_weight, qkv_bias, out_weight, out_bias, up_weight, up_bias, down_weight, down_bias, first_gain, first_shift, second_gain, second_shift, query_gain, key_gain = params
    count = tokens.shape[0]
    width = tokens.shape[1]
    heads = width // HEAD
    normed = low(layer_norm(tokens, first_gain, first_shift))
    mixed = low_back(jnp.dot(normed, qkv_weight, precision=highest) + qkv_bias)
    query = mixed[:, :width].reshape(count, heads, HEAD)
    keys = mixed[:, width:2 * width].reshape(count, heads, HEAD)
    values = low(mixed[:, 2 * width:].reshape(count, heads, HEAD))
    query_low = low(head_scale(query, query_gain))
    key_low = low(head_scale(keys, key_gain))
    scores = low_back(jnp.einsum('qhe,khe->hqk', query_low, key_low, precision=highest) * 0.125)
    allowed = segments[:, None] == segments[None, :]
    scores = jnp.where(allowed[None], scores, -1e+30)
    weights = low(jax.nn.softmax(scores, axis=-1))
    attended = low_back(jnp.einsum('hqk,khe->qhe', weights, values, precision=highest).reshape(count, width))
    branch = low_back(jnp.dot(low(attended), out_weight, precision=highest) + out_bias)
    residual = tokens + branch
    second = low(layer_norm(residual, second_gain, second_shift))
    hidden = low_back(jnp.dot(second, up_weight, precision=highest) + up_bias)
    active = low(jax.nn.gelu(hidden, approximate=False))
    result = low_back(jnp.dot(active, down_weight, precision=highest) + down_bias)
    valid = (segments >= 0)[:, None]
    return jnp.where(valid, residual + result, 0.0)

def reference(tokens, segments, cotangent, qkv_weight, qkv_bias, out_weight, out_bias, up_weight, up_bias, down_weight, down_bias, first_gain, first_shift, second_gain, second_shift, query_gain, key_gain):
    params = tuple((item.astype(jnp.float32) for item in (qkv_weight, qkv_bias, out_weight, out_bias, up_weight, up_bias, down_weight, down_bias, first_gain, first_shift, second_gain, second_shift, query_gain, key_gain)))
    width = tokens.shape[1]
    blocks = tokens.shape[0] // LONG
    token_blocks = tokens.astype(jnp.float32).reshape(blocks, LONG, width)
    segment_blocks = segments.astype(jnp.int32).reshape(blocks, LONG)
    cotangent_blocks = cotangent.astype(jnp.float32).reshape(blocks, LONG, width)

    def step(total, item):
        block_tokens, block_segments, block_cotangent = item
        output, back = jax.vjp(lambda value, prm: forward(value, block_segments, prm), block_tokens, params)
        grad_tokens, grad_params = back(block_cotangent)
        summed = tuple((left + right for left, right in zip(total, grad_params)))
        return (summed, (output.astype(jnp.bfloat16), grad_tokens.astype(jnp.bfloat16)))
    zeros = tuple((jnp.zeros(item.shape, jnp.float32) for item in params))
    total, (outputs, grads) = lax.scan(step, zeros, (token_blocks, segment_blocks, cotangent_blocks))
    return (outputs.reshape(-1, width), grads.reshape(-1, width), total[0], total[1], total[2], total[3], total[4], total[5], total[6], total[7], total[8], total[9], total[10], total[11], total[12], total[13])
```

```python
import functools

import jax
import jax.numpy as jnp
from jax import lax
from jax.experimental import pallas as pl
from jax.experimental.pallas import tpu as pltpu
from jax.sharding import PartitionSpec as P

norm_eps = 1e-06
low = jnp.bfloat16
full = jnp.float32


def layer_norm(value, gain, shift):
    centred = value - jnp.mean(value, axis=-1, keepdims=True)
    scaled = centred * lax.rsqrt(jnp.mean(centred * centred, axis=-1, keepdims=True) + norm_eps)
    return scaled * gain + shift


def exact_gelu(value):
    return jax.nn.gelu(value, approximate=False)


def left_product(left, right):
    return lax.dot_general(
        left, right, (((0,), (0,)), ((), ())), preferred_element_type=jnp.float32
    )


def right_product(left, right):
    return lax.dot_general(
        left, right, (((1,), (1,)), ((), ())), preferred_element_type=jnp.float32
    )


def plain(left, right):
    return jnp.dot(left, right, preferred_element_type=jnp.float32)


def lane_index(shape):
    return lax.broadcasted_iota(jnp.int32, shape, len(shape) - 1)


def same_head(scale):
    row = lax.broadcasted_iota(jnp.int32, (128, 128), 0) // 64
    column = lax.broadcasted_iota(jnp.int32, (128, 128), 1) // 64
    return jnp.where(row == column, scale, 0.0).astype(low)


def head_norm(raw, mean_map):
    value = raw.astype(full)
    centred = value - plain(raw, mean_map)
    scale = lax.rsqrt(plain((centred * centred).astype(low), mean_map) + norm_eps)
    return centred * scale, scale


def half_mask(head, lanes):
    return (lanes < 64) if head == 0 else (lanes >= 64)


def query_codes(segments, lanes):
    spot = lanes % 64
    match = jnp.where(spot == segments + 1, 128.0, 0.0)
    return jnp.where(spot == 17, -128.0, match)


def key_codes(segments, lanes):
    spot = lanes % 64
    match = jnp.where(spot == segments + 1, 1.0, 0.0)
    return jnp.where((spot >= 17) & (spot < 20), 1.0, match)


def spans(count):
    cut = count * 9 // 16
    return ((0, cut), (cut, count))


def attend_kernel(flag_ref, q_ref, k_ref, v_ref, seg_ref, gq_ref, gk_ref, o_ref, total_ref):
    count = q_ref.shape[0]
    lanes = lane_index((count, 128))
    mean_map = same_head(1.0 / 64)
    q_unit, _ = head_norm(q_ref[...], mean_map)
    k_unit, _ = head_norm(k_ref[...], mean_map)
    q_low = q_unit * (gq_ref[...] * 0.125)
    k_low = k_unit * gk_ref[...]
    segments = seg_ref[...]
    q_code = query_codes(segments, lanes)
    k_code = key_codes(segments, lanes)
    values = v_ref[...]
    q_heads = [jnp.where(half_mask(h, lanes), q_low, q_code).astype(low) for h in (0, 1)]
    k_heads = [jnp.where(half_mask(h, lanes), k_low, k_code).astype(low) for h in (0, 1)]
    v_heads = [
        jnp.where(half_mask(h, lanes), values.astype(full), 1.0).astype(low) for h in (0, 1)
    ]

    def run(first, last, keys_first, keys_last, tile):
        for start in range(first, last, tile):
            parts = []
            for h in (0, 1):
                scores = right_product(
                    q_heads[h][start : start + tile], k_heads[h][keys_first:keys_last]
                )
                parts.append(plain(jnp.exp(scores).astype(low), v_heads[h][keys_first:keys_last]))
            here = lane_index((tile, 128)) < 64
            raw = jnp.where(here, parts[0], parts[1])
            sums = jnp.where(here, parts[1], parts[0])
            total = pltpu.roll(sums, 64, 1)
            o_ref[start : start + tile] = (raw / total).astype(o_ref.dtype)
            total_ref[start : start + tile] = jnp.log(sums)

    @pl.when(flag_ref[0] == 0)
    def _():
        for first, last in spans(count):
            run(first, last, first, last, (last - first) // 2)

    @pl.when(flag_ref[0] != 0)
    def _():
        run(0, count, 0, count, 256)


def attend_back_kernel(
    flag_ref,
    q_ref,
    k_ref,
    v_ref,
    seg_ref,
    gq_ref,
    gk_ref,
    o_ref,
    total_ref,
    do_ref,
    grad_ref,
    gain_ref,
    dq_scr,
):
    count = q_ref.shape[0]
    lanes = lane_index((count, 128))
    spot = lanes % 64
    mean_map = same_head(1.0 / 64)
    q_unit, q_scale = head_norm(q_ref[...], mean_map)
    k_unit, k_scale = head_norm(k_ref[...], mean_map)
    q_low = (q_unit * (gq_ref[...] * 0.125)).astype(low)
    k_low = (k_unit * gk_ref[...]).astype(low)
    segments = seg_ref[...]
    log_total = total_ref[...]
    log_high = log_total.astype(low).astype(full)
    q_code = jnp.where(
        spot == 18,
        -log_high,
        jnp.where(spot == 19, log_high - log_total, query_codes(segments, lanes)),
    ).astype(low)
    k_code = key_codes(segments, lanes).astype(low)
    grads = do_ref[...]
    product = (grads.astype(full) * o_ref[...].astype(full)).astype(low)
    row = lax.broadcasted_iota(jnp.int32, (128, 128), 0) // 64
    column = lax.broadcasted_iota(jnp.int32, (128, 128), 1) // 64
    delta = plain(product, jnp.where(row != column, 1.0, 0.0).astype(low))
    delta_high = delta.astype(low).astype(full)
    g_code = jnp.where(
        spot == 0, -delta_high, jnp.where(spot == 1, delta_high - delta, 0.0)
    ).astype(low)
    v_code = jnp.where(spot < 2, 1.0, 0.0).astype(low)
    values = v_ref[...]
    masks = [half_mask(h, lanes) for h in (0, 1)]
    q_heads = [jnp.where(masks[h], q_low, q_code) for h in (0, 1)]
    k_heads = [jnp.where(masks[h], k_low, k_code) for h in (0, 1)]
    v_heads = [jnp.where(masks[h], values, v_code) for h in (0, 1)]
    g_heads = [jnp.where(masks[h], grads, g_code) for h in (0, 1)]
    dk_parts = []

    def run(first, last, other_first, other_last, tile):
        for start in range(first, last, tile):
            rows = slice(start, start + tile)
            others = slice(other_first, other_last)
            dv_parts, dk_parts, dq_parts = [], [], []
            for h in (0, 1):
                scores = right_product(k_heads[h][rows], q_heads[h][others])
                weights = jnp.exp(scores)
                change = right_product(v_heads[h][rows], g_heads[h][others])
                sloped = (weights * change).astype(low)
                dv_parts.append(plain(weights.astype(low), grads[others]))
                dk_parts.append(plain(sloped, q_low[others]))
                dq_parts.append(left_product(sloped, k_low[rows]))
            here = lane_index((tile, 128)) < 64
            there = lane_index((other_last - other_first, 128)) < 64
            grad_ref[2, rows] = jnp.where(here, dv_parts[0], dv_parts[1]).astype(low)
            dk = jnp.where(here, dk_parts[0], dk_parts[1])
            dk_scr_store(rows, dk)
            dq = jnp.where(there, dq_parts[0], dq_parts[1])
            if start == first:
                dq_scr[0, others] = dq
            else:
                dq_scr[0, others] += dq

    def dk_scr_store(rows, value):
        dq_scr[1, rows] = value

    @pl.when(flag_ref[0] == 0)
    def _():
        for first, last in spans(count):
            run(first, last, first, last, (last - first) // 2)

    @pl.when(flag_ref[0] != 0)
    def _():
        run(0, count, 0, count, 256)

    def norm_back(slot, factor, unit, scale, gain):
        slope = dq_scr[slot] * factor
        inner = slope * gain
        shared = inner * unit
        result = scale * (
            inner
            - plain(inner.astype(low), mean_map)
            - unit * plain(shared.astype(low), mean_map)
        )
        grad_ref[slot] = result.astype(low)
        gain_ref[0, slot : slot + 1] = jnp.sum(slope * unit, axis=0, keepdims=True)

    norm_back(0, 0.125, q_unit, q_scale, gq_ref[...])
    norm_back(1, 1.0, k_unit, k_scale, gk_ref[...])


def attend_specs(count, width):
    pairs = width // 128
    column = lambda offset: pl.BlockSpec((count, 128), lambda i, flag: (0, i + offset))
    fixed = lambda shape: pl.BlockSpec(shape, lambda i, flag: (0, 0))
    shared = [
        column(0),
        column(pairs),
        column(2 * pairs),
        fixed((count, 1)),
        fixed((1, 128)),
        fixed((1, 128)),
    ]
    return pairs, column, shared


def attend(flag, mixed, segments, gain_q, gain_k):
    count = mixed.shape[0]
    width = mixed.shape[1] // 3
    pairs, column, shared = attend_specs(count, width)
    return pl.pallas_call(
        attend_kernel,
        grid_spec=pltpu.PrefetchScalarGridSpec(
            num_scalar_prefetch=1,
            grid=(pairs,),
            in_specs=shared,
            out_specs=[column(0), column(0)],
        ),
        out_shape=[
            jax.ShapeDtypeStruct((count, width), low),
            jax.ShapeDtypeStruct((count, width), full),
        ],
        compiler_params=pltpu.CompilerParams(vmem_limit_bytes=50 * 2**20),
        cost_estimate=pl.CostEstimate(
            flops=16 * count * count * width,
            bytes_accessed=count * width * 12,
            transcendentals=count * count * width // 64,
        ),
        name="attend",
    )(flag, mixed, mixed, mixed, segments, gain_q, gain_k)


def attend_back(flag, mixed, segments, gain_q, gain_k, attended, log_total, grad):
    count = mixed.shape[0]
    width = mixed.shape[1] // 3
    pairs, column, shared = attend_specs(count, width)
    return pl.pallas_call(
        attend_back_kernel,
        grid_spec=pltpu.PrefetchScalarGridSpec(
            num_scalar_prefetch=1,
            grid=(pairs,),
            in_specs=shared + [column(0), column(0), column(0)],
            out_specs=[
                pl.BlockSpec((3, count, 128), lambda i, flag: (0, 0, i)),
                pl.BlockSpec((1, 2, 128), lambda i, flag: (i, 0, 0)),
            ],
            scratch_shapes=[pltpu.VMEM((2, count, 128), full)],
        ),
        out_shape=[
            jax.ShapeDtypeStruct((3, count, width), low),
            jax.ShapeDtypeStruct((pairs, 2, 128), full),
        ],
        compiler_params=pltpu.CompilerParams(vmem_limit_bytes=56 * 2**20),
        cost_estimate=pl.CostEstimate(
            flops=40 * count * count * width,
            bytes_accessed=count * width * 18,
            transcendentals=count * count * width // 64,
        ),
        name="attend_back",
    )(flag, mixed, mixed, mixed, segments, gain_q, gain_k, attended, log_total, grad)


def gather_small(parts):
    lengths = [part.shape[0] for part in parts]
    flat = jnp.concatenate(parts).reshape(1, -1)
    whole = lax.all_gather(flat, "fsdp", axis=0, tiled=True)
    result, start = [], 0
    for length in lengths:
        result.append(whole[:, start : start + length].reshape(-1))
        start += length
    return result


def sum_small(parts, groups):
    lengths = [part.shape[0] // groups for part in parts]
    rows = jnp.concatenate([part.reshape(groups, -1) for part in parts], axis=1).astype(low)
    mine = lax.psum_scatter(rows, "fsdp", scatter_dimension=0, tiled=True)
    mine = lax.psum(mine, "dp").astype(full).reshape(-1)
    result, start = [], 0
    for length in lengths:
        result.append(mine[start : start + length])
        start += length
    return result


def sum_large(part):
    mine = lax.psum_scatter(part.astype(low), "fsdp", scatter_dimension=0, tiled=True)
    return lax.psum(mine, "dp").astype(full)


def gather_large(part):
    return lax.all_gather(part, "fsdp", axis=0, tiled=True)


def shards(
    groups,
    tokens,
    segments,
    cotangent,
    qkv_weight,
    qkv_bias,
    out_weight,
    out_bias,
    up_weight,
    up_bias,
    down_weight,
    down_bias,
    first_gain,
    first_shift,
    second_gain,
    second_shift,
    query_gain,
    key_gain,
):
    small = gather_small(
        [
            qkv_bias,
            out_bias,
            up_bias,
            down_bias,
            first_gain,
            first_shift,
            second_gain,
            second_shift,
            query_gain,
            key_gain,
        ]
    )
    small = [part.astype(full) for part in small]
    (qkv_b, out_b, up_b, down_b, gain_1, shift_1, gain_2, shift_2, gain_q, gain_k) = small
    qkv_w = gather_large(qkv_weight)
    out_w = gather_large(out_weight)
    up_w = gather_large(up_weight)
    down_w = gather_large(down_weight)
    count, width = tokens.shape
    cut = spans(count)[0][1]
    crossing = jnp.any(segments[:cut, None] == segments[None, cut:])
    flag = crossing.astype(jnp.int32).reshape(1)
    column = segments.reshape(count, 1)
    pair_q = jnp.tile(gain_q, 2).reshape(1, 128)
    pair_k = jnp.tile(gain_k, 2).reshape(1, 128)
    valid = (segments >= 0)[:, None]

    inputs = tokens.astype(full)
    normed, first_back = jax.vjp(layer_norm, inputs, gain_1, shift_1)
    normed = normed.astype(low)
    mixed = (plain(normed, qkv_w) + qkv_b).astype(low)
    attended, log_total = attend(flag, mixed, column, pair_q, pair_k)
    residual = inputs + plain(attended, out_w) + out_b
    second, second_back = jax.vjp(layer_norm, residual, gain_2, shift_2)
    second = second.astype(low)
    hidden = plain(second, up_w) + up_b
    active, gelu_back = jax.vjp(exact_gelu, hidden)
    active = active.astype(low)
    output = jnp.where(valid, residual + plain(active, down_w) + down_b, 0.0).astype(low)

    grad_low = jnp.where(valid, cotangent, jnp.zeros_like(cotangent))
    grad_output = grad_low.astype(full)
    down_grad = sum_large(left_product(active, grad_low))
    down_b_grad = jnp.sum(grad_output, axis=0)
    (grad_hidden,) = gelu_back(right_product(grad_low, down_w))
    grad_hidden = grad_hidden.astype(low)
    up_grad = sum_large(left_product(second, grad_hidden))
    up_b_grad = jnp.sum(grad_hidden.astype(full), axis=0)
    grad_norm_2, gain_2_grad, shift_2_grad = second_back(right_product(grad_hidden, up_w))
    grad_residual = grad_output + grad_norm_2
    branch = grad_residual.astype(low)
    out_grad = sum_large(left_product(attended, branch))
    out_b_grad = jnp.sum(branch.astype(full), axis=0)
    grad_attended = right_product(branch, out_w).astype(low)
    grad_mixed, pair_gains = attend_back(
        flag, mixed, column, pair_q, pair_k, attended, log_total, grad_attended
    )
    gain_sums = jnp.sum(pair_gains, axis=0).reshape(2, 2, -1).sum(axis=1)
    pieces = [grad_mixed[i] for i in range(3)]
    qkv_grad = sum_large(
        jnp.concatenate([left_product(normed, piece).astype(low) for piece in pieces], axis=1)
    )
    qkv_b_grad = jnp.sum(grad_mixed.astype(full), axis=1).reshape(-1)
    grad_norm = sum(
        right_product(piece, qkv_w[:, i * width : (i + 1) * width])
        for i, piece in enumerate(pieces)
    )
    grad_norm_1, gain_1_grad, shift_1_grad = first_back(grad_norm)
    grad_input = (grad_residual + grad_norm_1).astype(low)
    sums = sum_small(
        [
            qkv_b_grad,
            out_b_grad,
            up_b_grad,
            down_b_grad,
            gain_1_grad,
            shift_1_grad,
            gain_2_grad,
            shift_2_grad,
            gain_sums[0],
            gain_sums[1],
        ],
        groups,
    )
    return (
        output,
        grad_input,
        qkv_grad,
        sums[0],
        out_grad,
        sums[1],
        up_grad,
        sums[2],
        down_grad,
        sums[3],
        *sums[4:],
    )


def solution(mesh):
    rows = P(("dp", "fsdp"), None)
    matrix = P("fsdp", None)
    vector = P("fsdp")
    params = (matrix, vector) * 4 + (vector,) * 6
    return jax.shard_map(
        functools.partial(shards, mesh.shape["fsdp"]),
        mesh=mesh,
        in_specs=(rows, P(("dp", "fsdp")), rows) + params,
        out_specs=(rows, rows) + params,
        check_vma=False,
    )
```

```python
import functools

import jax
import jax.numpy as jnp
from jax import lax
from jax.experimental import pallas as pl
from jax.experimental.pallas import tpu as pltpu
from jax.sharding import PartitionSpec as P

norm_eps = 1e-06
low = jnp.bfloat16
full = jnp.float32


def layer_norm(value, gain, shift):
    centred = value - jnp.mean(value, axis=-1, keepdims=True)
    scaled = centred * lax.rsqrt(jnp.mean(centred * centred, axis=-1, keepdims=True) + norm_eps)
    return scaled * gain + shift


def exact_gelu(value):
    return jax.nn.gelu(value, approximate=False)


def left_product(left, right):
    return lax.dot_general(
        left, right, (((0,), (0,)), ((), ())), preferred_element_type=jnp.float32
    )


def right_product(left, right):
    return lax.dot_general(
        left, right, (((1,), (1,)), ((), ())), preferred_element_type=jnp.float32
    )


def plain(left, right):
    return jnp.dot(left, right, preferred_element_type=jnp.float32)


def lane_index(shape):
    return lax.broadcasted_iota(jnp.int32, shape, len(shape) - 1)


def same_head(scale):
    row = lax.broadcasted_iota(jnp.int32, (128, 128), 0) // 64
    column = lax.broadcasted_iota(jnp.int32, (128, 128), 1) // 64
    return jnp.where(row == column, scale, 0.0).astype(low)


def head_norm(raw, mean_map):
    value = raw.astype(full)
    centred = value - plain(raw, mean_map)
    scale = lax.rsqrt(plain((centred * centred).astype(low), mean_map) + norm_eps)
    return centred * scale, scale


def half_mask(head, lanes):
    return (lanes < 64) if head == 0 else (lanes >= 64)


def query_codes(segments, lanes):
    spot = lanes % 64
    match = jnp.where(spot == segments + 1, 128.0, 0.0)
    return jnp.where(spot == 17, -128.0, match)


def key_codes(segments, lanes):
    spot = lanes % 64
    match = jnp.where(spot == segments + 1, 1.0, 0.0)
    return jnp.where((spot >= 17) & (spot < 20), 1.0, match)


def spans(count):
    cut = count * 9 // 16
    return ((0, cut), (cut, count))


def attend_kernel(flag_ref, q_ref, k_ref, v_ref, seg_ref, gq_ref, gk_ref, o_ref, total_ref):
    count = q_ref.shape[0]
    lanes = lane_index((count, 128))
    mean_map = same_head(1.0 / 64)
    q_unit, _ = head_norm(q_ref[...], mean_map)
    k_unit, _ = head_norm(k_ref[...], mean_map)
    q_low = q_unit * (gq_ref[...] * 0.125)
    k_low = k_unit * gk_ref[...]
    segments = seg_ref[...]
    q_code = query_codes(segments, lanes)
    k_code = key_codes(segments, lanes)
    values = v_ref[...]
    q_heads = [jnp.where(half_mask(h, lanes), q_low, q_code).astype(low) for h in (0, 1)]
    k_heads = [jnp.where(half_mask(h, lanes), k_low, k_code).astype(low) for h in (0, 1)]
    v_heads = [
        jnp.where(half_mask(h, lanes), values.astype(full), 1.0).astype(low) for h in (0, 1)
    ]

    def run(first, last, keys_first, keys_last, tile):
        for start in range(first, last, tile):
            parts = []
            for h in (0, 1):
                scores = right_product(
                    q_heads[h][start : start + tile], k_heads[h][keys_first:keys_last]
                )
                parts.append(plain(jnp.exp(scores).astype(low), v_heads[h][keys_first:keys_last]))
            here = lane_index((tile, 128)) < 64
            raw = jnp.where(here, parts[0], parts[1])
            sums = jnp.where(here, parts[1], parts[0])
            total = pltpu.roll(sums, 64, 1)
            o_ref[start : start + tile] = (raw / total).astype(o_ref.dtype)
            total_ref[start : start + tile] = jnp.log(sums)

    @pl.when(flag_ref[0] == 0)
    def _():
        for first, last in spans(count):
            run(first, last, first, last, (last - first) // 2)

    @pl.when(flag_ref[0] != 0)
    def _():
        run(0, count, 0, count, 256)


def attend_back_kernel(
    flag_ref,
    q_ref,
    k_ref,
    v_ref,
    seg_ref,
    gq_ref,
    gk_ref,
    o_ref,
    total_ref,
    do_ref,
    grad_ref,
    gain_ref,
    dq_scr,
):
    count = q_ref.shape[0]
    lanes = lane_index((count, 128))
    spot = lanes % 64
    mean_map = same_head(1.0 / 64)
    q_unit, q_scale = head_norm(q_ref[...], mean_map)
    k_unit, k_scale = head_norm(k_ref[...], mean_map)
    q_low = (q_unit * (gq_ref[...] * 0.125)).astype(low)
    k_low = (k_unit * gk_ref[...]).astype(low)
    segments = seg_ref[...]
    log_total = total_ref[...]
    log_high = log_total.astype(low).astype(full)
    q_code = jnp.where(
        spot == 18,
        -log_high,
        jnp.where(spot == 19, log_high - log_total, query_codes(segments, lanes)),
    ).astype(low)
    k_code = key_codes(segments, lanes).astype(low)
    grads = do_ref[...]
    product = (grads.astype(full) * o_ref[...].astype(full)).astype(low)
    row = lax.broadcasted_iota(jnp.int32, (128, 128), 0) // 64
    column = lax.broadcasted_iota(jnp.int32, (128, 128), 1) // 64
    delta = plain(product, jnp.where(row != column, 1.0, 0.0).astype(low))
    delta_high = delta.astype(low).astype(full)
    g_code = jnp.where(
        spot == 0, -delta_high, jnp.where(spot == 1, delta_high - delta, 0.0)
    ).astype(low)
    v_code = jnp.where(spot < 2, 1.0, 0.0).astype(low)
    values = v_ref[...]
    masks = [half_mask(h, lanes) for h in (0, 1)]
    q_heads = [jnp.where(masks[h], q_low, q_code) for h in (0, 1)]
    k_heads = [jnp.where(masks[h], k_low, k_code) for h in (0, 1)]
    v_heads = [jnp.where(masks[h], values, v_code) for h in (0, 1)]
    g_heads = [jnp.where(masks[h], grads, g_code) for h in (0, 1)]
    dk_parts = []

    def run(first, last, other_first, other_last, tile):
        for start in range(first, last, tile):
            rows = slice(start, start + tile)
            others = slice(other_first, other_last)
            dv_parts, dk_parts, dq_parts = [], [], []
            for h in (0, 1):
                scores = right_product(k_heads[h][rows], q_heads[h][others])
                weights = jnp.exp(scores)
                change = right_product(v_heads[h][rows], g_heads[h][others])
                sloped = (weights * change).astype(low)
                dv_parts.append(plain(weights.astype(low), grads[others]))
                dk_parts.append(plain(sloped, q_low[others]))
                dq_parts.append(left_product(sloped, k_low[rows]))
            here = lane_index((tile, 128)) < 64
            there = lane_index((other_last - other_first, 128)) < 64
            grad_ref[2, rows] = jnp.where(here, dv_parts[0], dv_parts[1]).astype(low)
            dk = jnp.where(here, dk_parts[0], dk_parts[1])
            dk_scr_store(rows, dk)
            dq = jnp.where(there, dq_parts[0], dq_parts[1])
            if start == first:
                dq_scr[0, others] = dq
            else:
                dq_scr[0, others] += dq

    def dk_scr_store(rows, value):
        dq_scr[1, rows] = value

    @pl.when(flag_ref[0] == 0)
    def _():
        for first, last in spans(count):
            run(first, last, first, last, (last - first) // 2)

    @pl.when(flag_ref[0] != 0)
    def _():
        run(0, count, 0, count, 256)

    def norm_back(slot, factor, unit, scale, gain):
        slope = dq_scr[slot] * factor
        inner = slope * gain
        shared = inner * unit
        result = scale * (
            inner
            - plain(inner.astype(low), mean_map)
            - unit * plain(shared.astype(low), mean_map)
        )
        grad_ref[slot] = result.astype(low)
        gain_ref[0, slot : slot + 1] = jnp.sum(slope * unit, axis=0, keepdims=True)

    norm_back(0, 0.125, q_unit, q_scale, gq_ref[...])
    norm_back(1, 1.0, k_unit, k_scale, gk_ref[...])


def attend_specs(count, width):
    pairs = width // 128
    column = lambda offset: pl.BlockSpec((count, 128), lambda i, flag: (0, i + offset))
    fixed = lambda shape: pl.BlockSpec(shape, lambda i, flag: (0, 0))
    shared = [
        column(0),
        column(pairs),
        column(2 * pairs),
        fixed((count, 1)),
        fixed((1, 128)),
        fixed((1, 128)),
    ]
    return pairs, column, shared


def attend(flag, mixed, segments, gain_q, gain_k):
    count = mixed.shape[0]
    width = mixed.shape[1] // 3
    pairs, column, shared = attend_specs(count, width)
    return pl.pallas_call(
        attend_kernel,
        grid_spec=pltpu.PrefetchScalarGridSpec(
            num_scalar_prefetch=1,
            grid=(pairs,),
            in_specs=shared,
            out_specs=[column(0), column(0)],
        ),
        out_shape=[
            jax.ShapeDtypeStruct((count, width), low),
            jax.ShapeDtypeStruct((count, width), full),
        ],
        compiler_params=pltpu.CompilerParams(vmem_limit_bytes=50 * 2**20),
        cost_estimate=pl.CostEstimate(
            flops=16 * count * count * width,
            bytes_accessed=count * width * 12,
            transcendentals=count * count * width // 64,
        ),
        name="attend",
    )(flag, mixed, mixed, mixed, segments, gain_q, gain_k)


def attend_back(flag, mixed, segments, gain_q, gain_k, attended, log_total, grad):
    count = mixed.shape[0]
    width = mixed.shape[1] // 3
    pairs, column, shared = attend_specs(count, width)
    return pl.pallas_call(
        attend_back_kernel,
        grid_spec=pltpu.PrefetchScalarGridSpec(
            num_scalar_prefetch=1,
            grid=(pairs,),
            in_specs=shared + [column(0), column(0), column(0)],
            out_specs=[
                pl.BlockSpec((3, count, 128), lambda i, flag: (0, 0, i)),
                pl.BlockSpec((1, 2, 128), lambda i, flag: (i, 0, 0)),
            ],
            scratch_shapes=[pltpu.VMEM((2, count, 128), full)],
        ),
        out_shape=[
            jax.ShapeDtypeStruct((3, count, width), low),
            jax.ShapeDtypeStruct((pairs, 2, 128), full),
        ],
        compiler_params=pltpu.CompilerParams(vmem_limit_bytes=56 * 2**20),
        cost_estimate=pl.CostEstimate(
            flops=40 * count * count * width,
            bytes_accessed=count * width * 18,
            transcendentals=count * count * width // 64,
        ),
        name="attend_back",
    )(flag, mixed, mixed, mixed, segments, gain_q, gain_k, attended, log_total, grad)


def place(axis, bit):
    return lax.rem(lax.div(lax.axis_index(axis), 1 << bit), 2)


def swap(value, axis, size, offset):
    return lax.ppermute(value, axis, [(i, i ^ offset) for i in range(size)])


def pick(pair, index):
    return lax.dynamic_index_in_dim(pair, index, 0, keepdims=False)


def order(own, other, bit):
    return jnp.where(bit == 0, own, other), jnp.where(bit == 0, other, own)


def gather_small(parts, groups):
    lengths = [part.shape[0] for part in parts]
    flat = jnp.concatenate(parts).reshape(1, -1)
    bits = groups.bit_length() - 1
    for bit in range(bits):
        other = swap(flat, "fsdp", groups, 1 << bit)
        flat = jnp.concatenate(order(flat, other, place("fsdp", bit)), axis=0)
    result, start = [], 0
    for length in lengths:
        result.append(flat[:, start : start + length].reshape(-1))
        start += length
    return result


def sum_small(parts, groups, copies):
    lengths = [part.shape[0] // groups for part in parts]
    rows = jnp.concatenate([part.reshape(groups, -1) for part in parts], axis=1)
    for bit in reversed(range(groups.bit_length() - 1)):
        mine = place("fsdp", bit)
        pair = rows.reshape(2, -1, rows.shape[1])
        rows = pick(pair, mine) + swap(pick(pair, 1 - mine), "fsdp", groups, 1 << bit)
    for bit in range(copies.bit_length() - 1):
        rows = rows + swap(rows, "dp", copies, 1 << bit)
    mine = rows.reshape(-1)
    result, start = [], 0
    for length in lengths:
        result.append(mine[start : start + length])
        start += length
    return result


def gather_large(part, groups, copies):
    if groups != 4:
        return lax.all_gather(part, "fsdp", axis=0, tiled=True)
    rows, columns = part.shape
    core = place("dp", 0)
    x, y = place("fsdp", 0), place("fsdp", 1)
    half = rows // 2
    mine = pick(part.reshape(2, half, columns), core)
    from_x = swap(mine, "fsdp", groups, 1)
    from_y = swap(mine, "fsdp", groups, 2)
    quarter = half // 2
    far_low = swap(from_x[:quarter], "fsdp", groups, 2)
    far_high = swap(from_y[quarter:], "fsdp", groups, 1)
    far = jnp.concatenate([far_low, far_high], axis=0)
    pieces = []
    for value in (from_x, from_y, far):
        other = swap(value, "dp", copies, 1)
        pieces.append(jnp.concatenate(order(value, other, core), axis=0))
    row = order(part, pieces[0], x)
    other_row = order(pieces[1], pieces[2], x)
    first, second = order(jnp.concatenate(row), jnp.concatenate(other_row), y)
    return jnp.concatenate([first, second])


def halve(value, axis, size, bit):
    mine = place(axis, bit)
    return pick(value, mine) + swap(pick(value, 1 - mine), axis, size, 1 << bit)


def double(value, axis, size, bit):
    other = swap(value, axis, size, 1 << bit)
    return order(value, other, place(axis, bit))


def sum_large(part, groups, copies):
    part = part.astype(low)
    if groups != 4:
        mine = lax.psum_scatter(part, "fsdp", scatter_dimension=0, tiled=True)
        return lax.psum(mine, "dp").astype(full)
    total, columns = part.shape
    rows = total // groups
    pair = part.reshape(groups, 2, rows // 2, columns).swapaxes(0, 1)
    part = halve(pair, "dp", copies, 0).reshape(2, 2, 2, rows // 4, columns)
    left = halve(part[:, :, 0].swapaxes(0, 1), "fsdp", groups, 0)
    left = halve(left, "fsdp", groups, 1)
    right = halve(part[:, :, 1], "fsdp", groups, 1)
    right = halve(right, "fsdp", groups, 0)
    part = jnp.concatenate([left, right])
    if copies > 2:
        part = halve(part.reshape(2, rows // 4, columns), "dp", copies, 1)
        for bit in range(2, copies.bit_length() - 1):
            part = part + swap(part, "dp", copies, 1 << bit)
        part = jnp.concatenate(double(part, "dp", copies, 1))
    return jnp.concatenate(double(part, "dp", copies, 0)).astype(full)


def shards(
    groups,
    copies,
    tokens,
    segments,
    cotangent,
    qkv_weight,
    qkv_bias,
    out_weight,
    out_bias,
    up_weight,
    up_bias,
    down_weight,
    down_bias,
    first_gain,
    first_shift,
    second_gain,
    second_shift,
    query_gain,
    key_gain,
):
    small = gather_small(
        [
            qkv_bias,
            out_bias,
            up_bias,
            down_bias,
            first_gain,
            first_shift,
            second_gain,
            second_shift,
            query_gain,
            key_gain,
        ],
        groups,
    )
    small = [part.astype(full) for part in small]
    (qkv_b, out_b, up_b, down_b, gain_1, shift_1, gain_2, shift_2, gain_q, gain_k) = small
    qkv_w = gather_large(qkv_weight, groups, copies)
    out_w = gather_large(out_weight, groups, copies)
    up_w = gather_large(up_weight, groups, copies)
    down_w = gather_large(down_weight, groups, copies)
    count, width = tokens.shape
    cut = spans(count)[0][1]
    crossing = jnp.any(segments[:cut, None] == segments[None, cut:])
    flag = crossing.astype(jnp.int32).reshape(1)
    column = segments.reshape(count, 1)
    pair_q = jnp.tile(gain_q, 2).reshape(1, 128)
    pair_k = jnp.tile(gain_k, 2).reshape(1, 128)
    valid = (segments >= 0)[:, None]

    inputs = tokens.astype(full)
    normed, first_back = jax.vjp(layer_norm, inputs, gain_1, shift_1)
    normed = normed.astype(low)
    mixed = (plain(normed, qkv_w) + qkv_b).astype(low)
    attended, log_total = attend(flag, mixed, column, pair_q, pair_k)
    residual = inputs + plain(attended, out_w) + out_b
    second, second_back = jax.vjp(layer_norm, residual, gain_2, shift_2)
    second = second.astype(low)
    hidden = plain(second, up_w) + up_b
    active, gelu_back = jax.vjp(exact_gelu, hidden)
    active = active.astype(low)
    output = jnp.where(valid, residual + plain(active, down_w) + down_b, 0.0).astype(low)

    grad_low = jnp.where(valid, cotangent, jnp.zeros_like(cotangent))
    grad_output = grad_low.astype(full)
    down_grad = sum_large(left_product(active, grad_low), groups, copies)
    down_b_grad = jnp.sum(grad_output, axis=0)
    (grad_hidden,) = gelu_back(right_product(grad_low, down_w))
    grad_hidden = grad_hidden.astype(low)
    up_grad = sum_large(left_product(second, grad_hidden), groups, copies)
    up_b_grad = jnp.sum(grad_hidden.astype(full), axis=0)
    grad_norm_2, gain_2_grad, shift_2_grad = second_back(right_product(grad_hidden, up_w))
    grad_residual = grad_output + grad_norm_2
    branch = grad_residual.astype(low)
    out_grad = sum_large(left_product(attended, branch), groups, copies)
    out_b_grad = jnp.sum(branch.astype(full), axis=0)
    grad_attended = right_product(branch, out_w).astype(low)
    grad_mixed, pair_gains = attend_back(
        flag, mixed, column, pair_q, pair_k, attended, log_total, grad_attended
    )
    gain_sums = jnp.sum(pair_gains, axis=0).reshape(2, 2, -1).sum(axis=1)
    pieces = [grad_mixed[i] for i in range(3)]
    qkv_grad = sum_large(
        jnp.concatenate([left_product(normed, piece).astype(low) for piece in pieces], axis=1),
        groups,
        copies,
    )
    qkv_b_grad = jnp.sum(grad_mixed.astype(full), axis=1).reshape(-1)
    grad_norm = sum(
        right_product(piece, qkv_w[:, i * width : (i + 1) * width])
        for i, piece in enumerate(pieces)
    )
    grad_norm_1, gain_1_grad, shift_1_grad = first_back(grad_norm)
    grad_input = (grad_residual + grad_norm_1).astype(low)
    sums = sum_small(
        [
            qkv_b_grad,
            out_b_grad,
            up_b_grad,
            down_b_grad,
            gain_1_grad,
            shift_1_grad,
            gain_2_grad,
            shift_2_grad,
            gain_sums[0],
            gain_sums[1],
        ],
        groups,
        copies,
    )
    return (
        output,
        grad_input,
        qkv_grad,
        sums[0],
        out_grad,
        sums[1],
        up_grad,
        sums[2],
        down_grad,
        sums[3],
        *sums[4:],
    )


def solution(mesh):
    rows = P(("dp", "fsdp"), None)
    matrix = P("fsdp", None)
    vector = P("fsdp")
    params = (matrix, vector) * 4 + (vector,) * 6
    return jax.shard_map(
        functools.partial(shards, mesh.shape["fsdp"], mesh.shape["dp"]),
        mesh=mesh,
        in_specs=(rows, P(("dp", "fsdp")), rows) + params,
        out_specs=(rows, rows) + params,
        check_vma=False,
    )
```

```python
import functools

import jax
import jax.numpy as jnp
from jax import lax
from jax.experimental import pallas as pl
from jax.experimental.pallas import tpu as pltpu
from jax.sharding import PartitionSpec as P

norm_eps = 1e-06
low = jnp.bfloat16
full = jnp.float32


def layer_norm(value, gain, shift):
    centred = value - jnp.mean(value, axis=-1, keepdims=True)
    scaled = centred * lax.rsqrt(jnp.mean(centred * centred, axis=-1, keepdims=True) + norm_eps)
    return scaled * gain + shift


def exact_gelu(value):
    return jax.nn.gelu(value, approximate=False)


def left_product(left, right):
    return lax.dot_general(
        left, right, (((0,), (0,)), ((), ())), preferred_element_type=jnp.float32
    )


def right_product(left, right):
    return lax.dot_general(
        left, right, (((1,), (1,)), ((), ())), preferred_element_type=jnp.float32
    )


def plain(left, right):
    return jnp.dot(left, right, preferred_element_type=jnp.float32)


def lane_index(shape):
    return lax.broadcasted_iota(jnp.int32, shape, len(shape) - 1)


def same_head(scale):
    row = lax.broadcasted_iota(jnp.int32, (128, 128), 0) // 64
    column = lax.broadcasted_iota(jnp.int32, (128, 128), 1) // 64
    return jnp.where(row == column, scale, 0.0).astype(low)


def head_norm(raw, mean_map):
    value = raw.astype(full)
    centred = value - plain(raw, mean_map)
    scale = lax.rsqrt(plain((centred * centred).astype(low), mean_map) + norm_eps)
    return centred * scale, scale


def half_mask(head, lanes):
    return (lanes < 64) if head == 0 else (lanes >= 64)


def query_codes(segments, lanes):
    spot = lanes % 64
    match = jnp.where(spot == segments + 1, 128.0, 0.0)
    return jnp.where(spot == 17, -128.0, match)


def key_codes(segments, lanes):
    spot = lanes % 64
    match = jnp.where(spot == segments + 1, 1.0, 0.0)
    return jnp.where((spot >= 17) & (spot < 20), 1.0, match)


def spans(count):
    cut = count * 9 // 16
    return ((0, cut), (cut, count))


def attend_kernel(flag_ref, q_ref, k_ref, v_ref, seg_ref, gq_ref, gk_ref, o_ref, total_ref):
    count = q_ref.shape[0]
    lanes = lane_index((count, 128))
    mean_map = same_head(1.0 / 64)
    q_unit, _ = head_norm(q_ref[...], mean_map)
    k_unit, _ = head_norm(k_ref[...], mean_map)
    q_low = q_unit * (gq_ref[...] * 0.125)
    k_low = k_unit * gk_ref[...]
    segments = seg_ref[...]
    q_code = query_codes(segments, lanes)
    k_code = key_codes(segments, lanes)
    values = v_ref[...]
    q_heads = [jnp.where(half_mask(h, lanes), q_low, q_code).astype(low) for h in (0, 1)]
    k_heads = [jnp.where(half_mask(h, lanes), k_low, k_code).astype(low) for h in (0, 1)]
    v_heads = [
        jnp.where(half_mask(h, lanes), values.astype(full), 1.0).astype(low) for h in (0, 1)
    ]

    def run(first, last, keys_first, keys_last, tile):
        for start in range(first, last, tile):
            parts = []
            for h in (0, 1):
                scores = right_product(
                    q_heads[h][start : start + tile], k_heads[h][keys_first:keys_last]
                )
                parts.append(plain(jnp.exp(scores).astype(low), v_heads[h][keys_first:keys_last]))
            here = lane_index((tile, 128)) < 64
            raw = jnp.where(here, parts[0], parts[1])
            sums = jnp.where(here, parts[1], parts[0])
            total = pltpu.roll(sums, 64, 1)
            o_ref[start : start + tile] = (raw / total).astype(o_ref.dtype)
            total_ref[start : start + tile] = jnp.log(sums)

    @pl.when(flag_ref[0] == 0)
    def _():
        for first, last in spans(count):
            run(first, last, first, last, (last - first) // 2)

    @pl.when(flag_ref[0] != 0)
    def _():
        run(0, count, 0, count, 256)


def attend_back_kernel(
    flag_ref,
    q_ref,
    k_ref,
    v_ref,
    seg_ref,
    gq_ref,
    gk_ref,
    o_ref,
    total_ref,
    do_ref,
    grad_ref,
    gain_ref,
    dq_scr,
):
    count = q_ref.shape[0]
    lanes = lane_index((count, 128))
    spot = lanes % 64
    mean_map = same_head(1.0 / 64)
    q_unit, q_scale = head_norm(q_ref[...], mean_map)
    k_unit, k_scale = head_norm(k_ref[...], mean_map)
    q_low = (q_unit * (gq_ref[...] * 0.125)).astype(low)
    k_low = (k_unit * gk_ref[...]).astype(low)
    segments = seg_ref[...]
    log_total = total_ref[...]
    log_high = log_total.astype(low).astype(full)
    q_code = jnp.where(
        spot == 18,
        -log_high,
        jnp.where(spot == 19, log_high - log_total, query_codes(segments, lanes)),
    ).astype(low)
    k_code = key_codes(segments, lanes).astype(low)
    grads = do_ref[...]
    product = (grads.astype(full) * o_ref[...].astype(full)).astype(low)
    row = lax.broadcasted_iota(jnp.int32, (128, 128), 0) // 64
    column = lax.broadcasted_iota(jnp.int32, (128, 128), 1) // 64
    delta = plain(product, jnp.where(row != column, 1.0, 0.0).astype(low))
    delta_high = delta.astype(low).astype(full)
    g_code = jnp.where(
        spot == 0, -delta_high, jnp.where(spot == 1, delta_high - delta, 0.0)
    ).astype(low)
    v_code = jnp.where(spot < 2, 1.0, 0.0).astype(low)
    values = v_ref[...]
    masks = [half_mask(h, lanes) for h in (0, 1)]
    q_heads = [jnp.where(masks[h], q_low, q_code) for h in (0, 1)]
    k_heads = [jnp.where(masks[h], k_low, k_code) for h in (0, 1)]
    v_heads = [jnp.where(masks[h], values, v_code) for h in (0, 1)]
    g_heads = [jnp.where(masks[h], grads, g_code) for h in (0, 1)]
    dk_parts = []

    def run(first, last, other_first, other_last, tile):
        for start in range(first, last, tile):
            rows = slice(start, start + tile)
            others = slice(other_first, other_last)
            dv_parts, dk_parts, dq_parts = [], [], []
            for h in (0, 1):
                scores = right_product(k_heads[h][rows], q_heads[h][others])
                weights = jnp.exp(scores)
                change = right_product(v_heads[h][rows], g_heads[h][others])
                sloped = (weights * change).astype(low)
                dv_parts.append(plain(weights.astype(low), grads[others]))
                dk_parts.append(plain(sloped, q_low[others]))
                dq_parts.append(left_product(sloped, k_low[rows]))
            here = lane_index((tile, 128)) < 64
            there = lane_index((other_last - other_first, 128)) < 64
            grad_ref[2, rows] = jnp.where(here, dv_parts[0], dv_parts[1]).astype(low)
            dk = jnp.where(here, dk_parts[0], dk_parts[1])
            dk_scr_store(rows, dk)
            dq = jnp.where(there, dq_parts[0], dq_parts[1])
            if start == first:
                dq_scr[0, others] = dq
            else:
                dq_scr[0, others] += dq

    def dk_scr_store(rows, value):
        dq_scr[1, rows] = value

    @pl.when(flag_ref[0] == 0)
    def _():
        for first, last in spans(count):
            run(first, last, first, last, (last - first) // 2)

    @pl.when(flag_ref[0] != 0)
    def _():
        run(0, count, 0, count, 256)

    def norm_back(slot, factor, unit, scale, gain):
        slope = dq_scr[slot] * factor
        inner = slope * gain
        shared = inner * unit
        result = scale * (
            inner
            - plain(inner.astype(low), mean_map)
            - unit * plain(shared.astype(low), mean_map)
        )
        grad_ref[slot] = result.astype(low)
        gain_ref[0, slot : slot + 1] = jnp.sum(slope * unit, axis=0, keepdims=True)

    norm_back(0, 0.125, q_unit, q_scale, gq_ref[...])
    norm_back(1, 1.0, k_unit, k_scale, gk_ref[...])


def attend_specs(count, width, first=0):
    pairs = width // 128
    column = lambda offset: pl.BlockSpec((count, 128), lambda i, flag: (0, i + first + offset))
    fixed = lambda shape: pl.BlockSpec(shape, lambda i, flag: (0, 0))
    shared = [
        column(0),
        column(pairs),
        column(2 * pairs),
        fixed((count, 1)),
        fixed((1, 128)),
        fixed((1, 128)),
    ]
    return pairs, column, shared


def attend(flag, mixed, segments, gain_q, gain_k):
    count = mixed.shape[0]
    width = mixed.shape[1] // 3
    pairs, column, shared = attend_specs(count, width)
    return pl.pallas_call(
        attend_kernel,
        grid_spec=pltpu.PrefetchScalarGridSpec(
            num_scalar_prefetch=1,
            grid=(pairs,),
            in_specs=shared,
            out_specs=[column(0), column(0)],
        ),
        out_shape=[
            jax.ShapeDtypeStruct((count, width), low),
            jax.ShapeDtypeStruct((count, width), full),
        ],
        compiler_params=pltpu.CompilerParams(vmem_limit_bytes=50 * 2**20),
        cost_estimate=pl.CostEstimate(
            flops=16 * count * count * width,
            bytes_accessed=count * width * 12,
            transcendentals=count * count * width // 64,
        ),
        name="attend",
    )(flag, mixed, mixed, mixed, segments, gain_q, gain_k)


def attend_back(flag, mixed, segments, gain_q, gain_k, attended, log_total, grad, first, pairs):
    count = mixed.shape[0]
    width = mixed.shape[1] // 3
    _, column, shared = attend_specs(count, width, first)
    return pl.pallas_call(
        attend_back_kernel,
        grid_spec=pltpu.PrefetchScalarGridSpec(
            num_scalar_prefetch=1,
            grid=(pairs,),
            in_specs=shared + [column(0), column(0), column(0)],
            out_specs=[
                pl.BlockSpec((3, count, 128), lambda i, flag: (0, 0, i)),
                pl.BlockSpec((1, 2, 128), lambda i, flag: (i, 0, 0)),
            ],
            scratch_shapes=[pltpu.VMEM((2, count, 128), full)],
        ),
        out_shape=[
            jax.ShapeDtypeStruct((3, count, pairs * 128), low),
            jax.ShapeDtypeStruct((pairs, 2, 128), full),
        ],
        compiler_params=pltpu.CompilerParams(vmem_limit_bytes=50 * 2**20),
        cost_estimate=pl.CostEstimate(
            flops=40 * count * count * pairs * 128,
            bytes_accessed=count * pairs * 128 * 18,
            transcendentals=count * count * pairs * 2,
        ),
        name="attend_back",
    )(flag, mixed, mixed, mixed, segments, gain_q, gain_k, attended, log_total, grad)


def input_grad_kernel(tokens_ref, gain_ref, above_ref, *refs):
    parts, (weight_ref, out_ref, sums_ref) = refs[:-3], refs[-3:]
    width = tokens_ref.shape[1]
    size = width // len(parts)
    slope = 0.0
    for p, part_ref in enumerate(parts):
        for kind in range(3):
            start = kind * width + p * size
            slope += right_product(part_ref[kind], weight_ref[:, start : start + size])
    value = tokens_ref[...].astype(full)
    centred = value - jnp.mean(value, axis=-1, keepdims=True)
    scale = lax.rsqrt(jnp.mean(centred * centred, axis=-1, keepdims=True) + norm_eps)
    unit = centred * scale
    inner = slope * gain_ref[...]
    shared = slope * unit
    back = scale * (
        inner
        - jnp.mean(inner, axis=-1, keepdims=True)
        - unit * jnp.mean(inner * unit, axis=-1, keepdims=True)
    )
    out_ref[...] = (above_ref[...] + back).astype(out_ref.dtype)
    sums = jnp.concatenate(
        [jnp.sum(shared, axis=0, keepdims=True), jnp.sum(slope, axis=0, keepdims=True)]
    )
    first = pl.program_id(0) == 0

    @pl.when(first)
    def _():
        sums_ref[...] = sums

    @pl.when(jnp.logical_not(first))
    def _():
        sums_ref[...] += sums


def input_grad(tokens, gain, above, parts, weight):
    count, width = tokens.shape
    tile = min(256, count)
    rows = pl.BlockSpec((tile, width), lambda i: (i, 0))
    whole = lambda array: pl.BlockSpec(array.shape, lambda i: (0, 0))
    return pl.pallas_call(
        input_grad_kernel,
        grid=(count // tile,),
        in_specs=[rows, whole(gain), rows]
        + [pl.BlockSpec((3, tile, part.shape[2]), lambda i: (0, i, 0)) for part in parts]
        + [whole(weight)],
        out_specs=[rows, pl.BlockSpec((2, width), lambda i: (0, 0))],
        out_shape=[
            jax.ShapeDtypeStruct((count, width), low),
            jax.ShapeDtypeStruct((2, width), full),
        ],
        compiler_params=pltpu.CompilerParams(vmem_limit_bytes=50 * 2**20),
        cost_estimate=pl.CostEstimate(
            flops=6 * count * width * width,
            bytes_accessed=count * width * 14 + 6 * width * width,
            transcendentals=0,
        ),
        name="input_grad",
    )(tokens, gain, above, *parts, weight)


def place(axis, bit):
    return lax.rem(lax.div(lax.axis_index(axis), 1 << bit), 2)


def pick(pair, index):
    return lax.dynamic_index_in_dim(pair, index, 0, keepdims=False)


def order(own, other, bit):
    return jnp.where(bit == 0, own, other), jnp.where(bit == 0, other, own)


class Exchange:
    def __init__(self, sizes):
        self.sizes = sizes
        self.active = []

    def swap(self, value, axis, bit):
        size = self.sizes[axis]
        return lax.ppermute(value, axis, [(i, i ^ (1 << bit)) for i in range(size)])

    def start(self, steps):
        entry = {"steps": steps, "flying": None, "left": 0, "result": None}
        self.advance(entry, None)
        if entry["flying"] is not None:
            self.active.append(entry)
        return entry

    def advance(self, entry, landed):
        try:
            flying, hold = entry["steps"].send(landed)
            entry["flying"], entry["left"] = flying, hold
        except StopIteration as stop:
            entry["flying"], entry["result"] = None, stop.value

    def close(self, *values):
        due = []
        for entry in self.active:
            entry["left"] -= 1
            if entry["left"] <= 0:
                due.append(entry)
        landed = [entry["flying"] for entry in due]
        values, landed = lax.optimization_barrier((values, landed))
        for entry, arrived in zip(due, landed):
            self.advance(entry, arrived)
        self.active = [entry for entry in self.active if entry["flying"] is not None]
        return values

    def drain(self):
        while self.active:
            self.close()

    def gather_small(self, parts):
        flat = jnp.concatenate(parts).reshape(1, -1)
        if self.sizes["fsdp"] != 4:
            return lax.all_gather(flat, "fsdp", axis=0, tiled=True)
        for bit in range(self.sizes["fsdp"].bit_length() - 1):
            (other,) = yield [self.swap(flat, "fsdp", bit)], 1
            flat = jnp.concatenate(order(flat, other, place("fsdp", bit)), axis=0)
        return flat

    def sum_small(self, rows):
        for bit in reversed(range(self.sizes["fsdp"].bit_length() - 1)):
            mine = place("fsdp", bit)
            pair = rows.reshape(2, -1, rows.shape[1])
            (other,) = yield [self.swap(pick(pair, 1 - mine), "fsdp", bit)], 1
            rows = pick(pair, mine) + other
        for bit in range(self.sizes["dp"].bit_length() - 1):
            (other,) = yield [self.swap(rows, "dp", bit)], 1
            rows = rows + other
        return rows.reshape(-1)

    def gather(self, part, hold):
        if self.sizes["fsdp"] != 4:
            return lax.all_gather(part, "fsdp", axis=0, tiled=True)
        rows, columns = part.shape
        core = place("dp", 0)
        x, y = place("fsdp", 0), place("fsdp", 1)
        half = rows // 2
        mine = pick(part.reshape(2, half, columns), core)
        from_x, from_y = (
            yield [self.swap(mine, "fsdp", 0), self.swap(mine, "fsdp", 1)],
            hold,
        )
        quarter = half // 2
        far_low, far_high, other_x, other_y = (
            yield [
                self.swap(from_x[:quarter], "fsdp", 1),
                self.swap(from_y[quarter:], "fsdp", 0),
                self.swap(from_x, "dp", 0),
                self.swap(from_y, "dp", 0),
            ],
            1,
        )
        far = jnp.concatenate([far_low, far_high], axis=0)
        (other_far,) = yield [self.swap(far, "dp", 0)], 1
        pieces = [
            jnp.concatenate(order(value, other, core), axis=0)
            for value, other in ((from_x, other_x), (from_y, other_y), (far, other_far))
        ]
        row = order(part, pieces[0], x)
        other_row = order(pieces[1], pieces[2], x)
        first, second = order(jnp.concatenate(row), jnp.concatenate(other_row), y)
        return jnp.concatenate([first, second])

    def sum(self, part):
        sizes = self.sizes
        part = part.astype(low)
        if sizes["fsdp"] != 4:
            mine = lax.psum_scatter(part, "fsdp", scatter_dimension=0, tiled=True)
            return lax.psum(mine, "dp").astype(full)
        total, columns = part.shape
        rows = total // 4
        core, x, y = place("dp", 0), place("fsdp", 0), place("fsdp", 1)
        pair = part.reshape(4, 2, rows // 2, columns).swapaxes(0, 1)
        (other,) = yield [self.swap(pick(pair, 1 - core), "dp", 0)], 1
        part = (pick(pair, core) + other).reshape(2, 2, 2, rows // 4, columns)
        left, right = part[:, :, 0].swapaxes(0, 1), part[:, :, 1]
        other_left, other_right = (
            yield [
                self.swap(pick(left, 1 - x), "fsdp", 0),
                self.swap(pick(right, 1 - y), "fsdp", 1),
            ],
            1,
        )
        left, right = pick(left, x) + other_left, pick(right, y) + other_right
        other_left, other_right = (
            yield [
                self.swap(pick(left, 1 - y), "fsdp", 1),
                self.swap(pick(right, 1 - x), "fsdp", 0),
            ],
            1,
        )
        left, right = pick(left, y) + other_left, pick(right, x) + other_right
        part = jnp.concatenate([left, right])
        last = sizes["dp"].bit_length() - 1
        if last > 1:
            chip = place("dp", 1)
            pair = part.reshape(2, rows // 4, columns)
            (other,) = yield [self.swap(pick(pair, 1 - chip), "dp", 1)], 1
            part = pick(pair, chip) + other
            for bit in range(2, last):
                (other,) = yield [self.swap(part, "dp", bit)], 1
                part = part + other
            (other,) = yield [self.swap(part, "dp", 1)], 1
            part = jnp.concatenate(order(part, other, chip))
        (other,) = yield [self.swap(part, "dp", 0)], 1
        return jnp.concatenate(order(part, other, core)).astype(full)


def shards(
    groups,
    copies,
    tokens,
    segments,
    cotangent,
    qkv_weight,
    qkv_bias,
    out_weight,
    out_bias,
    up_weight,
    up_bias,
    down_weight,
    down_bias,
    first_gain,
    first_shift,
    second_gain,
    second_shift,
    query_gain,
    key_gain,
):
    link = Exchange({"fsdp": groups, "dp": copies})
    vectors = [
        qkv_bias,
        out_bias,
        up_bias,
        down_bias,
        first_gain,
        first_shift,
        second_gain,
        second_shift,
        query_gain,
        key_gain,
    ]
    count, width = tokens.shape
    cut = spans(count)[0][1]
    crossing = jnp.any(segments[:cut, None] == segments[None, cut:])
    flag = crossing.astype(jnp.int32).reshape(1)
    column = segments.reshape(count, 1)
    valid = (segments >= 0)[:, None]

    small = link.start(link.gather_small(vectors))
    qkv_w = link.start(link.gather(qkv_weight, 1))
    flag, out_weight, up_weight, down_weight = link.close(
        flag, out_weight, up_weight, down_weight
    )
    out_w = link.start(link.gather(out_weight, 1))
    up_weight, down_weight = link.close(up_weight, down_weight)
    up_w = link.start(link.gather(up_weight, 2))
    whole, start = [], 0
    for vector in vectors:
        size = vector.shape[0]
        whole.append(small["result"][:, start : start + size].reshape(-1).astype(full))
        start += size
    (qkv_b, out_b, up_b, down_b, gain_1, shift_1, gain_2, shift_2, gain_q, gain_k) = whole
    pair_q = jnp.tile(gain_q, 2).reshape(1, 128)
    pair_k = jnp.tile(gain_k, 2).reshape(1, 128)
    normed = layer_norm(tokens.astype(full), gain_1, shift_1).astype(low)
    (normed, down_weight) = link.close(normed, down_weight)
    mixed = (plain(normed, qkv_w["result"]) + qkv_b).astype(low)
    (mixed, down_weight) = link.close(mixed, down_weight)
    down_w = link.start(link.gather(down_weight, 1))
    attended, log_total = link.close(*attend(flag, mixed, column, pair_q, pair_k))
    inputs = tokens.astype(full)
    residual = inputs + plain(attended, out_w["result"]) + out_b
    second, second_back = jax.vjp(layer_norm, residual, gain_2, shift_2)
    (second,) = link.close(second.astype(low))
    hidden = plain(second, up_w["result"]) + up_b
    active, gelu_back = jax.vjp(exact_gelu, hidden)
    (active,) = link.close(active.astype(low))
    down_w, up_w, out_w, qkv_w = (entry["result"] for entry in (down_w, up_w, out_w, qkv_w))

    grad_low = jnp.where(valid, cotangent, jnp.zeros_like(cotangent))
    grad_output = grad_low.astype(full)
    down_b_grad = jnp.sum(grad_output, axis=0)
    down_grad, down_b_grad = link.close(
        left_product(active, grad_low).astype(low), down_b_grad
    )
    down_sum = link.start(link.sum(down_grad))
    (grad_hidden,) = gelu_back(right_product(grad_low, down_w))
    grad_hidden = grad_hidden.astype(low)
    up_b_grad = jnp.sum(grad_hidden.astype(full), axis=0)
    grad_hidden, up_b_grad, active = link.close(grad_hidden, up_b_grad, active)
    output = jnp.where(valid, residual + plain(active, down_w) + down_b, 0.0).astype(low)
    up_grad = left_product(second, grad_hidden).astype(low)
    output, up_grad, grad_hidden = link.close(output, up_grad, grad_hidden)
    up_sum = link.start(link.sum(up_grad))
    grad_norm_2, gain_2_grad, shift_2_grad = second_back(right_product(grad_hidden, up_w))
    grad_residual = grad_output + grad_norm_2
    branch = grad_residual.astype(low)
    out_b_grad = jnp.sum(branch.astype(full), axis=0)
    out_grad = left_product(attended, branch).astype(low)
    grad_attended = right_product(branch, out_w).astype(low)
    grad_residual, grad_attended, out_grad = link.close(grad_residual, grad_attended, out_grad)
    out_sum = link.start(link.sum(out_grad))
    pairs = width // 128
    step = pairs // 3
    parts, gains, part_sums = [], [], []

    def finish(part):
        grad = jnp.concatenate([left_product(normed, part[i]).astype(low) for i in range(3)], 1)
        return grad

    waiting = None
    for first in range(0, pairs, step):
        grads = None if waiting is None else finish(waiting)
        part, gain = attend_back(
            flag, mixed, column, pair_q, pair_k, attended, log_total, grad_attended, first, step
        )
        if grads is None:
            part, gain, grad_attended = link.close(part, gain, grad_attended)
        else:
            part, gain, grad_attended, grads = link.close(part, gain, grad_attended, grads)
            part_sums.append(link.start(link.sum(grads)))
        parts.append(part)
        gains.append(gain)
        waiting = part
    (grads,) = link.close(finish(waiting))
    part_sums.append(link.start(link.sum(grads)))
    pair_gains = jnp.concatenate(gains)
    gain_sums = jnp.sum(pair_gains, axis=0).reshape(2, 2, -1).sum(axis=1)
    qkv_b_grad = jnp.concatenate(
        [jnp.sum(part.astype(full), axis=1) for part in parts], axis=1
    ).reshape(-1)
    grad_input, sums_1 = input_grad(tokens, gain_1.reshape(1, -1), grad_residual, parts, qkv_w)
    vectors = [
        qkv_b_grad,
        out_b_grad,
        up_b_grad,
        down_b_grad,
        sums_1[0],
        sums_1[1],
        gain_2_grad,
        shift_2_grad,
        gain_sums[0],
        gain_sums[1],
    ]
    rows = jnp.concatenate([vector.reshape(groups, -1) for vector in vectors], axis=1)
    grad_input, rows = link.close(grad_input, rows)
    small_sum = link.start(link.sum_small(rows))
    link.drain()
    final, start = [], 0
    for vector in vectors:
        size = vector.shape[0] // groups
        final.append(small_sum["result"][start : start + size])
        start += size
    size = step * 128
    qkv_grad = jnp.concatenate(
        [
            part["result"][:, kind * size : (kind + 1) * size]
            for kind in range(3)
            for part in part_sums
        ],
        axis=1,
    )
    return (
        output,
        grad_input,
        qkv_grad,
        final[0],
        out_sum["result"],
        final[1],
        up_sum["result"],
        final[2],
        down_sum["result"],
        final[3],
        *final[4:],
    )


def solution(mesh):
    rows = P(("dp", "fsdp"), None)
    matrix = P("fsdp", None)
    vector = P("fsdp")
    params = (matrix, vector) * 4 + (vector,) * 6
    return jax.shard_map(
        functools.partial(shards, mesh.shape["fsdp"], mesh.shape["dp"]),
        mesh=mesh,
        in_specs=(rows, P(("dp", "fsdp")), rows) + params,
        out_specs=(rows, rows) + params,
        check_vma=False,
    )
```

```python
import functools

import jax
import jax.numpy as jnp
from jax import lax
from jax.experimental import pallas as pl
from jax.experimental.pallas import tpu as pltpu
from jax.sharding import PartitionSpec as P

norm_eps = 1e-06
low = jnp.bfloat16
full = jnp.float32


def layer_norm(value, gain, shift):
    centred = value - jnp.mean(value, axis=-1, keepdims=True)
    scaled = centred * lax.rsqrt(jnp.mean(centred * centred, axis=-1, keepdims=True) + norm_eps)
    return scaled * gain + shift


def exact_gelu(value):
    return jax.nn.gelu(value, approximate=False)


def left_product(left, right):
    return lax.dot_general(
        left, right, (((0,), (0,)), ((), ())), preferred_element_type=jnp.float32
    )


def right_product(left, right):
    return lax.dot_general(
        left, right, (((1,), (1,)), ((), ())), preferred_element_type=jnp.float32
    )


def plain(left, right):
    return jnp.dot(left, right, preferred_element_type=jnp.float32)


def lane_index(shape):
    return lax.broadcasted_iota(jnp.int32, shape, len(shape) - 1)


def same_head(scale):
    row = lax.broadcasted_iota(jnp.int32, (128, 128), 0) // 64
    column = lax.broadcasted_iota(jnp.int32, (128, 128), 1) // 64
    return jnp.where(row == column, scale, 0.0).astype(low)


def head_norm(raw, mean_map):
    value = raw.astype(full)
    centred = value - plain(raw, mean_map)
    scale = lax.rsqrt(plain((centred * centred).astype(low), mean_map) + norm_eps)
    return centred * scale, scale


def half_mask(head, lanes):
    return (lanes < 64) if head == 0 else (lanes >= 64)


def query_codes(segments, lanes):
    spot = lanes % 64
    match = jnp.where(spot == segments + 1, 128.0, 0.0)
    return jnp.where(spot == 17, -128.0, match)


def key_codes(segments, lanes):
    spot = lanes % 64
    match = jnp.where(spot == segments + 1, 1.0, 0.0)
    return jnp.where((spot >= 17) & (spot < 20), 1.0, match)


def spans(count):
    cut = count * 9 // 16
    return ((0, cut), (cut, count))


def attend_kernel(flag_ref, q_ref, k_ref, v_ref, seg_ref, gq_ref, gk_ref, o_ref, total_ref):
    count = q_ref.shape[0]
    lanes = lane_index((count, 128))
    mean_map = same_head(1.0 / 64)
    q_unit, _ = head_norm(q_ref[...], mean_map)
    k_unit, _ = head_norm(k_ref[...], mean_map)
    q_low = q_unit * (gq_ref[...] * 0.125)
    k_low = k_unit * gk_ref[...]
    segments = seg_ref[...]
    q_code = query_codes(segments, lanes)
    k_code = key_codes(segments, lanes)
    values = v_ref[...]
    q_heads = [jnp.where(half_mask(h, lanes), q_low, q_code).astype(low) for h in (0, 1)]
    k_heads = [jnp.where(half_mask(h, lanes), k_low, k_code).astype(low) for h in (0, 1)]
    v_heads = [
        jnp.where(half_mask(h, lanes), values.astype(full), 1.0).astype(low) for h in (0, 1)
    ]

    def run(first, last, keys_first, keys_last, tile):
        for start in range(first, last, tile):
            parts = []
            for h in (0, 1):
                scores = right_product(
                    q_heads[h][start : start + tile], k_heads[h][keys_first:keys_last]
                )
                parts.append(plain(jnp.exp(scores).astype(low), v_heads[h][keys_first:keys_last]))
            here = lane_index((tile, 128)) < 64
            raw = jnp.where(here, parts[0], parts[1])
            sums = jnp.where(here, parts[1], parts[0])
            total = pltpu.roll(sums, 64, 1)
            o_ref[start : start + tile] = (raw / total).astype(o_ref.dtype)
            total_ref[start : start + tile] = jnp.log(sums)

    @pl.when(flag_ref[0] == 0)
    def _():
        for first, last in spans(count):
            run(first, last, first, last, (last - first) // 2)

    @pl.when(flag_ref[0] != 0)
    def _():
        run(0, count, 0, count, 256)


def attend_back_kernel(
    flag_ref,
    q_ref,
    k_ref,
    v_ref,
    seg_ref,
    gq_ref,
    gk_ref,
    o_ref,
    total_ref,
    do_ref,
    grad_ref,
    gain_ref,
    dq_scr,
):
    count = q_ref.shape[0]
    lanes = lane_index((count, 128))
    spot = lanes % 64
    mean_map = same_head(1.0 / 64)
    q_unit, q_scale = head_norm(q_ref[...], mean_map)
    k_unit, k_scale = head_norm(k_ref[...], mean_map)
    q_low = (q_unit * (gq_ref[...] * 0.125)).astype(low)
    k_low = (k_unit * gk_ref[...]).astype(low)
    segments = seg_ref[...]
    log_total = total_ref[...]
    log_high = log_total.astype(low).astype(full)
    q_code = jnp.where(
        spot == 18,
        -log_high,
        jnp.where(spot == 19, log_high - log_total, query_codes(segments, lanes)),
    ).astype(low)
    k_code = key_codes(segments, lanes).astype(low)
    grads = do_ref[...]
    product = (grads.astype(full) * o_ref[...].astype(full)).astype(low)
    row = lax.broadcasted_iota(jnp.int32, (128, 128), 0) // 64
    column = lax.broadcasted_iota(jnp.int32, (128, 128), 1) // 64
    delta = plain(product, jnp.where(row != column, 1.0, 0.0).astype(low))
    delta_high = delta.astype(low).astype(full)
    g_code = jnp.where(
        spot == 0, -delta_high, jnp.where(spot == 1, delta_high - delta, 0.0)
    ).astype(low)
    v_code = jnp.where(spot < 2, 1.0, 0.0).astype(low)
    values = v_ref[...]
    masks = [half_mask(h, lanes) for h in (0, 1)]
    q_heads = [jnp.where(masks[h], q_low, q_code) for h in (0, 1)]
    k_heads = [jnp.where(masks[h], k_low, k_code) for h in (0, 1)]
    v_heads = [jnp.where(masks[h], values, v_code) for h in (0, 1)]
    g_heads = [jnp.where(masks[h], grads, g_code) for h in (0, 1)]
    dk_parts = []

    def run(first, last, other_first, other_last, tile):
        for start in range(first, last, tile):
            rows = slice(start, start + tile)
            others = slice(other_first, other_last)
            dv_parts, dk_parts, dq_parts = [], [], []
            for h in (0, 1):
                scores = right_product(k_heads[h][rows], q_heads[h][others])
                weights = jnp.exp(scores)
                change = right_product(v_heads[h][rows], g_heads[h][others])
                sloped = (weights * change).astype(low)
                dv_parts.append(plain(weights.astype(low), grads[others]))
                dk_parts.append(plain(sloped, q_low[others]))
                dq_parts.append(left_product(sloped, k_low[rows]))
            here = lane_index((tile, 128)) < 64
            there = lane_index((other_last - other_first, 128)) < 64
            grad_ref[2, rows] = jnp.where(here, dv_parts[0], dv_parts[1]).astype(low)
            dk = jnp.where(here, dk_parts[0], dk_parts[1])
            dk_scr_store(rows, dk)
            dq = jnp.where(there, dq_parts[0], dq_parts[1])
            if start == first:
                dq_scr[0, others] = dq
            else:
                dq_scr[0, others] += dq

    def dk_scr_store(rows, value):
        dq_scr[1, rows] = value

    @pl.when(flag_ref[0] == 0)
    def _():
        for first, last in spans(count):
            run(first, last, first, last, (last - first) // 2)

    @pl.when(flag_ref[0] != 0)
    def _():
        run(0, count, 0, count, 256)

    def norm_back(slot, factor, unit, scale, gain):
        slope = dq_scr[slot] * factor
        inner = slope * gain
        shared = inner * unit
        result = scale * (
            inner
            - plain(inner.astype(low), mean_map)
            - unit * plain(shared.astype(low), mean_map)
        )
        grad_ref[slot] = result.astype(low)
        gain_ref[0, slot : slot + 1] = jnp.sum(slope * unit, axis=0, keepdims=True)

    norm_back(0, 0.125, q_unit, q_scale, gq_ref[...])
    norm_back(1, 1.0, k_unit, k_scale, gk_ref[...])


def attend_specs(count, width, first=0):
    pairs = width // 128
    column = lambda offset: pl.BlockSpec((count, 128), lambda i, flag: (0, i + first + offset))
    fixed = lambda shape: pl.BlockSpec(shape, lambda i, flag: (0, 0))
    shared = [
        column(0),
        column(pairs),
        column(2 * pairs),
        fixed((count, 1)),
        fixed((1, 128)),
        fixed((1, 128)),
    ]
    return pairs, column, shared


def attend(flag, mixed, segments, gain_q, gain_k):
    count = mixed.shape[0]
    width = mixed.shape[1] // 3
    pairs, column, shared = attend_specs(count, width)
    return pl.pallas_call(
        attend_kernel,
        grid_spec=pltpu.PrefetchScalarGridSpec(
            num_scalar_prefetch=1,
            grid=(pairs,),
            in_specs=shared,
            out_specs=[column(0), column(0)],
        ),
        out_shape=[
            jax.ShapeDtypeStruct((count, width), low),
            jax.ShapeDtypeStruct((count, width), full),
        ],
        compiler_params=pltpu.CompilerParams(vmem_limit_bytes=50 * 2**20),
        cost_estimate=pl.CostEstimate(
            flops=16 * count * count * width,
            bytes_accessed=count * width * 12,
            transcendentals=count * count * width // 64,
        ),
        name="attend",
    )(flag, mixed, mixed, mixed, segments, gain_q, gain_k)


def attend_back(flag, mixed, segments, gain_q, gain_k, attended, log_total, grad, first, pairs):
    count = mixed.shape[0]
    width = mixed.shape[1] // 3
    _, column, shared = attend_specs(count, width, first)
    return pl.pallas_call(
        attend_back_kernel,
        grid_spec=pltpu.PrefetchScalarGridSpec(
            num_scalar_prefetch=1,
            grid=(pairs,),
            in_specs=shared + [column(0), column(0), column(0)],
            out_specs=[
                pl.BlockSpec((3, count, 128), lambda i, flag: (0, 0, i)),
                pl.BlockSpec((1, 2, 128), lambda i, flag: (i, 0, 0)),
            ],
            scratch_shapes=[pltpu.VMEM((2, count, 128), full)],
        ),
        out_shape=[
            jax.ShapeDtypeStruct((3, count, pairs * 128), low),
            jax.ShapeDtypeStruct((pairs, 2, 128), full),
        ],
        compiler_params=pltpu.CompilerParams(vmem_limit_bytes=50 * 2**20),
        cost_estimate=pl.CostEstimate(
            flops=40 * count * count * pairs * 128,
            bytes_accessed=count * pairs * 128 * 18,
            transcendentals=count * count * pairs * 2,
        ),
        name="attend_back",
    )(flag, mixed, mixed, mixed, segments, gain_q, gain_k, attended, log_total, grad)


def input_grad_kernel(tokens_ref, gain_ref, above_ref, *refs):
    parts, (weight_ref, out_ref, sums_ref) = refs[:-3], refs[-3:]
    width = tokens_ref.shape[1]
    size = width // len(parts)
    slope = 0.0
    for p, part_ref in enumerate(parts):
        for kind in range(3):
            start = kind * width + p * size
            slope += right_product(part_ref[kind], weight_ref[:, start : start + size])
    value = tokens_ref[...].astype(full)
    centred = value - jnp.mean(value, axis=-1, keepdims=True)
    scale = lax.rsqrt(jnp.mean(centred * centred, axis=-1, keepdims=True) + norm_eps)
    unit = centred * scale
    inner = slope * gain_ref[...]
    shared = slope * unit
    back = scale * (
        inner
        - jnp.mean(inner, axis=-1, keepdims=True)
        - unit * jnp.mean(inner * unit, axis=-1, keepdims=True)
    )
    out_ref[...] = (above_ref[...] + back).astype(out_ref.dtype)
    sums = jnp.concatenate(
        [jnp.sum(shared, axis=0, keepdims=True), jnp.sum(slope, axis=0, keepdims=True)]
    )
    first = pl.program_id(0) == 0

    @pl.when(first)
    def _():
        sums_ref[...] = sums

    @pl.when(jnp.logical_not(first))
    def _():
        sums_ref[...] += sums


def input_grad(tokens, gain, above, parts, weight):
    count, width = tokens.shape
    tile = min(256, count)
    rows = pl.BlockSpec((tile, width), lambda i: (i, 0))
    whole = lambda array: pl.BlockSpec(array.shape, lambda i: (0, 0))
    return pl.pallas_call(
        input_grad_kernel,
        grid=(count // tile,),
        in_specs=[rows, whole(gain), rows]
        + [pl.BlockSpec((3, tile, part.shape[2]), lambda i: (0, i, 0)) for part in parts]
        + [whole(weight)],
        out_specs=[rows, pl.BlockSpec((2, width), lambda i: (0, 0))],
        out_shape=[
            jax.ShapeDtypeStruct((count, width), low),
            jax.ShapeDtypeStruct((2, width), full),
        ],
        compiler_params=pltpu.CompilerParams(vmem_limit_bytes=50 * 2**20),
        cost_estimate=pl.CostEstimate(
            flops=6 * count * width * width,
            bytes_accessed=count * width * 14 + 6 * width * width,
            transcendentals=0,
        ),
        name="input_grad",
    )(tokens, gain, above, *parts, weight)


def place(axis, bit):
    return lax.rem(lax.div(lax.axis_index(axis), 1 << bit), 2)


def pick(pair, index):
    return lax.dynamic_index_in_dim(pair, index, 0, keepdims=False)


def order(own, other, bit):
    return jnp.where(bit == 0, own, other), jnp.where(bit == 0, other, own)


class Exchange:
    def __init__(self, sizes):
        self.sizes = sizes
        self.active = []

    def swap(self, value, axis, bit):
        size = self.sizes[axis]
        return lax.ppermute(value, axis, [(i, i ^ (1 << bit)) for i in range(size)])

    def start(self, steps):
        entry = {"steps": steps, "flying": None, "left": 0, "result": None}
        self.advance(entry, None)
        if entry["flying"] is not None:
            self.active.append(entry)
        return entry

    def advance(self, entry, landed):
        try:
            flying, hold = entry["steps"].send(landed)
            entry["flying"], entry["left"] = flying, hold
        except StopIteration as stop:
            entry["flying"], entry["result"] = None, stop.value

    def close(self, *values):
        due = []
        for entry in self.active:
            entry["left"] -= 1
            if entry["left"] <= 0:
                due.append(entry)
        landed = [entry["flying"] for entry in due]
        values, landed = lax.optimization_barrier((values, landed))
        for entry, arrived in zip(due, landed):
            self.advance(entry, arrived)
        self.active = [entry for entry in self.active if entry["flying"] is not None]
        return values

    def drain(self):
        while self.active:
            self.close()

    def gather_small(self, parts):
        flat = jnp.concatenate(parts).reshape(1, -1)
        if self.sizes["fsdp"] != 4:
            return lax.all_gather(flat, "fsdp", axis=0, tiled=True)
        for bit in range(self.sizes["fsdp"].bit_length() - 1):
            (other,) = yield [self.swap(flat, "fsdp", bit)], 1
            flat = jnp.concatenate(order(flat, other, place("fsdp", bit)), axis=0)
        return flat

    def sum_small(self, rows):
        for bit in reversed(range(self.sizes["fsdp"].bit_length() - 1)):
            mine = place("fsdp", bit)
            pair = rows.reshape(2, -1, rows.shape[1])
            (other,) = yield [self.swap(pick(pair, 1 - mine), "fsdp", bit)], 1
            rows = pick(pair, mine) + other
        for axis in ("core", "z"):
            for bit in range(self.sizes[axis].bit_length() - 1):
                (other,) = yield [self.swap(rows, axis, bit)], 1
                rows = rows + other
        return rows.reshape(-1)

    def gather(self, part, hold):
        if self.sizes["fsdp"] != 4:
            return lax.all_gather(part, "fsdp", axis=0, tiled=True)
        rows, columns = part.shape
        core = place("core", 0)
        x, y = place("fsdp", 0), place("fsdp", 1)
        half = rows // 2
        mine = pick(part.reshape(2, half, columns), core)
        from_x, from_y = (
            yield [self.swap(mine, "fsdp", 0), self.swap(mine, "fsdp", 1)],
            hold,
        )
        quarter = half // 2
        far_low, far_high, other_x, other_y = (
            yield [
                self.swap(from_x[:quarter], "fsdp", 1),
                self.swap(from_y[quarter:], "fsdp", 0),
                self.swap(from_x, "core", 0),
                self.swap(from_y, "core", 0),
            ],
            1,
        )
        far = jnp.concatenate([far_low, far_high], axis=0)
        (other_far,) = yield [self.swap(far, "core", 0)], 1
        pieces = [
            jnp.concatenate(order(value, other, core), axis=0)
            for value, other in ((from_x, other_x), (from_y, other_y), (far, other_far))
        ]
        row = order(part, pieces[0], x)
        other_row = order(pieces[1], pieces[2], x)
        first, second = order(jnp.concatenate(row), jnp.concatenate(other_row), y)
        return jnp.concatenate([first, second])

    def sum(self, part):
        sizes = self.sizes
        part = part.astype(low)
        if sizes["fsdp"] != 4:
            mine = lax.psum_scatter(part, "fsdp", scatter_dimension=0, tiled=True)
            return lax.psum(mine, ("z", "core")).astype(full)
        total, columns = part.shape
        rows = total // 4
        core, x, y = place("core", 0), place("fsdp", 0), place("fsdp", 1)
        pair = part.reshape(4, 2, rows // 2, columns).swapaxes(0, 1)
        (other,) = yield [self.swap(pick(pair, 1 - core), "core", 0)], 1
        part = (pick(pair, core) + other).reshape(2, 2, 2, rows // 4, columns)
        left, right = part[:, :, 0].swapaxes(0, 1), part[:, :, 1]
        other_left, other_right = (
            yield [
                self.swap(pick(left, 1 - x), "fsdp", 0),
                self.swap(pick(right, 1 - y), "fsdp", 1),
            ],
            1,
        )
        left, right = pick(left, x) + other_left, pick(right, y) + other_right
        other_left, other_right = (
            yield [
                self.swap(pick(left, 1 - y), "fsdp", 1),
                self.swap(pick(right, 1 - x), "fsdp", 0),
            ],
            1,
        )
        left, right = pick(left, y) + other_left, pick(right, x) + other_right
        part = jnp.concatenate([left, right])
        last = sizes["z"].bit_length() - 1
        if last > 0:
            chip = place("z", 0)
            pair = part.reshape(2, rows // 4, columns)
            (other,) = yield [self.swap(pick(pair, 1 - chip), "z", 0)], 1
            part = pick(pair, chip) + other
            for bit in range(1, last):
                (other,) = yield [self.swap(part, "z", bit)], 1
                part = part + other
            (other,) = yield [self.swap(part, "z", 0)], 1
            part = jnp.concatenate(order(part, other, chip))
        (other,) = yield [self.swap(part, "core", 0)], 1
        return jnp.concatenate(order(part, other, core)).astype(full)

    def sum_offloaded(self, part):
        part = part.astype(low)
        core = place("core", 0)
        total, columns = part.shape
        groups = self.sizes["fsdp"]
        rows = total // groups
        pair = part.reshape(groups, 2, rows // 2, columns).swapaxes(0, 1)
        (other,) = yield [self.swap(pick(pair, 1 - core), "core", 0)], 1
        mine = (pick(pair, core) + other).reshape(total // 2, columns)
        (mine,) = yield [lax.psum_scatter(mine, "fsdp", scatter_dimension=0, tiled=True)], 2
        (mine,) = yield [lax.psum(mine, "z")], 2
        (other,) = yield [self.swap(mine, "core", 0)], 1
        return jnp.concatenate(order(mine, other, core)).astype(full)


def shards(
    groups,
    copies,
    tokens,
    segments,
    cotangent,
    qkv_weight,
    qkv_bias,
    out_weight,
    out_bias,
    up_weight,
    up_bias,
    down_weight,
    down_bias,
    first_gain,
    first_shift,
    second_gain,
    second_shift,
    query_gain,
    key_gain,
):
    link = Exchange({"fsdp": groups, "core": 2, "z": copies // 2})
    vectors = [
        qkv_bias,
        out_bias,
        up_bias,
        down_bias,
        first_gain,
        first_shift,
        second_gain,
        second_shift,
        query_gain,
        key_gain,
    ]
    count, width = tokens.shape
    cut = spans(count)[0][1]
    crossing = jnp.any(segments[:cut, None] == segments[None, cut:])
    flag = crossing.astype(jnp.int32).reshape(1)
    column = segments.reshape(count, 1)
    valid = (segments >= 0)[:, None]

    small = link.start(link.gather_small(vectors))
    qkv_w = link.start(link.gather(qkv_weight, 1))
    up_w = lax.all_gather(up_weight, "fsdp", axis=0, tiled=True)
    flag, out_weight, down_weight = link.close(flag, out_weight, down_weight)
    down_w = lax.all_gather(down_weight, "fsdp", axis=0, tiled=True)
    out_w = link.start(link.gather(out_weight, 1))
    (flag,) = link.close(flag)
    whole, start = [], 0
    for vector in vectors:
        size = vector.shape[0]
        whole.append(small["result"][:, start : start + size].reshape(-1).astype(full))
        start += size
    (qkv_b, out_b, up_b, down_b, gain_1, shift_1, gain_2, shift_2, gain_q, gain_k) = whole
    pair_q = jnp.tile(gain_q, 2).reshape(1, 128)
    pair_k = jnp.tile(gain_k, 2).reshape(1, 128)
    normed = layer_norm(tokens.astype(full), gain_1, shift_1).astype(low)
    (normed,) = link.close(normed)
    mixed = (plain(normed, qkv_w["result"]) + qkv_b).astype(low)
    (mixed,) = link.close(mixed)
    attended, log_total = link.close(*attend(flag, mixed, column, pair_q, pair_k))
    inputs = tokens.astype(full)
    residual = inputs + plain(attended, out_w["result"]) + out_b
    second, second_back = jax.vjp(layer_norm, residual, gain_2, shift_2)
    (second,) = link.close(second.astype(low))
    hidden = plain(second, up_w) + up_b
    active, gelu_back = jax.vjp(exact_gelu, hidden)
    (active,) = link.close(active.astype(low))
    out_w, qkv_w = out_w["result"], qkv_w["result"]

    grad_low = jnp.where(valid, cotangent, jnp.zeros_like(cotangent))
    grad_output = grad_low.astype(full)
    down_b_grad = jnp.sum(grad_output, axis=0)
    down_grad, down_b_grad = link.close(
        left_product(active, grad_low).astype(low), down_b_grad
    )
    down_sum = link.start(link.sum_offloaded(down_grad))
    (grad_hidden,) = gelu_back(right_product(grad_low, down_w))
    grad_hidden = grad_hidden.astype(low)
    up_b_grad = jnp.sum(grad_hidden.astype(full), axis=0)
    grad_hidden, up_b_grad, active = link.close(grad_hidden, up_b_grad, active)
    output = jnp.where(valid, residual + plain(active, down_w) + down_b, 0.0).astype(low)
    up_grad = left_product(second, grad_hidden).astype(low)
    output, up_grad, grad_hidden = link.close(output, up_grad, grad_hidden)
    up_sum = link.start(link.sum_offloaded(up_grad))
    grad_norm_2, gain_2_grad, shift_2_grad = second_back(right_product(grad_hidden, up_w))
    grad_residual = grad_output + grad_norm_2
    branch = grad_residual.astype(low)
    out_b_grad = jnp.sum(branch.astype(full), axis=0)
    out_grad = left_product(attended, branch).astype(low)
    grad_attended = right_product(branch, out_w).astype(low)
    grad_residual, grad_attended, out_grad = link.close(grad_residual, grad_attended, out_grad)
    out_sum = link.start(link.sum_offloaded(out_grad))
    pairs = width // 128
    step = pairs // 3
    parts, gains, part_sums = [], [], []

    def finish(part):
        grad = jnp.concatenate([left_product(normed, part[i]).astype(low) for i in range(3)], 1)
        return grad

    waiting = None
    for first in range(0, pairs, step):
        grads = None if waiting is None else finish(waiting)
        part, gain = attend_back(
            flag, mixed, column, pair_q, pair_k, attended, log_total, grad_attended, first, step
        )
        if grads is None:
            part, gain, grad_attended = link.close(part, gain, grad_attended)
        else:
            part, gain, grad_attended, grads = link.close(part, gain, grad_attended, grads)
            part_sums.append(link.start(link.sum(grads)))
        parts.append(part)
        gains.append(gain)
        waiting = part
    (grads,) = link.close(finish(waiting))
    part_sums.append(link.start(link.sum(grads)))
    pair_gains = jnp.concatenate(gains)
    gain_sums = jnp.sum(pair_gains, axis=0).reshape(2, 2, -1).sum(axis=1)
    qkv_b_grad = jnp.concatenate(
        [jnp.sum(part.astype(full), axis=1) for part in parts], axis=1
    ).reshape(-1)
    grad_input, sums_1 = input_grad(tokens, gain_1.reshape(1, -1), grad_residual, parts, qkv_w)
    vectors = [
        qkv_b_grad,
        out_b_grad,
        up_b_grad,
        down_b_grad,
        sums_1[0],
        sums_1[1],
        gain_2_grad,
        shift_2_grad,
        gain_sums[0],
        gain_sums[1],
    ]
    rows = jnp.concatenate([vector.reshape(groups, -1) for vector in vectors], axis=1)
    grad_input, rows = link.close(grad_input, rows)
    small_sum = link.start(link.sum_small(rows))
    link.drain()
    final, start = [], 0
    for vector in vectors:
        size = vector.shape[0] // groups
        final.append(small_sum["result"][start : start + size])
        start += size
    size = step * 128
    qkv_grad = jnp.concatenate(
        [
            part["result"][:, kind * size : (kind + 1) * size]
            for kind in range(3)
            for part in part_sums
        ],
        axis=1,
    )
    return (
        output,
        grad_input,
        qkv_grad,
        final[0],
        out_sum["result"],
        final[1],
        up_sum["result"],
        final[2],
        down_sum["result"],
        final[3],
        *final[4:],
    )


def solution(mesh):
    copies, groups = mesh.shape["dp"], mesh.shape["fsdp"]
    devices = mesh.devices.reshape(copies // 2, 2, groups)
    mesh = jax.sharding.Mesh(devices, ("z", "core", "fsdp"))
    rows = P(("z", "core", "fsdp"), None)
    matrix = P("fsdp", None)
    vector = P("fsdp")
    params = (matrix, vector) * 4 + (vector,) * 6
    return jax.shard_map(
        functools.partial(shards, groups, copies),
        mesh=mesh,
        in_specs=(rows, P(("z", "core", "fsdp")), rows) + params,
        out_specs=(rows, rows) + params,
        check_vma=False,
    )
```

```python
import functools

import jax
import jax.numpy as jnp
from jax import lax
from jax.experimental import pallas as pl
from jax.experimental.pallas import tpu as pltpu
from jax.sharding import PartitionSpec as P

norm_eps = 1e-06
low = jnp.bfloat16
full = jnp.float32


def layer_norm(value, gain, shift):
    centred = value - jnp.mean(value, axis=-1, keepdims=True)
    scaled = centred * lax.rsqrt(jnp.mean(centred * centred, axis=-1, keepdims=True) + norm_eps)
    return scaled * gain + shift


def exact_gelu(value):
    return jax.nn.gelu(value, approximate=False)


def left_product(left, right):
    return lax.dot_general(
        left, right, (((0,), (0,)), ((), ())), preferred_element_type=jnp.float32
    )


def right_product(left, right):
    return lax.dot_general(
        left, right, (((1,), (1,)), ((), ())), preferred_element_type=jnp.float32
    )


def plain(left, right):
    return jnp.dot(left, right, preferred_element_type=jnp.float32)


def lane_index(shape):
    return lax.broadcasted_iota(jnp.int32, shape, len(shape) - 1)


def same_head(scale):
    row = lax.broadcasted_iota(jnp.int32, (128, 128), 0) // 64
    column = lax.broadcasted_iota(jnp.int32, (128, 128), 1) // 64
    return jnp.where(row == column, scale, 0.0).astype(low)


def head_norm(raw, mean_map):
    value = raw.astype(full)
    centred = value - plain(raw, mean_map)
    scale = lax.rsqrt(plain((centred * centred).astype(low), mean_map) + norm_eps)
    return centred * scale, scale


def half_mask(head, lanes):
    return (lanes < 64) if head == 0 else (lanes >= 64)


def query_codes(segments, lanes):
    spot = lanes % 64
    match = jnp.where(spot == segments + 1, 128.0, 0.0)
    return jnp.where(spot == 17, -128.0, match)


def key_codes(segments, lanes):
    spot = lanes % 64
    match = jnp.where(spot == segments + 1, 1.0, 0.0)
    return jnp.where((spot >= 17) & (spot < 20), 1.0, match)


def spans(count):
    cut = count * 9 // 16
    return ((0, cut), (cut, count))


def attend_kernel(flag_ref, q_ref, k_ref, v_ref, seg_ref, gq_ref, gk_ref, o_ref, total_ref):
    count = q_ref.shape[0]
    lanes = lane_index((count, 128))
    mean_map = same_head(1.0 / 64)
    q_unit, _ = head_norm(q_ref[...], mean_map)
    k_unit, _ = head_norm(k_ref[...], mean_map)
    q_low = q_unit * (gq_ref[...] * 0.125)
    k_low = k_unit * gk_ref[...]
    segments = seg_ref[...]
    q_code = query_codes(segments, lanes)
    k_code = key_codes(segments, lanes)
    values = v_ref[...]
    q_heads = [jnp.where(half_mask(h, lanes), q_low, q_code).astype(low) for h in (0, 1)]
    k_heads = [jnp.where(half_mask(h, lanes), k_low, k_code).astype(low) for h in (0, 1)]
    v_heads = [
        jnp.where(half_mask(h, lanes), values.astype(full), 1.0).astype(low) for h in (0, 1)
    ]

    def run(first, last, keys_first, keys_last, tile):
        for start in range(first, last, tile):
            parts = []
            for h in (0, 1):
                scores = right_product(
                    q_heads[h][start : start + tile], k_heads[h][keys_first:keys_last]
                )
                parts.append(plain(jnp.exp(scores).astype(low), v_heads[h][keys_first:keys_last]))
            here = lane_index((tile, 128)) < 64
            raw = jnp.where(here, parts[0], parts[1])
            sums = jnp.where(here, parts[1], parts[0])
            total = pltpu.roll(sums, 64, 1)
            o_ref[start : start + tile] = (raw / total).astype(o_ref.dtype)
            total_ref[start : start + tile] = jnp.log(sums)

    @pl.when(flag_ref[0] == 0)
    def _():
        for first, last in spans(count):
            run(first, last, first, last, (last - first) // 2)

    @pl.when(flag_ref[0] != 0)
    def _():
        run(0, count, 0, count, 256)


def attend_back_kernel(
    flag_ref,
    q_ref,
    k_ref,
    v_ref,
    seg_ref,
    gq_ref,
    gk_ref,
    o_ref,
    total_ref,
    do_ref,
    grad_ref,
    gain_ref,
    dq_scr,
):
    count = q_ref.shape[0]
    lanes = lane_index((count, 128))
    spot = lanes % 64
    mean_map = same_head(1.0 / 64)
    q_unit, q_scale = head_norm(q_ref[...], mean_map)
    k_unit, k_scale = head_norm(k_ref[...], mean_map)
    q_low = (q_unit * (gq_ref[...] * 0.125)).astype(low)
    k_low = (k_unit * gk_ref[...]).astype(low)
    segments = seg_ref[...]
    log_total = total_ref[...]
    log_high = log_total.astype(low).astype(full)
    q_code = jnp.where(
        spot == 18,
        -log_high,
        jnp.where(spot == 19, log_high - log_total, query_codes(segments, lanes)),
    ).astype(low)
    k_code = key_codes(segments, lanes).astype(low)
    grads = do_ref[...]
    product = (grads.astype(full) * o_ref[...].astype(full)).astype(low)
    row = lax.broadcasted_iota(jnp.int32, (128, 128), 0) // 64
    column = lax.broadcasted_iota(jnp.int32, (128, 128), 1) // 64
    delta = plain(product, jnp.where(row != column, 1.0, 0.0).astype(low))
    delta_high = delta.astype(low).astype(full)
    g_code = jnp.where(
        spot == 0, -delta_high, jnp.where(spot == 1, delta_high - delta, 0.0)
    ).astype(low)
    v_code = jnp.where(spot < 2, 1.0, 0.0).astype(low)
    values = v_ref[...]
    masks = [half_mask(h, lanes) for h in (0, 1)]
    q_heads = [jnp.where(masks[h], q_low, q_code) for h in (0, 1)]
    k_heads = [jnp.where(masks[h], k_low, k_code) for h in (0, 1)]
    v_heads = [jnp.where(masks[h], values, v_code) for h in (0, 1)]
    g_heads = [jnp.where(masks[h], grads, g_code) for h in (0, 1)]
    dk_parts = []

    def run(first, last, other_first, other_last, tile):
        for start in range(first, last, tile):
            rows = slice(start, start + tile)
            others = slice(other_first, other_last)
            dv_parts, dk_parts, dq_parts = [], [], []
            for h in (0, 1):
                scores = right_product(k_heads[h][rows], q_heads[h][others])
                weights = jnp.exp(scores)
                change = right_product(v_heads[h][rows], g_heads[h][others])
                sloped = (weights * change).astype(low)
                dv_parts.append(plain(weights.astype(low), grads[others]))
                dk_parts.append(plain(sloped, q_low[others]))
                dq_parts.append(left_product(sloped, k_low[rows]))
            here = lane_index((tile, 128)) < 64
            there = lane_index((other_last - other_first, 128)) < 64
            grad_ref[2, rows] = jnp.where(here, dv_parts[0], dv_parts[1]).astype(low)
            dk = jnp.where(here, dk_parts[0], dk_parts[1])
            dk_scr_store(rows, dk)
            dq = jnp.where(there, dq_parts[0], dq_parts[1])
            if start == first:
                dq_scr[0, others] = dq
            else:
                dq_scr[0, others] += dq

    def dk_scr_store(rows, value):
        dq_scr[1, rows] = value

    @pl.when(flag_ref[0] == 0)
    def _():
        for first, last in spans(count):
            run(first, last, first, last, (last - first) // 2)

    @pl.when(flag_ref[0] != 0)
    def _():
        run(0, count, 0, count, 256)

    def norm_back(slot, factor, unit, scale, gain):
        slope = dq_scr[slot] * factor
        inner = slope * gain
        shared = inner * unit
        result = scale * (
            inner
            - plain(inner.astype(low), mean_map)
            - unit * plain(shared.astype(low), mean_map)
        )
        grad_ref[slot] = result.astype(low)
        gain_ref[0, slot : slot + 1] = jnp.sum(slope * unit, axis=0, keepdims=True)

    norm_back(0, 0.125, q_unit, q_scale, gq_ref[...])
    norm_back(1, 1.0, k_unit, k_scale, gk_ref[...])


def attend_specs(count, width, first=0):
    pairs = width // 128
    column = lambda offset: pl.BlockSpec((count, 128), lambda i, flag: (0, i + first + offset))
    fixed = lambda shape: pl.BlockSpec(shape, lambda i, flag: (0, 0))
    shared = [
        column(0),
        column(pairs),
        column(2 * pairs),
        fixed((count, 1)),
        fixed((1, 128)),
        fixed((1, 128)),
    ]
    return pairs, column, shared


def attend(flag, mixed, segments, gain_q, gain_k):
    count = mixed.shape[0]
    width = mixed.shape[1] // 3
    pairs, column, shared = attend_specs(count, width)
    return pl.pallas_call(
        attend_kernel,
        grid_spec=pltpu.PrefetchScalarGridSpec(
            num_scalar_prefetch=1,
            grid=(pairs,),
            in_specs=shared,
            out_specs=[column(0), column(0)],
        ),
        out_shape=[
            jax.ShapeDtypeStruct((count, width), low),
            jax.ShapeDtypeStruct((count, width), full),
        ],
        compiler_params=pltpu.CompilerParams(vmem_limit_bytes=50 * 2**20),
        cost_estimate=pl.CostEstimate(
            flops=16 * count * count * width,
            bytes_accessed=count * width * 12,
            transcendentals=count * count * width // 64,
        ),
        name="attend",
    )(flag, mixed, mixed, mixed, segments, gain_q, gain_k)


def attend_back(flag, mixed, segments, gain_q, gain_k, attended, log_total, grad, first, pairs):
    count = mixed.shape[0]
    width = mixed.shape[1] // 3
    _, column, shared = attend_specs(count, width, first)
    return pl.pallas_call(
        attend_back_kernel,
        grid_spec=pltpu.PrefetchScalarGridSpec(
            num_scalar_prefetch=1,
            grid=(pairs,),
            in_specs=shared + [column(0), column(0), column(0)],
            out_specs=[
                pl.BlockSpec((3, count, 128), lambda i, flag: (0, 0, i)),
                pl.BlockSpec((1, 2, 128), lambda i, flag: (i, 0, 0)),
            ],
            scratch_shapes=[pltpu.VMEM((2, count, 128), full)],
        ),
        out_shape=[
            jax.ShapeDtypeStruct((3, count, pairs * 128), low),
            jax.ShapeDtypeStruct((pairs, 2, 128), full),
        ],
        compiler_params=pltpu.CompilerParams(vmem_limit_bytes=50 * 2**20),
        cost_estimate=pl.CostEstimate(
            flops=40 * count * count * pairs * 128,
            bytes_accessed=count * pairs * 128 * 18,
            transcendentals=count * count * pairs * 2,
        ),
        name="attend_back",
    )(flag, mixed, mixed, mixed, segments, gain_q, gain_k, attended, log_total, grad)


def input_grad_kernel(tokens_ref, gain_ref, above_ref, *refs):
    parts, (weight_ref, out_ref, sums_ref) = refs[:-3], refs[-3:]
    width = tokens_ref.shape[1]
    size = width // len(parts)
    slope = 0.0
    for p, part_ref in enumerate(parts):
        for kind in range(3):
            start = kind * width + p * size
            slope += right_product(part_ref[kind], weight_ref[:, start : start + size])
    value = tokens_ref[...].astype(full)
    centred = value - jnp.mean(value, axis=-1, keepdims=True)
    scale = lax.rsqrt(jnp.mean(centred * centred, axis=-1, keepdims=True) + norm_eps)
    unit = centred * scale
    inner = slope * gain_ref[...]
    shared = slope * unit
    back = scale * (
        inner
        - jnp.mean(inner, axis=-1, keepdims=True)
        - unit * jnp.mean(inner * unit, axis=-1, keepdims=True)
    )
    out_ref[...] = (above_ref[...] + back).astype(out_ref.dtype)
    sums = jnp.concatenate(
        [jnp.sum(shared, axis=0, keepdims=True), jnp.sum(slope, axis=0, keepdims=True)]
    )
    first = pl.program_id(0) == 0

    @pl.when(first)
    def _():
        sums_ref[...] = sums

    @pl.when(jnp.logical_not(first))
    def _():
        sums_ref[...] += sums


def input_grad(tokens, gain, above, parts, weight):
    count, width = tokens.shape
    tile = min(256, count)
    rows = pl.BlockSpec((tile, width), lambda i: (i, 0))
    whole = lambda array: pl.BlockSpec(array.shape, lambda i: (0, 0))
    return pl.pallas_call(
        input_grad_kernel,
        grid=(count // tile,),
        in_specs=[rows, whole(gain), rows]
        + [pl.BlockSpec((3, tile, part.shape[2]), lambda i: (0, i, 0)) for part in parts]
        + [whole(weight)],
        out_specs=[rows, pl.BlockSpec((2, width), lambda i: (0, 0))],
        out_shape=[
            jax.ShapeDtypeStruct((count, width), low),
            jax.ShapeDtypeStruct((2, width), full),
        ],
        compiler_params=pltpu.CompilerParams(vmem_limit_bytes=50 * 2**20),
        cost_estimate=pl.CostEstimate(
            flops=6 * count * width * width,
            bytes_accessed=count * width * 14 + 6 * width * width,
            transcendentals=0,
        ),
        name="input_grad",
    )(tokens, gain, above, *parts, weight)


def place(axis, bit):
    return lax.rem(lax.div(lax.axis_index(axis), 1 << bit), 2)


def across(axis, bit):
    index = lax.axis_index(axis)
    return {axis: index + (1 - 2 * place(axis, bit)) * (1 << bit)}


def greet(partners):
    barrier = pltpu.get_barrier_semaphore()
    for partner in partners:
        pl.semaphore_signal(
            barrier, inc=1, device_id=partner, device_id_type=pl.DeviceIdType.MESH
        )
    pl.semaphore_wait(barrier, len(partners))


class Copies:
    def __init__(self, send_sems, recv_sems):
        self.send_sems, self.recv_sems = send_sems, recv_sems
        self.all = []

    def send(self, source, target, partner):
        index = len(self.all)
        copy = pltpu.make_async_remote_copy(
            src_ref=source,
            dst_ref=target,
            send_sem=self.send_sems.at[index],
            recv_sem=self.recv_sems.at[index],
            device_id=partner,
            device_id_type=pl.DeviceIdType.MESH,
        )
        copy.start()
        self.all.append(copy)
        return copy

    def finish(self):
        for copy in self.all:
            copy.wait_send()


def fetch_kernel(qkv_ref, out_ref, small_ref, qkv_all, out_all, small_all, send, recv, local):
    core, x, y = place("core", 0), place("fsdp", 0), place("fsdp", 1)
    me = lax.axis_index("fsdp")
    to_core, to_x, to_y = across("core", 0), across("fsdp", 0), across("fsdp", 1)
    to_far = {"fsdp": 3 - me}
    greet([to_core, to_x, to_y, to_far])
    copies = Copies(send, recv)
    arrivals = []
    for partner in (to_x, to_y, to_far):
        arrivals.append(copies.send(small_ref, small_all.at[me], partner))
    whole = ((qkv_ref, qkv_all), (out_ref, out_all))
    from_x_row, from_y_row, far_row = 2 * y + 1 - x, 2 * (1 - y) + x, 3 - me
    near = []
    for own, target in whole:
        mine = own.at[core]
        near.append(
            (
                copies.send(mine, target.at[me, core], to_x),
                copies.send(mine, target.at[me, core], to_y),
            )
        )
    own_copies = [
        pltpu.make_async_copy(own, target.at[me], local.at[i])
        for i, (own, target) in enumerate(whole + ((small_ref, small_all),))
    ]
    for copy in own_copies:
        copy.start()
    far = []
    for (own, target), (by_x, by_y) in zip(whole, near):
        by_x.wait_recv()
        quarter = target.at[from_x_row, core, 0]
        low_far = copies.send(quarter, quarter, to_y)
        half = target.at[from_x_row, core]
        arrivals.append(copies.send(half, half, to_core))
        by_y.wait_recv()
        quarter = target.at[from_y_row, core, 1]
        high_far = copies.send(quarter, quarter, to_x)
        half = target.at[from_y_row, core]
        arrivals.append(copies.send(half, half, to_core))
        far.append((low_far, high_far))
    for (own, target), (low_far, high_far) in zip(whole, far):
        low_far.wait_recv()
        high_far.wait_recv()
        half = target.at[far_row, core]
        arrivals.append(copies.send(half, half, to_core))
    for copy in arrivals:
        copy.wait_recv()
    for copy in own_copies:
        copy.wait()
    copies.finish()


def fetch(qkv_weight, out_weight, small):
    def split(part):
        rows, columns = part.shape
        return part.reshape(2, 2, rows // 4, columns)

    parts = (split(qkv_weight), split(out_weight), small)
    count = 3 + 2 * 7
    qkv_w, out_w, vectors = pl.pallas_call(
        fetch_kernel,
        in_specs=[pl.BlockSpec(memory_space=pltpu.VMEM)] * 3,
        out_specs=[pl.BlockSpec(memory_space=pltpu.VMEM)] * 3,
        out_shape=[jax.ShapeDtypeStruct((4,) + part.shape, part.dtype) for part in parts],
        scratch_shapes=[
            pltpu.SemaphoreType.DMA((count,)),
            pltpu.SemaphoreType.DMA((count,)),
            pltpu.SemaphoreType.DMA((3,)),
        ],
        compiler_params=pltpu.CompilerParams(
            collective_id=0, has_side_effects=True, vmem_limit_bytes=24 * 2**20
        ),
        name="fetch",
    )(*parts)
    return (
        qkv_w.reshape(-1, qkv_weight.shape[1]),
        out_w.reshape(-1, out_weight.shape[1]),
        vectors.reshape(4, -1),
    )


def total_kernel(chips, kinds, *refs):
    count = len(kinds)
    ins, small_ref = refs[:count], refs[count]
    outs, small_out = refs[count + 1 : 2 * count + 1], refs[2 * count + 1]
    first, left, right, second, third, fourth, last, small_in, send, recv = refs[2 * count + 2 :]
    core, x, y, chip = place("core", 0), place("fsdp", 0), place("fsdp", 1), place("z", 0)
    me = lax.axis_index("fsdp")
    to_core, to_x, to_y = across("core", 0), across("fsdp", 0), across("fsdp", 1)
    to_z = [across("z", bit) for bit in range(chips.bit_length() - 1)]
    partners = [to_core, to_x, to_y] + to_z
    greet(partners)
    copies = Copies(send, recv)
    width = last.shape[-1]

    chunks = []
    for index, kind in enumerate(kinds):
        stack, columns = kind
        for q in range(stack):
            for p in range(columns // width):
                span = slice(p * width, (p + 1) * width)
                chunks.append((ins[index], outs[index], q, span))

    def steps(c):
        source, target, q, span = chunks[c]
        lanes = pl.ds(span.start, width)
        copy = copies.send(source.at[:, :, q, 1 - core, :, :, lanes], first.at[c], to_core)
        yield
        copy.wait_recv()
        for row in range(2):
            first[c, row] = first[c, row] + source[row, :, q, core, :, :, lanes]
        by_x = copies.send(first.at[c, :, 1 - x, 0], left.at[c], to_x)
        by_y = copies.send(first.at[c, 1 - y, :, 1], right.at[c], to_y)
        yield
        by_x.wait_recv()
        left[c] = left[c] + first[c, :, x, 0]
        by_y.wait_recv()
        right[c] = right[c] + first[c, y, :, 1]
        by_y = copies.send(left.at[c, 1 - y], second.at[c, 0], to_y)
        by_x = copies.send(right.at[c, 1 - x], second.at[c, 1], to_x)
        yield
        by_y.wait_recv()
        second[c, 0] = second[c, 0] + left[c, y]
        by_x.wait_recv()
        second[c, 1] = second[c, 1] + right[c, x]
        copy = copies.send(second.at[c, 1 - chip], third.at[c], to_z[0])
        yield
        copy.wait_recv()
        third[c] = third[c] + second[c, chip]
        summed = third
        for bit, partner in enumerate(to_z[1:]):
            buffer = fourth.at[bit]
            copy = copies.send(summed.at[c], buffer.at[c], partner)
            yield
            copy.wait_recv()
            buffer[c] = buffer[c] + summed[c]
            summed = buffer
        last[c, core, chip] = summed[c]
        copy = copies.send(summed.at[c], last.at[c, core, chip], to_z[0])
        yield
        copy.wait_recv()
        half = last.at[c, core]
        copy = copies.send(half, half, to_core)
        yield
        copy.wait_recv()
        target[q, :, :, :, lanes] = last[c].astype(full)

    def small_steps():
        source = small_ref
        for index, partner in enumerate(partners):
            copy = copies.send(source, small_in.at[index], partner)
            yield
            copy.wait_recv()
            small_in[index] = small_in[index] + source[...]
            source = small_in.at[index]
        small_out[...] = source[me]

    waiting = [small_steps()] + [steps(c) for c in range(len(chunks))]
    active = []
    while waiting or active:
        left_over = []
        for chain in active:
            try:
                next(chain)
                left_over.append(chain)
            except StopIteration:
                pass
        active = left_over
        for chain in waiting[:1] if active else waiting[:2]:
            next(chain)
            active.append(chain)
            waiting = waiting[1:]
    copies.finish()


def total(parts, small, chips, width):
    kinds, views, count = [], [], 0
    for part in parts:
        rows, columns = part.shape
        stack = rows // width
        kinds.append((stack, columns))
        views.append(part.reshape(2, 2, stack, 2, 2, rows // (16 * stack), columns))
        count += stack * (columns // width)
    piece = width // 16
    stages = chips.bit_length() - 1
    copies = count * (7 + stages + 1) + 3 + stages
    outs = [
        jax.ShapeDtypeStruct(view.shape[2:], full) for view in views
    ] + [jax.ShapeDtypeStruct(small.shape[1:], full)]
    vmem = pl.BlockSpec(memory_space=pltpu.VMEM)
    sums = pl.pallas_call(
        functools.partial(total_kernel, chips, tuple(kinds)),
        in_specs=[vmem] * (len(parts) + 1),
        out_specs=[vmem] * (len(parts) + 1),
        out_shape=outs,
        scratch_shapes=[
            pltpu.VMEM((count, 2, 2, 2, piece, width), low),
            pltpu.VMEM((count, 2, piece, width), low),
            pltpu.VMEM((count, 2, piece, width), low),
            pltpu.VMEM((count, 2, piece, width), low),
            pltpu.VMEM((count, piece, width), low),
            pltpu.VMEM((stages - 1, count, piece, width), low),
            pltpu.VMEM((count, 2, 2, piece, width), low),
            pltpu.VMEM((3 + stages,) + small.shape, full),
            pltpu.SemaphoreType.DMA((copies,)),
            pltpu.SemaphoreType.DMA((copies,)),
        ],
        compiler_params=pltpu.CompilerParams(
            collective_id=1, has_side_effects=True, vmem_limit_bytes=60 * 2**20
        ),
        name="total",
    )(*views, small)
    return [
        result.reshape(-1, part.shape[1]) for result, part in zip(sums, parts)
    ], sums[-1].reshape(-1)


def shards(
    groups,
    copies,
    tokens,
    segments,
    cotangent,
    qkv_weight,
    qkv_bias,
    out_weight,
    out_bias,
    up_weight,
    up_bias,
    down_weight,
    down_bias,
    first_gain,
    first_shift,
    second_gain,
    second_shift,
    query_gain,
    key_gain,
):
    vectors = [
        qkv_bias,
        out_bias,
        up_bias,
        down_bias,
        first_gain,
        first_shift,
        second_gain,
        second_shift,
        query_gain,
        key_gain,
    ]
    count, width = tokens.shape
    cut = spans(count)[0][1]
    crossing = jnp.any(segments[:cut, None] == segments[None, cut:])
    flag = crossing.astype(jnp.int32).reshape(1)
    column = segments.reshape(count, 1)
    valid = (segments >= 0)[:, None]

    small = jnp.concatenate(vectors).reshape(1, -1)
    gather = functools.partial(lax.all_gather, axis_name="fsdp", axis=0, tiled=True)
    up_w = gather(up_weight)
    kernels = groups == 4 and copies >= 8
    if kernels:
        qkv_w, out_w, small = fetch(qkv_weight, out_weight, small)
    else:
        qkv_w, out_w, small = gather(qkv_weight), gather(out_weight), gather(small)
    down_weight, small = lax.optimization_barrier((down_weight, small))
    down_w = gather(down_weight)
    whole, start = [], 0
    for vector in vectors:
        size = vector.shape[0]
        whole.append(small[:, start : start + size].reshape(-1).astype(full))
        start += size
    (qkv_b, out_b, up_b, down_b, gain_1, shift_1, gain_2, shift_2, gain_q, gain_k) = whole
    pair_q = jnp.tile(gain_q, 2).reshape(1, 128)
    pair_k = jnp.tile(gain_k, 2).reshape(1, 128)
    normed = layer_norm(tokens.astype(full), gain_1, shift_1).astype(low)
    mixed = (plain(normed, qkv_w) + qkv_b).astype(low)
    attended, log_total = attend(flag, mixed, column, pair_q, pair_k)
    inputs = tokens.astype(full)
    residual = inputs + plain(attended, out_w) + out_b
    second, second_back = jax.vjp(layer_norm, residual, gain_2, shift_2)
    second = second.astype(low)
    hidden = plain(second, up_w) + up_b
    active, gelu_back = jax.vjp(exact_gelu, hidden)
    active = active.astype(low)

    grad_low = jnp.where(valid, cotangent, jnp.zeros_like(cotangent))
    grad_output = grad_low.astype(full)
    down_b_grad = jnp.sum(grad_output, axis=0)
    down_grad = left_product(active, grad_low).astype(low)
    (grad_hidden,) = gelu_back(right_product(grad_low, down_w))
    grad_hidden = grad_hidden.astype(low)
    up_b_grad = jnp.sum(grad_hidden.astype(full), axis=0)
    output = jnp.where(valid, residual + plain(active, down_w) + down_b, 0.0).astype(low)
    up_grad = left_product(second, grad_hidden).astype(low)
    grad_norm_2, gain_2_grad, shift_2_grad = second_back(right_product(grad_hidden, up_w))
    grad_residual = grad_output + grad_norm_2
    branch = grad_residual.astype(low)
    out_b_grad = jnp.sum(branch.astype(full), axis=0)
    out_grad = left_product(attended, branch).astype(low)
    grad_attended = right_product(branch, out_w).astype(low)
    part, pair_gains = attend_back(
        flag,
        mixed,
        column,
        pair_q,
        pair_k,
        attended,
        log_total,
        grad_attended,
        0,
        width // 128,
    )
    qkv_grad = jnp.concatenate([left_product(normed, part[i]).astype(low) for i in range(3)], 1)
    gain_sums = jnp.sum(pair_gains, axis=0).reshape(2, 2, -1).sum(axis=1)
    qkv_b_grad = jnp.sum(part.astype(full), axis=1).reshape(-1)
    grad_input, sums_1 = input_grad(tokens, gain_1.reshape(1, -1), grad_residual, [part], qkv_w)
    vectors = [
        qkv_b_grad,
        out_b_grad,
        up_b_grad,
        down_b_grad,
        sums_1[0],
        sums_1[1],
        gain_2_grad,
        shift_2_grad,
        gain_sums[0],
        gain_sums[1],
    ]
    rows = jnp.concatenate([vector.reshape(groups, -1) for vector in vectors], axis=1)
    grads = [down_grad, up_grad, out_grad, qkv_grad]
    if kernels:
        grads, sums = total(grads, rows.reshape(groups, 1, -1), copies // 2, width)
    else:
        scatter = functools.partial(
            lax.psum_scatter, axis_name="fsdp", scatter_dimension=0, tiled=True
        )
        grads = [lax.psum(scatter(grad), ("z", "core")).astype(full) for grad in grads]
        sums = lax.psum(scatter(rows), ("z", "core")).reshape(-1)
    final, start = [], 0
    for vector in vectors:
        size = vector.shape[0] // groups
        final.append(sums[start : start + size])
        start += size
    return (
        output,
        grad_input,
        grads[3],
        final[0],
        grads[2],
        final[1],
        grads[1],
        final[2],
        grads[0],
        final[3],
        *final[4:],
    )


def solution(mesh):
    copies, groups = mesh.shape["dp"], mesh.shape["fsdp"]
    devices = mesh.devices.reshape(copies // 2, 2, groups)
    mesh = jax.sharding.Mesh(devices, ("z", "core", "fsdp"))
    rows = P(("z", "core", "fsdp"), None)
    matrix = P("fsdp", None)
    vector = P("fsdp")
    params = (matrix, vector) * 4 + (vector,) * 6
    return jax.shard_map(
        functools.partial(shards, groups, copies),
        mesh=mesh,
        in_specs=(rows, P(("z", "core", "fsdp")), rows) + params,
        out_specs=(rows, rows) + params,
        check_vma=False,
    )
```

```python
import functools

import jax
import jax.numpy as jnp
from jax import lax
from jax.experimental import pallas as pl
from jax.experimental.pallas import tpu as pltpu
from jax.sharding import PartitionSpec as P

norm_eps = 1e-06
low = jnp.bfloat16
full = jnp.float32


def layer_norm(value, gain, shift):
    centred = value - jnp.mean(value, axis=-1, keepdims=True)
    scaled = centred * lax.rsqrt(jnp.mean(centred * centred, axis=-1, keepdims=True) + norm_eps)
    return scaled * gain + shift


def exact_gelu(value):
    return jax.nn.gelu(value, approximate=False)


def left_product(left, right):
    return lax.dot_general(
        left, right, (((0,), (0,)), ((), ())), preferred_element_type=jnp.float32
    )


def right_product(left, right):
    return lax.dot_general(
        left, right, (((1,), (1,)), ((), ())), preferred_element_type=jnp.float32
    )


def plain(left, right):
    return jnp.dot(left, right, preferred_element_type=jnp.float32)


def lane_index(shape):
    return lax.broadcasted_iota(jnp.int32, shape, len(shape) - 1)


def same_head(scale):
    row = lax.broadcasted_iota(jnp.int32, (128, 128), 0) // 64
    column = lax.broadcasted_iota(jnp.int32, (128, 128), 1) // 64
    return jnp.where(row == column, scale, 0.0).astype(low)


def head_norm(raw, mean_map):
    value = raw.astype(full)
    centred = value - plain(raw, mean_map)
    scale = lax.rsqrt(plain((centred * centred).astype(low), mean_map) + norm_eps)
    return centred * scale, scale


def half_mask(head, lanes):
    return (lanes < 64) if head == 0 else (lanes >= 64)


def query_codes(segments, lanes):
    spot = lanes % 64
    match = jnp.where(spot == segments + 1, 128.0, 0.0)
    return jnp.where(spot == 17, -128.0, match)


def key_codes(segments, lanes):
    spot = lanes % 64
    match = jnp.where(spot == segments + 1, 1.0, 0.0)
    return jnp.where((spot >= 17) & (spot < 20), 1.0, match)


def spans(count):
    cut = count * 9 // 16
    return ((0, cut), (cut, count))


def attend_kernel(flag_ref, q_ref, k_ref, v_ref, seg_ref, gq_ref, gk_ref, o_ref, total_ref):
    count = q_ref.shape[0]
    lanes = lane_index((count, 128))
    mean_map = same_head(1.0 / 64)
    q_unit, _ = head_norm(q_ref[...], mean_map)
    k_unit, _ = head_norm(k_ref[...], mean_map)
    q_low = q_unit * (gq_ref[...] * 0.125)
    k_low = k_unit * gk_ref[...]
    segments = seg_ref[...]
    q_code = query_codes(segments, lanes)
    k_code = key_codes(segments, lanes)
    values = v_ref[...]
    q_heads = [jnp.where(half_mask(h, lanes), q_low, q_code).astype(low) for h in (0, 1)]
    k_heads = [jnp.where(half_mask(h, lanes), k_low, k_code).astype(low) for h in (0, 1)]
    v_heads = [
        jnp.where(half_mask(h, lanes), values.astype(full), 1.0).astype(low) for h in (0, 1)
    ]

    def run(first, last, keys_first, keys_last, tile):
        for start in range(first, last, tile):
            parts = []
            for h in (0, 1):
                scores = right_product(
                    q_heads[h][start : start + tile], k_heads[h][keys_first:keys_last]
                )
                parts.append(plain(jnp.exp(scores).astype(low), v_heads[h][keys_first:keys_last]))
            here = lane_index((tile, 128)) < 64
            raw = jnp.where(here, parts[0], parts[1])
            sums = jnp.where(here, parts[1], parts[0])
            total = pltpu.roll(sums, 64, 1)
            o_ref[start : start + tile] = (raw / total).astype(o_ref.dtype)
            total_ref[start : start + tile] = jnp.log(sums)

    @pl.when(flag_ref[0] == 0)
    def _():
        for first, last in spans(count):
            run(first, last, first, last, (last - first) // 2)

    @pl.when(flag_ref[0] != 0)
    def _():
        run(0, count, 0, count, 256)


def attend_back_kernel(
    flag_ref,
    q_ref,
    k_ref,
    v_ref,
    seg_ref,
    gq_ref,
    gk_ref,
    o_ref,
    total_ref,
    do_ref,
    grad_ref,
    gain_ref,
    dq_scr,
):
    count = q_ref.shape[0]
    lanes = lane_index((count, 128))
    spot = lanes % 64
    mean_map = same_head(1.0 / 64)
    q_unit, q_scale = head_norm(q_ref[...], mean_map)
    k_unit, k_scale = head_norm(k_ref[...], mean_map)
    q_low = (q_unit * (gq_ref[...] * 0.125)).astype(low)
    k_low = (k_unit * gk_ref[...]).astype(low)
    segments = seg_ref[...]
    log_total = total_ref[...]
    log_high = log_total.astype(low).astype(full)
    q_code = jnp.where(
        spot == 18,
        -log_high,
        jnp.where(spot == 19, log_high - log_total, query_codes(segments, lanes)),
    ).astype(low)
    k_code = key_codes(segments, lanes).astype(low)
    grads = do_ref[...]
    product = (grads.astype(full) * o_ref[...].astype(full)).astype(low)
    row = lax.broadcasted_iota(jnp.int32, (128, 128), 0) // 64
    column = lax.broadcasted_iota(jnp.int32, (128, 128), 1) // 64
    delta = plain(product, jnp.where(row != column, 1.0, 0.0).astype(low))
    delta_high = delta.astype(low).astype(full)
    g_code = jnp.where(
        spot == 0, -delta_high, jnp.where(spot == 1, delta_high - delta, 0.0)
    ).astype(low)
    v_code = jnp.where(spot < 2, 1.0, 0.0).astype(low)
    values = v_ref[...]
    masks = [half_mask(h, lanes) for h in (0, 1)]
    q_heads = [jnp.where(masks[h], q_low, q_code) for h in (0, 1)]
    k_heads = [jnp.where(masks[h], k_low, k_code) for h in (0, 1)]
    v_heads = [jnp.where(masks[h], values, v_code) for h in (0, 1)]
    g_heads = [jnp.where(masks[h], grads, g_code) for h in (0, 1)]
    dk_parts = []

    def run(first, last, other_first, other_last, tile):
        for start in range(first, last, tile):
            rows = slice(start, start + tile)
            others = slice(other_first, other_last)
            dv_parts, dk_parts, dq_parts = [], [], []
            for h in (0, 1):
                scores = right_product(k_heads[h][rows], q_heads[h][others])
                weights = jnp.exp(scores)
                change = right_product(v_heads[h][rows], g_heads[h][others])
                sloped = (weights * change).astype(low)
                dv_parts.append(plain(weights.astype(low), grads[others]))
                dk_parts.append(plain(sloped, q_low[others]))
                dq_parts.append(left_product(sloped, k_low[rows]))
            here = lane_index((tile, 128)) < 64
            there = lane_index((other_last - other_first, 128)) < 64
            grad_ref[2, rows] = jnp.where(here, dv_parts[0], dv_parts[1]).astype(low)
            dk = jnp.where(here, dk_parts[0], dk_parts[1])
            dk_scr_store(rows, dk)
            dq = jnp.where(there, dq_parts[0], dq_parts[1])
            if start == first:
                dq_scr[0, others] = dq
            else:
                dq_scr[0, others] += dq

    def dk_scr_store(rows, value):
        dq_scr[1, rows] = value

    @pl.when(flag_ref[0] == 0)
    def _():
        for first, last in spans(count):
            run(first, last, first, last, (last - first) // 2)

    @pl.when(flag_ref[0] != 0)
    def _():
        run(0, count, 0, count, 256)

    def norm_back(slot, factor, unit, scale, gain):
        slope = dq_scr[slot] * factor
        inner = slope * gain
        shared = inner * unit
        result = scale * (
            inner
            - plain(inner.astype(low), mean_map)
            - unit * plain(shared.astype(low), mean_map)
        )
        grad_ref[slot] = result.astype(low)
        gain_ref[0, slot : slot + 1] = jnp.sum(slope * unit, axis=0, keepdims=True)

    norm_back(0, 0.125, q_unit, q_scale, gq_ref[...])
    norm_back(1, 1.0, k_unit, k_scale, gk_ref[...])


def attend_specs(count, width, first=0):
    pairs = width // 128
    column = lambda offset: pl.BlockSpec((count, 128), lambda i, flag: (0, i + first + offset))
    fixed = lambda shape: pl.BlockSpec(shape, lambda i, flag: (0, 0))
    shared = [
        column(0),
        column(pairs),
        column(2 * pairs),
        fixed((count, 1)),
        fixed((1, 128)),
        fixed((1, 128)),
    ]
    return pairs, column, shared


def attend(flag, mixed, segments, gain_q, gain_k):
    count = mixed.shape[0]
    width = mixed.shape[1] // 3
    pairs, column, shared = attend_specs(count, width)
    return pl.pallas_call(
        attend_kernel,
        grid_spec=pltpu.PrefetchScalarGridSpec(
            num_scalar_prefetch=1,
            grid=(pairs,),
            in_specs=shared,
            out_specs=[column(0), column(0)],
        ),
        out_shape=[
            jax.ShapeDtypeStruct((count, width), low),
            jax.ShapeDtypeStruct((count, width), full),
        ],
        compiler_params=pltpu.CompilerParams(vmem_limit_bytes=50 * 2**20),
        cost_estimate=pl.CostEstimate(
            flops=16 * count * count * width,
            bytes_accessed=count * width * 12,
            transcendentals=count * count * width // 64,
        ),
        name="attend",
    )(flag, mixed, mixed, mixed, segments, gain_q, gain_k)


def attend_back(flag, mixed, segments, gain_q, gain_k, attended, log_total, grad, first, pairs):
    count = mixed.shape[0]
    width = mixed.shape[1] // 3
    _, column, shared = attend_specs(count, width, first)
    return pl.pallas_call(
        attend_back_kernel,
        grid_spec=pltpu.PrefetchScalarGridSpec(
            num_scalar_prefetch=1,
            grid=(pairs,),
            in_specs=shared + [column(0), column(0), column(0)],
            out_specs=[
                pl.BlockSpec((3, count, 128), lambda i, flag: (0, 0, i)),
                pl.BlockSpec((1, 2, 128), lambda i, flag: (i, 0, 0)),
            ],
            scratch_shapes=[pltpu.VMEM((2, count, 128), full)],
        ),
        out_shape=[
            jax.ShapeDtypeStruct((3, count, pairs * 128), low),
            jax.ShapeDtypeStruct((pairs, 2, 128), full),
        ],
        compiler_params=pltpu.CompilerParams(vmem_limit_bytes=50 * 2**20),
        cost_estimate=pl.CostEstimate(
            flops=40 * count * count * pairs * 128,
            bytes_accessed=count * pairs * 128 * 18,
            transcendentals=count * count * pairs * 2,
        ),
        name="attend_back",
    )(flag, mixed, mixed, mixed, segments, gain_q, gain_k, attended, log_total, grad)


def input_grad_kernel(tokens_ref, gain_ref, above_ref, *refs):
    parts, (weight_ref, out_ref, sums_ref) = refs[:-3], refs[-3:]
    width = tokens_ref.shape[1]
    size = width // len(parts)
    slope = 0.0
    for p, part_ref in enumerate(parts):
        for kind in range(3):
            start = kind * width + p * size
            slope += right_product(part_ref[kind], weight_ref[:, start : start + size])
    value = tokens_ref[...].astype(full)
    centred = value - jnp.mean(value, axis=-1, keepdims=True)
    scale = lax.rsqrt(jnp.mean(centred * centred, axis=-1, keepdims=True) + norm_eps)
    unit = centred * scale
    inner = slope * gain_ref[...]
    shared = slope * unit
    back = scale * (
        inner
        - jnp.mean(inner, axis=-1, keepdims=True)
        - unit * jnp.mean(inner * unit, axis=-1, keepdims=True)
    )
    out_ref[...] = (above_ref[...] + back).astype(out_ref.dtype)
    sums = jnp.concatenate(
        [jnp.sum(shared, axis=0, keepdims=True), jnp.sum(slope, axis=0, keepdims=True)]
    )
    first = pl.program_id(0) == 0

    @pl.when(first)
    def _():
        sums_ref[...] = sums

    @pl.when(jnp.logical_not(first))
    def _():
        sums_ref[...] += sums


def input_grad(tokens, gain, above, parts, weight):
    count, width = tokens.shape
    tile = min(256, count)
    rows = pl.BlockSpec((tile, width), lambda i: (i, 0))
    whole = lambda array: pl.BlockSpec(array.shape, lambda i: (0, 0))
    return pl.pallas_call(
        input_grad_kernel,
        grid=(count // tile,),
        in_specs=[rows, whole(gain), rows]
        + [pl.BlockSpec((3, tile, part.shape[2]), lambda i: (0, i, 0)) for part in parts]
        + [whole(weight)],
        out_specs=[rows, pl.BlockSpec((2, width), lambda i: (0, 0))],
        out_shape=[
            jax.ShapeDtypeStruct((count, width), low),
            jax.ShapeDtypeStruct((2, width), full),
        ],
        compiler_params=pltpu.CompilerParams(vmem_limit_bytes=50 * 2**20),
        cost_estimate=pl.CostEstimate(
            flops=6 * count * width * width,
            bytes_accessed=count * width * 14 + 6 * width * width,
            transcendentals=0,
        ),
        name="input_grad",
    )(tokens, gain, above, *parts, weight)


def gelu_terms(value):
    size = jnp.abs(value)
    t = 1.0 / (1.0 + 0.3275911 * 0.70710678118 * size)
    expo = jnp.exp(-0.5 * value * value)
    series = 0.254829592 + t * (
        -0.284496736 + t * (1.421413741 + t * (-1.453152027 + t * 1.061405429))
    )
    below = 0.5 * t * series * expo
    share = jnp.where(value >= 0.0, 1.0 - below, below)
    return value * share, share + value * expo * 0.3989422804


def expand_kernel(rows_ref, weight_ref, shift_ref, active_ref, slope_ref):
    rows = rows_ref[...]
    columns = weight_ref.shape[1]
    tile = 256
    for start in range(0, columns, tile):
        span = slice(start, start + tile)
        hidden = plain(rows, weight_ref[:, span]) + shift_ref[:, span]
        active, slope = gelu_terms(hidden)
        active_ref[:, span] = active.astype(low)
        slope_ref[:, span] = slope.astype(low)


def expand(rows, weight, shift):
    count, width = rows.shape
    columns = weight.shape[1]
    tile = min(256, count)
    block = pl.BlockSpec((tile, columns), lambda i: (i, 0))
    return pl.pallas_call(
        expand_kernel,
        grid=(count // tile,),
        in_specs=[
            pl.BlockSpec((tile, width), lambda i: (i, 0)),
            pl.BlockSpec((width, columns), lambda i: (0, 0)),
            pl.BlockSpec((1, columns), lambda i: (0, 0)),
        ],
        out_specs=[block, block],
        out_shape=[jax.ShapeDtypeStruct((count, columns), low)] * 2,
        compiler_params=pltpu.CompilerParams(vmem_limit_bytes=40 * 2**20),
        cost_estimate=pl.CostEstimate(
            flops=2 * count * width * columns,
            bytes_accessed=2 * width * columns + 4 * count * columns,
            transcendentals=2 * count * columns,
        ),
        name="expand",
    )(rows, weight, shift.reshape(1, -1))


def place(axis, bit):
    return lax.rem(lax.div(lax.axis_index(axis), 1 << bit), 2)


def across(axis, bit):
    index = lax.axis_index(axis)
    return {axis: index + (1 - 2 * place(axis, bit)) * (1 << bit)}


def greet(partners):
    barrier = pltpu.get_barrier_semaphore()
    for partner in partners:
        pl.semaphore_signal(
            barrier, inc=1, device_id=partner, device_id_type=pl.DeviceIdType.MESH
        )
    pl.semaphore_wait(barrier, len(partners))


class Copies:
    def __init__(self, send_sems, recv_sems):
        self.send_sems, self.recv_sems = send_sems, recv_sems
        self.all = []

    def send(self, source, target, partner):
        index = len(self.all)
        copy = pltpu.make_async_remote_copy(
            src_ref=source,
            dst_ref=target,
            send_sem=self.send_sems.at[index],
            recv_sem=self.recv_sems.at[index],
            device_id=partner,
            device_id_type=pl.DeviceIdType.MESH,
        )
        copy.start()
        self.all.append(copy)
        return copy

    def finish(self):
        for copy in self.all:
            copy.wait_send()


def fetch_kernel(qkv_ref, out_ref, small_ref, qkv_all, out_all, small_all, send, recv, local):
    core, x, y = place("core", 0), place("fsdp", 0), place("fsdp", 1)
    me = lax.axis_index("fsdp")
    to_core, to_x, to_y = across("core", 0), across("fsdp", 0), across("fsdp", 1)
    to_far = {"fsdp": 3 - me}
    greet([to_core, to_x, to_y, to_far])
    copies = Copies(send, recv)
    arrivals = []
    for partner in (to_x, to_y, to_far):
        arrivals.append(copies.send(small_ref, small_all.at[me], partner))
    whole = ((qkv_ref, qkv_all), (out_ref, out_all))
    from_x_row, from_y_row, far_row = 2 * y + 1 - x, 2 * (1 - y) + x, 3 - me
    near = []
    for own, target in whole:
        mine = own.at[core]
        near.append(
            (
                copies.send(mine, target.at[me, core], to_x),
                copies.send(mine, target.at[me, core], to_y),
            )
        )
    own_copies = [
        pltpu.make_async_copy(own, target.at[me], local.at[i])
        for i, (own, target) in enumerate(whole + ((small_ref, small_all),))
    ]
    for copy in own_copies:
        copy.start()
    far = []
    for (own, target), (by_x, by_y) in zip(whole, near):
        by_x.wait_recv()
        quarter = target.at[from_x_row, core, 0]
        low_far = copies.send(quarter, quarter, to_y)
        half = target.at[from_x_row, core]
        arrivals.append(copies.send(half, half, to_core))
        by_y.wait_recv()
        quarter = target.at[from_y_row, core, 1]
        high_far = copies.send(quarter, quarter, to_x)
        half = target.at[from_y_row, core]
        arrivals.append(copies.send(half, half, to_core))
        far.append((low_far, high_far))
    for (own, target), (low_far, high_far) in zip(whole, far):
        low_far.wait_recv()
        high_far.wait_recv()
        half = target.at[far_row, core]
        arrivals.append(copies.send(half, half, to_core))
    for copy in arrivals:
        copy.wait_recv()
    for copy in own_copies:
        copy.wait()
    copies.finish()


def fetch(qkv_weight, out_weight, small):
    def split(part):
        rows, columns = part.shape
        return part.reshape(2, 2, rows // 4, columns)

    parts = (split(qkv_weight), split(out_weight), small)
    count = 3 + 2 * 7
    qkv_w, out_w, vectors = pl.pallas_call(
        fetch_kernel,
        in_specs=[pl.BlockSpec(memory_space=pltpu.VMEM)] * 3,
        out_specs=[pl.BlockSpec(memory_space=pltpu.VMEM)] * 3,
        out_shape=[jax.ShapeDtypeStruct((4,) + part.shape, part.dtype) for part in parts],
        scratch_shapes=[
            pltpu.SemaphoreType.DMA((count,)),
            pltpu.SemaphoreType.DMA((count,)),
            pltpu.SemaphoreType.DMA((3,)),
        ],
        compiler_params=pltpu.CompilerParams(
            collective_id=0, has_side_effects=True, vmem_limit_bytes=24 * 2**20
        ),
        name="fetch",
    )(*parts)
    return (
        qkv_w.reshape(-1, qkv_weight.shape[1]),
        out_w.reshape(-1, out_weight.shape[1]),
        vectors.reshape(4, -1),
    )


def total_kernel(chips, width, kinds, *refs):
    count = len(kinds)
    ins, small_ref = refs[:count], refs[count]
    outs, small_out = refs[count + 1 : 2 * count + 1], refs[2 * count + 1]
    first, left, right, second, third, fourth, last, small_in, send, recv = refs[2 * count + 2 :]
    core, x, y, chip = place("core", 0), place("fsdp", 0), place("fsdp", 1), place("z", 0)
    me = lax.axis_index("fsdp")
    to_core, to_x, to_y = across("core", 0), across("fsdp", 0), across("fsdp", 1)
    to_z = [across("z", bit) for bit in range(chips.bit_length() - 1)]
    partners = [to_core, to_x, to_y] + to_z
    greet(partners)
    copies = Copies(send, recv)

    chunks = []
    for index, kind in enumerate(kinds):
        stack, columns = kind
        for q in range(stack):
            for p in range(columns // width):
                span = slice(p * width, (p + 1) * width)
                chunks.append((ins[index], outs[index], q, span))

    def steps(c):
        source, target, q, span = chunks[c]
        lanes = pl.ds(span.start, width)
        copy = copies.send(source.at[:, :, q, 1 - core, :, :, lanes], first.at[c], to_core)
        yield
        copy.wait_recv()
        for row in range(2):
            first[c, row] = first[c, row] + source[row, :, q, core, :, :, lanes]
        by_x = copies.send(first.at[c, :, 1 - x, 0], left.at[c], to_x)
        by_y = copies.send(first.at[c, 1 - y, :, 1], right.at[c], to_y)
        yield
        by_x.wait_recv()
        left[c] = left[c] + first[c, :, x, 0]
        by_y.wait_recv()
        right[c] = right[c] + first[c, y, :, 1]
        by_y = copies.send(left.at[c, 1 - y], second.at[c, 0], to_y)
        by_x = copies.send(right.at[c, 1 - x], second.at[c, 1], to_x)
        yield
        by_y.wait_recv()
        second[c, 0] = second[c, 0] + left[c, y]
        by_x.wait_recv()
        second[c, 1] = second[c, 1] + right[c, x]
        copy = copies.send(second.at[c, 1 - chip], third.at[c], to_z[0])
        yield
        copy.wait_recv()
        third[c] = third[c] + second[c, chip]
        summed = third
        for bit, partner in enumerate(to_z[1:]):
            buffer = fourth.at[bit]
            copy = copies.send(summed.at[c], buffer.at[c], partner)
            yield
            copy.wait_recv()
            buffer[c] = buffer[c] + summed[c]
            summed = buffer
        last[c, core, chip] = summed[c]
        copy = copies.send(summed.at[c], last.at[c, core, chip], to_z[0])
        yield
        copy.wait_recv()
        half = last.at[c, core]
        copy = copies.send(half, half, to_core)
        yield
        copy.wait_recv()
        target[q, :, :, :, lanes] = last[c].astype(full)

    def small_steps():
        source = small_ref
        for index, partner in enumerate(partners):
            copy = copies.send(source, small_in.at[index], partner)
            yield
            copy.wait_recv()
            small_in[index] = small_in[index] + source[...]
            source = small_in.at[index]
        small_out[...] = source[me]

    waiting = [small_steps()] + [steps(c) for c in range(len(chunks))]
    active = []
    while waiting or active:
        left_over = []
        for chain in active:
            try:
                next(chain)
                left_over.append(chain)
            except StopIteration:
                pass
        active = left_over
        for chain in waiting[:1] if active else waiting[:2]:
            next(chain)
            active.append(chain)
            waiting = waiting[1:]
    copies.finish()


def total(parts, small, chips, height, width):
    kinds, views, count = [], [], 0
    for part in parts:
        rows, columns = part.shape
        stack = rows // height
        kinds.append((stack, columns))
        views.append(part.reshape(2, 2, stack, 2, 2, rows // (16 * stack), columns))
        count += stack * (columns // width)
    piece = height // 16
    stages = chips.bit_length() - 1
    copies = count * (7 + stages + 1) + 3 + stages
    outs = [
        jax.ShapeDtypeStruct(view.shape[2:], full) for view in views
    ] + [jax.ShapeDtypeStruct(small.shape[1:], full)]
    vmem = pl.BlockSpec(memory_space=pltpu.VMEM)
    sums = pl.pallas_call(
        functools.partial(total_kernel, chips, width, tuple(kinds)),
        in_specs=[vmem] * (len(parts) + 1),
        out_specs=[vmem] * (len(parts) + 1),
        out_shape=outs,
        scratch_shapes=[
            pltpu.VMEM((count, 2, 2, 2, piece, width), low),
            pltpu.VMEM((count, 2, piece, width), low),
            pltpu.VMEM((count, 2, piece, width), low),
            pltpu.VMEM((count, 2, piece, width), low),
            pltpu.VMEM((count, piece, width), low),
            pltpu.VMEM((stages - 1, count, piece, width), low),
            pltpu.VMEM((count, 2, 2, piece, width), low),
            pltpu.VMEM((3 + stages,) + small.shape, full),
            pltpu.SemaphoreType.DMA((copies,)),
            pltpu.SemaphoreType.DMA((copies,)),
        ],
        compiler_params=pltpu.CompilerParams(
            collective_id=1, has_side_effects=True, vmem_limit_bytes=60 * 2**20
        ),
        name="total",
    )(*views, small)
    return [
        result.reshape(-1, part.shape[1]) for result, part in zip(sums, parts)
    ], sums[-1].reshape(-1)


def shards(
    groups,
    copies,
    tokens,
    segments,
    cotangent,
    qkv_weight,
    qkv_bias,
    out_weight,
    out_bias,
    up_weight,
    up_bias,
    down_weight,
    down_bias,
    first_gain,
    first_shift,
    second_gain,
    second_shift,
    query_gain,
    key_gain,
):
    vectors = [
        qkv_bias,
        out_bias,
        up_bias,
        down_bias,
        first_gain,
        first_shift,
        second_gain,
        second_shift,
        query_gain,
        key_gain,
    ]
    count, width = tokens.shape
    cut = spans(count)[0][1]
    crossing = jnp.any(segments[:cut, None] == segments[None, cut:])
    flag = crossing.astype(jnp.int32).reshape(1)
    column = segments.reshape(count, 1)
    valid = (segments >= 0)[:, None]

    small = jnp.concatenate(vectors).reshape(1, -1)
    gather = functools.partial(lax.all_gather, axis_name="fsdp", axis=0, tiled=True)
    up_w = gather(up_weight)
    kernels = groups == 4 and copies >= 8
    if kernels:
        qkv_w, out_w, small = fetch(qkv_weight, out_weight, small)
    else:
        qkv_w, out_w, small = gather(qkv_weight), gather(out_weight), gather(small)
    down_weight, small = lax.optimization_barrier((down_weight, small))
    down_w = gather(down_weight)
    whole, start = [], 0
    for vector in vectors:
        size = vector.shape[0]
        whole.append(small[:, start : start + size].reshape(-1).astype(full))
        start += size
    (qkv_b, out_b, up_b, down_b, gain_1, shift_1, gain_2, shift_2, gain_q, gain_k) = whole
    pair_q = jnp.tile(gain_q, 2).reshape(1, 128)
    pair_k = jnp.tile(gain_k, 2).reshape(1, 128)
    normed = layer_norm(tokens.astype(full), gain_1, shift_1).astype(low)
    mixed = (plain(normed, qkv_w) + qkv_b).astype(low)
    attended, log_total = attend(flag, mixed, column, pair_q, pair_k)
    inputs = tokens.astype(full)
    residual = inputs + plain(attended, out_w) + out_b
    second, second_back = jax.vjp(layer_norm, residual, gain_2, shift_2)
    second = second.astype(low)
    active, slope = expand(second, up_w, up_b)

    grad_low = jnp.where(valid, cotangent, jnp.zeros_like(cotangent))
    grad_output = grad_low.astype(full)
    down_b_grad = jnp.sum(grad_output, axis=0)
    down_grad = left_product(active, grad_low).astype(low)
    grad_hidden = (right_product(grad_low, down_w) * slope.astype(full)).astype(low)
    up_b_grad = jnp.sum(grad_hidden.astype(full), axis=0)
    output = jnp.where(valid, residual + plain(active, down_w) + down_b, 0.0).astype(low)
    up_grad = left_product(second, grad_hidden).astype(low)
    grad_norm_2, gain_2_grad, shift_2_grad = second_back(right_product(grad_hidden, up_w))
    grad_residual = grad_output + grad_norm_2
    branch = grad_residual.astype(low)
    out_b_grad = jnp.sum(branch.astype(full), axis=0)
    out_grad = left_product(attended, branch).astype(low)
    grad_attended = right_product(branch, out_w).astype(low)
    part, pair_gains = attend_back(
        flag,
        mixed,
        column,
        pair_q,
        pair_k,
        attended,
        log_total,
        grad_attended,
        0,
        width // 128,
    )
    qkv_grad = jnp.concatenate([left_product(normed, part[i]).astype(low) for i in range(3)], 1)
    gain_sums = jnp.sum(pair_gains, axis=0).reshape(2, 2, -1).sum(axis=1)
    qkv_b_grad = jnp.sum(part.astype(full), axis=1).reshape(-1)
    grad_input, sums_1 = input_grad(tokens, gain_1.reshape(1, -1), grad_residual, [part], qkv_w)
    vectors = [
        qkv_b_grad,
        out_b_grad,
        up_b_grad,
        down_b_grad,
        sums_1[0],
        sums_1[1],
        gain_2_grad,
        shift_2_grad,
        gain_sums[0],
        gain_sums[1],
    ]
    rows = jnp.concatenate([vector.reshape(groups, -1) for vector in vectors], axis=1)
    grads = [down_grad, up_grad, out_grad, qkv_grad]
    if kernels:
        grads, sums = total(grads, rows.reshape(groups, 1, -1), copies // 2, width, width // 2)
    else:
        scatter = functools.partial(
            lax.psum_scatter, axis_name="fsdp", scatter_dimension=0, tiled=True
        )
        grads = [lax.psum(scatter(grad), ("z", "core")).astype(full) for grad in grads]
        sums = lax.psum(scatter(rows), ("z", "core")).reshape(-1)
    final, start = [], 0
    for vector in vectors:
        size = vector.shape[0] // groups
        final.append(sums[start : start + size])
        start += size
    return (
        output,
        grad_input,
        grads[3],
        final[0],
        grads[2],
        final[1],
        grads[1],
        final[2],
        grads[0],
        final[3],
        *final[4:],
    )


def solution(mesh):
    copies, groups = mesh.shape["dp"], mesh.shape["fsdp"]
    devices = mesh.devices.reshape(copies // 2, 2, groups)
    mesh = jax.sharding.Mesh(devices, ("z", "core", "fsdp"))
    rows = P(("z", "core", "fsdp"), None)
    matrix = P("fsdp", None)
    vector = P("fsdp")
    params = (matrix, vector) * 4 + (vector,) * 6
    return jax.shard_map(
        functools.partial(shards, groups, copies),
        mesh=mesh,
        in_specs=(rows, P(("z", "core", "fsdp")), rows) + params,
        out_specs=(rows, rows) + params,
        check_vma=False,
    )
```

```python
import functools

import jax
import jax.numpy as jnp
from jax import lax
from jax.experimental import pallas as pl
from jax.experimental.pallas import tpu as pltpu
from jax.sharding import PartitionSpec as P

norm_eps = 1e-06
low = jnp.bfloat16
full = jnp.float32


def layer_norm(value, gain, shift):
    centred = value - jnp.mean(value, axis=-1, keepdims=True)
    scaled = centred * lax.rsqrt(jnp.mean(centred * centred, axis=-1, keepdims=True) + norm_eps)
    return scaled * gain + shift


def exact_gelu(value):
    return jax.nn.gelu(value, approximate=False)


def left_product(left, right):
    return lax.dot_general(
        left, right, (((0,), (0,)), ((), ())), preferred_element_type=jnp.float32
    )


def right_product(left, right):
    return lax.dot_general(
        left, right, (((1,), (1,)), ((), ())), preferred_element_type=jnp.float32
    )


def plain(left, right):
    return jnp.dot(left, right, preferred_element_type=jnp.float32)


def lane_index(shape):
    return lax.broadcasted_iota(jnp.int32, shape, len(shape) - 1)


def same_head(scale):
    row = lax.broadcasted_iota(jnp.int32, (128, 128), 0) // 64
    column = lax.broadcasted_iota(jnp.int32, (128, 128), 1) // 64
    return jnp.where(row == column, scale, 0.0).astype(low)


def head_norm(raw, mean_map):
    value = raw.astype(full)
    centred = value - plain(raw, mean_map)
    scale = lax.rsqrt(plain((centred * centred).astype(low), mean_map) + norm_eps)
    return centred * scale, scale


def half_mask(head, lanes):
    return (lanes < 64) if head == 0 else (lanes >= 64)


def query_codes(segments, lanes):
    spot = lanes % 64
    match = jnp.where(spot == segments + 1, 128.0, 0.0)
    return jnp.where(spot == 17, -128.0, match)


def key_codes(segments, lanes):
    spot = lanes % 64
    match = jnp.where(spot == segments + 1, 1.0, 0.0)
    return jnp.where((spot >= 17) & (spot < 20), 1.0, match)


def spans(count):
    cut = count * 9 // 16
    return ((0, cut), (cut, count))


def attend_pair(queries, keys, values, segments, gain_q, gain_k, store):
    count = queries.shape[0]
    lanes = lane_index((count, 128))
    mean_map = same_head(1.0 / 64)
    q_unit, _ = head_norm(queries, mean_map)
    k_unit, _ = head_norm(keys, mean_map)
    q_low = q_unit * (gain_q * 0.125)
    k_low = k_unit * gain_k
    q_code = query_codes(segments, lanes)
    k_code = key_codes(segments, lanes)
    q_heads = [jnp.where(half_mask(h, lanes), q_low, q_code).astype(low) for h in (0, 1)]
    k_heads = [jnp.where(half_mask(h, lanes), k_low, k_code).astype(low) for h in (0, 1)]
    v_heads = [
        jnp.where(half_mask(h, lanes), values.astype(full), 1.0).astype(low) for h in (0, 1)
    ]
    for first, last in spans(count):
        tile = (last - first) // 2
        for start in range(first, last, tile):
            parts = []
            for h in (0, 1):
                scores = right_product(q_heads[h][start : start + tile], k_heads[h][first:last])
                parts.append(plain(jnp.exp(scores).astype(low), v_heads[h][first:last]))
            here = lane_index((tile, 128)) < 64
            raw = jnp.where(here, parts[0], parts[1])
            sums = jnp.where(here, parts[1], parts[0])
            total = pltpu.roll(sums, 64, 1)
            store(slice(start, start + tile), raw / total, jnp.log(sums))


def attend_kernel(fetching, mixed_ref, seg_ref, gq_ref, gk_ref, *refs):
    if fetching:
        own_ref, o_ref, total_ref, all_ref, send, recv, local = refs
        arrivals = fetch_steps(((own_ref, all_ref),), send, recv, local)
        next(arrivals)
    else:
        o_ref, total_ref = refs
    width = o_ref.shape[1]
    pairs = width // 128

    def one(i, carry):
        def columns(kind):
            return pl.ds(pl.multiple_of(kind * width + i * 128, 128), 128)

        def store(rows, value, log_total):
            o_ref[rows, columns(0)] = value.astype(low)
            total_ref[rows, columns(0)] = log_total

        attend_pair(
            mixed_ref[:, columns(0)],
            mixed_ref[:, columns(1)],
            mixed_ref[:, columns(2)],
            seg_ref[...],
            gq_ref[...],
            gk_ref[...],
            store,
        )
        return carry

    part = 2 * pairs // 3
    lax.fori_loop(0, part, one, 0)
    if fetching:
        next(arrivals)
    lax.fori_loop(part, pairs, one, 0)
    if fetching:
        for _ in arrivals:
            pass


def attend_back_kernel(
    q_ref,
    k_ref,
    v_ref,
    seg_ref,
    gq_ref,
    gk_ref,
    o_ref,
    total_ref,
    do_ref,
    grad_ref,
    gain_ref,
    dq_scr,
):
    count = q_ref.shape[0]
    lanes = lane_index((count, 128))
    spot = lanes % 64
    mean_map = same_head(1.0 / 64)
    q_unit, q_scale = head_norm(q_ref[...], mean_map)
    k_unit, k_scale = head_norm(k_ref[...], mean_map)
    q_low = (q_unit * (gq_ref[...] * 0.125)).astype(low)
    k_low = (k_unit * gk_ref[...]).astype(low)
    segments = seg_ref[...]
    log_total = total_ref[...]
    log_high = log_total.astype(low).astype(full)
    q_code = jnp.where(
        spot == 18,
        -log_high,
        jnp.where(spot == 19, log_high - log_total, query_codes(segments, lanes)),
    ).astype(low)
    k_code = key_codes(segments, lanes).astype(low)
    grads = do_ref[...]
    product = (grads.astype(full) * o_ref[...].astype(full)).astype(low)
    row = lax.broadcasted_iota(jnp.int32, (128, 128), 0) // 64
    column = lax.broadcasted_iota(jnp.int32, (128, 128), 1) // 64
    delta = plain(product, jnp.where(row != column, 1.0, 0.0).astype(low))
    delta_high = delta.astype(low).astype(full)
    g_code = jnp.where(
        spot == 0, -delta_high, jnp.where(spot == 1, delta_high - delta, 0.0)
    ).astype(low)
    v_code = jnp.where(spot < 2, 1.0, 0.0).astype(low)
    values = v_ref[...]
    masks = [half_mask(h, lanes) for h in (0, 1)]
    q_heads = [jnp.where(masks[h], q_low, q_code) for h in (0, 1)]
    k_heads = [jnp.where(masks[h], k_low, k_code) for h in (0, 1)]
    v_heads = [jnp.where(masks[h], values, v_code) for h in (0, 1)]
    g_heads = [jnp.where(masks[h], grads, g_code) for h in (0, 1)]
    dk_parts = []

    def run(first, last, other_first, other_last, tile):
        for start in range(first, last, tile):
            rows = slice(start, start + tile)
            others = slice(other_first, other_last)
            dv_parts, dk_parts, dq_parts = [], [], []
            for h in (0, 1):
                scores = right_product(k_heads[h][rows], q_heads[h][others])
                weights = jnp.exp(scores)
                change = right_product(v_heads[h][rows], g_heads[h][others])
                sloped = (weights * change).astype(low)
                dv_parts.append(plain(weights.astype(low), grads[others]))
                dk_parts.append(plain(sloped, q_low[others]))
                dq_parts.append(left_product(sloped, k_low[rows]))
            here = lane_index((tile, 128)) < 64
            there = lane_index((other_last - other_first, 128)) < 64
            grad_ref[2, rows] = jnp.where(here, dv_parts[0], dv_parts[1]).astype(low)
            dk = jnp.where(here, dk_parts[0], dk_parts[1])
            dk_scr_store(rows, dk)
            dq = jnp.where(there, dq_parts[0], dq_parts[1])
            if start == first:
                dq_scr[0, others] = dq
            else:
                dq_scr[0, others] += dq

    def dk_scr_store(rows, value):
        dq_scr[1, rows] = value

    for first, last in spans(count):
        run(first, last, first, last, (last - first) // 2)

    def norm_back(slot, factor, unit, scale, gain):
        slope = dq_scr[slot] * factor
        inner = slope * gain
        shared = inner * unit
        result = scale * (
            inner
            - plain(inner.astype(low), mean_map)
            - unit * plain(shared.astype(low), mean_map)
        )
        grad_ref[slot] = result.astype(low)
        gain_ref[0, slot : slot + 1] = jnp.sum(slope * unit, axis=0, keepdims=True)

    norm_back(0, 0.125, q_unit, q_scale, gq_ref[...])
    norm_back(1, 1.0, k_unit, k_scale, gk_ref[...])


def attend_specs(count, width, first=0):
    pairs = width // 128
    column = lambda offset: pl.BlockSpec((count, 128), lambda i: (0, i + first + offset))
    fixed = lambda shape: pl.BlockSpec(shape, lambda i: (0, 0))
    shared = [
        column(0),
        column(pairs),
        column(2 * pairs),
        fixed((count, 1)),
        fixed((1, 128)),
        fixed((1, 128)),
    ]
    return pairs, column, shared


VMEM = pl.BlockSpec(memory_space=pltpu.VMEM)


def attend(mixed, segments, gain_q, gain_k, weight, identity):
    count = mixed.shape[0]
    width = mixed.shape[1] // 3
    fetching = weight is not None
    extra = fetch_parts((weight,)) if fetching else ((), [], [])
    result = list(pl.pallas_call(
        functools.partial(attend_kernel, fetching),
        in_specs=[VMEM] * (4 + len(extra[0])),
        out_specs=[VMEM] * (2 + len(extra[1])),
        out_shape=[
            jax.ShapeDtypeStruct((count, width), low),
            jax.ShapeDtypeStruct((count, width), full),
        ]
        + extra[1],
        scratch_shapes=extra[2],
        compiler_params=sender(identity if fetching else None),
        cost_estimate=pl.CostEstimate(
            flops=16 * count * count * width,
            bytes_accessed=count * width * 12,
            transcendentals=count * count * width // 64,
        ),
        name="attend",
    )(mixed, segments, gain_q, gain_k, *extra[0]))
    if fetching:
        result[2] = result[2].reshape(-1, weight.shape[1])
    return result


def attend_back(mixed, segments, gain_q, gain_k, attended, log_total, grad, first, pairs):
    count = mixed.shape[0]
    width = mixed.shape[1] // 3
    _, column, shared = attend_specs(count, width, first)
    return pl.pallas_call(
        attend_back_kernel,
        grid=(pairs,),
        in_specs=shared + [column(0), column(0), column(0)],
        out_specs=[
            pl.BlockSpec((3, count, 128), lambda i: (0, 0, i)),
            pl.BlockSpec((1, 2, 128), lambda i: (i, 0, 0)),
        ],
        scratch_shapes=[pltpu.VMEM((2, count, 128), full)],
        out_shape=[
            jax.ShapeDtypeStruct((3, count, pairs * 128), low),
            jax.ShapeDtypeStruct((pairs, 2, 128), full),
        ],
        compiler_params=pltpu.CompilerParams(vmem_limit_bytes=50 * 2**20),
        cost_estimate=pl.CostEstimate(
            flops=40 * count * count * pairs * 128,
            bytes_accessed=count * pairs * 128 * 18,
            transcendentals=count * count * pairs * 2,
        ),
        name="attend_back",
    )(mixed, mixed, mixed, segments, gain_q, gain_k, attended, log_total, grad)


def input_grad_kernel(tokens_ref, gain_ref, above_ref, *refs):
    parts, (weight_ref, out_ref, sums_ref) = refs[:-3], refs[-3:]
    width = tokens_ref.shape[1]
    size = width // len(parts)
    slope = 0.0
    for p, part_ref in enumerate(parts):
        for kind in range(3):
            start = kind * width + p * size
            slope += right_product(part_ref[kind], weight_ref[:, start : start + size])
    value = tokens_ref[...].astype(full)
    centred = value - jnp.mean(value, axis=-1, keepdims=True)
    scale = lax.rsqrt(jnp.mean(centred * centred, axis=-1, keepdims=True) + norm_eps)
    unit = centred * scale
    inner = slope * gain_ref[...]
    shared = slope * unit
    back = scale * (
        inner
        - jnp.mean(inner, axis=-1, keepdims=True)
        - unit * jnp.mean(inner * unit, axis=-1, keepdims=True)
    )
    out_ref[...] = (above_ref[...] + back).astype(out_ref.dtype)
    sums = jnp.concatenate(
        [jnp.sum(shared, axis=0, keepdims=True), jnp.sum(slope, axis=0, keepdims=True)]
    )
    first = pl.program_id(0) == 0

    @pl.when(first)
    def _():
        sums_ref[...] = sums

    @pl.when(jnp.logical_not(first))
    def _():
        sums_ref[...] += sums


def input_grad(tokens, gain, above, parts, weight):
    count, width = tokens.shape
    tile = min(256, count)
    rows = pl.BlockSpec((tile, width), lambda i: (i, 0))
    whole = lambda array: pl.BlockSpec(array.shape, lambda i: (0, 0))
    return pl.pallas_call(
        input_grad_kernel,
        grid=(count // tile,),
        in_specs=[rows, whole(gain), rows]
        + [pl.BlockSpec((3, tile, part.shape[2]), lambda i: (0, i, 0)) for part in parts]
        + [whole(weight)],
        out_specs=[rows, pl.BlockSpec((2, width), lambda i: (0, 0))],
        out_shape=[
            jax.ShapeDtypeStruct((count, width), low),
            jax.ShapeDtypeStruct((2, width), full),
        ],
        compiler_params=pltpu.CompilerParams(vmem_limit_bytes=50 * 2**20),
        cost_estimate=pl.CostEstimate(
            flops=6 * count * width * width,
            bytes_accessed=count * width * 14 + 6 * width * width,
            transcendentals=0,
        ),
        name="input_grad",
    )(tokens, gain, above, *parts, weight)


def gelu_terms(value):
    size = jnp.abs(value)
    t = 1.0 / (1.0 + 0.3275911 * 0.70710678118 * size)
    expo = jnp.exp(-0.5 * value * value)
    series = 0.254829592 + t * (
        -0.284496736 + t * (1.421413741 + t * (-1.453152027 + t * 1.061405429))
    )
    below = 0.5 * t * series * expo
    share = jnp.where(value >= 0.0, 1.0 - below, below)
    return value * share, share + value * expo * 0.3989422804


def expand_kernel(fetching, rows_ref, weight_ref, shift_ref, *refs):
    if fetching:
        own_ref, active_ref, slope_ref, all_ref, send, recv, local = refs
        arrivals = fetch_steps(((own_ref, all_ref),), send, recv, local)
        next(arrivals)
    else:
        active_ref, slope_ref = refs
    columns = weight_ref.shape[1]
    count = rows_ref.shape[0]
    tile, height = 256, min(128, count)

    def one(i, carry):
        spot = pl.ds(pl.multiple_of(i * height, height), height)
        rows = rows_ref[spot, :]
        for start in range(0, columns, tile):
            span = slice(start, start + tile)
            hidden = plain(rows, weight_ref[:, span]) + shift_ref[:, span]
            active, slope = gelu_terms(hidden)
            active_ref[spot, span] = active.astype(low)
            slope_ref[spot, span] = slope.astype(low)
        return carry

    part = 3 * count // (4 * height)
    lax.fori_loop(0, part, one, 0)
    if fetching:
        next(arrivals)
    lax.fori_loop(part, count // height, one, 0)
    if fetching:
        for _ in arrivals:
            pass


def expand(rows, weight, shift, other, identity):
    count, width = rows.shape
    columns = weight.shape[1]
    fetching = other is not None
    extra = fetch_parts((other,)) if fetching else ((), [], [])
    result = list(pl.pallas_call(
        functools.partial(expand_kernel, fetching),
        in_specs=[VMEM] * (3 + len(extra[0])),
        out_specs=[VMEM] * (2 + len(extra[1])),
        out_shape=[jax.ShapeDtypeStruct((count, columns), low)] * 2 + extra[1],
        scratch_shapes=extra[2],
        compiler_params=sender(identity if fetching else None),
        cost_estimate=pl.CostEstimate(
            flops=2 * count * width * columns,
            bytes_accessed=2 * width * columns + 4 * count * columns,
            transcendentals=2 * count * columns,
        ),
        name="expand",
    )(rows, weight, shift.reshape(1, -1), *extra[0]))
    if fetching:
        result[2] = result[2].reshape(-1, other.shape[1])
    return result


def place(axis, bit):
    return lax.rem(lax.div(lax.axis_index(axis), 1 << bit), 2)


def across(axis, bit):
    index = lax.axis_index(axis)
    return {axis: index + (1 - 2 * place(axis, bit)) * (1 << bit)}


def greet(partners):
    barrier = pltpu.get_barrier_semaphore()
    for partner in partners:
        pl.semaphore_signal(
            barrier, inc=1, device_id=partner, device_id_type=pl.DeviceIdType.MESH
        )
    pl.semaphore_wait(barrier, len(partners))


class Copies:
    def __init__(self, send_sems, recv_sems):
        self.send_sems, self.recv_sems = send_sems, recv_sems
        self.all = []

    def send(self, source, target, partner):
        index = len(self.all)
        copy = pltpu.make_async_remote_copy(
            src_ref=source,
            dst_ref=target,
            send_sem=self.send_sems.at[index],
            recv_sem=self.recv_sems.at[index],
            device_id=partner,
            device_id_type=pl.DeviceIdType.MESH,
        )
        copy.start()
        self.all.append(copy)
        return copy

    def finish(self):
        for copy in self.all:
            copy.wait_send()


def sender(identity):
    if identity is None:
        return pltpu.CompilerParams(vmem_limit_bytes=50 * 2**20)
    return pltpu.CompilerParams(
        collective_id=identity, has_side_effects=True, vmem_limit_bytes=50 * 2**20
    )


def fetch_parts(weights):
    parts = []
    for weight in weights:
        rows, columns = weight.shape
        parts.append(weight.reshape(2, 2, rows // 4, columns))
    count = 3 + 7 * len(parts)
    shapes = [jax.ShapeDtypeStruct((4,) + part.shape, part.dtype) for part in parts]
    sems = [
        pltpu.SemaphoreType.DMA((count,)),
        pltpu.SemaphoreType.DMA((count,)),
        pltpu.SemaphoreType.DMA((len(parts) + 1,)),
    ]
    return parts, shapes, sems


def fetch_steps(whole, send, recv, local, small=None):
    core, x, y = place("core", 0), place("fsdp", 0), place("fsdp", 1)
    me = lax.axis_index("fsdp")
    to_core, to_x, to_y = across("core", 0), across("fsdp", 0), across("fsdp", 1)
    to_far = {"fsdp": 3 - me}
    partners = [to_core, to_x, to_y]
    greet(partners if small is None else partners + [to_far])
    copies = Copies(send, recv)
    arrivals = []
    if small is not None:
        for partner in (to_x, to_y, to_far):
            arrivals.append(copies.send(small[0], small[1].at[me], partner))
    from_x_row, from_y_row, far_row = 2 * y + 1 - x, 2 * (1 - y) + x, 3 - me
    near = []
    for own, target in whole:
        mine = own.at[core]
        near.append(
            (
                copies.send(mine, target.at[me, core], to_x),
                copies.send(mine, target.at[me, core], to_y),
            )
        )
    own_copies = [
        pltpu.make_async_copy(own, target.at[me], local.at[i])
        for i, (own, target) in enumerate(whole + (() if small is None else (small,)))
    ]
    for copy in own_copies:
        copy.start()
    yield
    far = []
    for (own, target), (by_x, by_y) in zip(whole, near):
        by_x.wait_recv()
        quarter = target.at[from_x_row, core, 0]
        low_far = copies.send(quarter, quarter, to_y)
        half = target.at[from_x_row, core]
        arrivals.append(copies.send(half, half, to_core))
        by_y.wait_recv()
        quarter = target.at[from_y_row, core, 1]
        high_far = copies.send(quarter, quarter, to_x)
        half = target.at[from_y_row, core]
        arrivals.append(copies.send(half, half, to_core))
        far.append((low_far, high_far))
    yield
    for (own, target), (low_far, high_far) in zip(whole, far):
        low_far.wait_recv()
        high_far.wait_recv()
        half = target.at[far_row, core]
        arrivals.append(copies.send(half, half, to_core))
    for copy in arrivals:
        copy.wait_recv()
    for copy in own_copies:
        copy.wait()
    copies.finish()


def fetch_kernel(qkv_ref, out_ref, small_ref, qkv_all, out_all, small_all, send, recv, local):
    whole = ((qkv_ref, qkv_all), (out_ref, out_all))
    for _ in fetch_steps(whole, send, recv, local, (small_ref, small_all)):
        pass


def fetch(qkv_weight, out_weight, small):
    parts, shapes, sems = fetch_parts((qkv_weight, out_weight))
    qkv_w, out_w, vectors = pl.pallas_call(
        fetch_kernel,
        in_specs=[VMEM] * 3,
        out_specs=[VMEM] * 3,
        out_shape=shapes + [jax.ShapeDtypeStruct((4,) + small.shape, small.dtype)],
        scratch_shapes=sems,
        compiler_params=sender(0),
        name="fetch",
    )(*parts, small)
    return (
        qkv_w.reshape(-1, qkv_weight.shape[1]),
        out_w.reshape(-1, out_weight.shape[1]),
        vectors.reshape(4, -1),
    )


def total_kernel(chips, width, kinds, *refs):
    count = len(kinds)
    ins, small_ref = refs[:count], refs[count]
    outs, small_out = refs[count + 1 : 2 * count + 1], refs[2 * count + 1]
    first, left, right, second, third, fourth, last, small_in, send, recv = refs[2 * count + 2 :]
    core, x, y, chip = place("core", 0), place("fsdp", 0), place("fsdp", 1), place("z", 0)
    me = lax.axis_index("fsdp")
    to_core, to_x, to_y = across("core", 0), across("fsdp", 0), across("fsdp", 1)
    to_z = [across("z", bit) for bit in range(chips.bit_length() - 1)]
    partners = [to_core, to_x, to_y] + to_z
    greet(partners)
    copies = Copies(send, recv)

    chunks = []
    for index, kind in enumerate(kinds):
        stack, columns = kind
        for q in range(stack):
            for p in range(columns // width):
                span = slice(p * width, (p + 1) * width)
                chunks.append((ins[index], outs[index], q, span))

    def steps(c):
        source, target, q, span = chunks[c]
        lanes = pl.ds(span.start, width)
        copy = copies.send(source.at[:, :, q, 1 - core, :, :, lanes], first.at[c], to_core)
        yield
        copy.wait_recv()
        for row in range(2):
            first[c, row] = first[c, row] + source[row, :, q, core, :, :, lanes]
        by_x = copies.send(first.at[c, :, 1 - x, 0], left.at[c], to_x)
        by_y = copies.send(first.at[c, 1 - y, :, 1], right.at[c], to_y)
        yield
        by_x.wait_recv()
        left[c] = left[c] + first[c, :, x, 0]
        by_y.wait_recv()
        right[c] = right[c] + first[c, y, :, 1]
        by_y = copies.send(left.at[c, 1 - y], second.at[c, 0], to_y)
        by_x = copies.send(right.at[c, 1 - x], second.at[c, 1], to_x)
        yield
        by_y.wait_recv()
        second[c, 0] = second[c, 0] + left[c, y]
        by_x.wait_recv()
        second[c, 1] = second[c, 1] + right[c, x]
        copy = copies.send(second.at[c, 1 - chip], third.at[c], to_z[0])
        yield
        copy.wait_recv()
        third[c] = third[c] + second[c, chip]
        summed = third
        for bit, partner in enumerate(to_z[1:]):
            buffer = fourth.at[bit]
            copy = copies.send(summed.at[c], buffer.at[c], partner)
            yield
            copy.wait_recv()
            buffer[c] = buffer[c] + summed[c]
            summed = buffer
        last[c, core, chip] = summed[c]
        copy = copies.send(summed.at[c], last.at[c, core, chip], to_z[0])
        yield
        copy.wait_recv()
        half = last.at[c, core]
        copy = copies.send(half, half, to_core)
        yield
        copy.wait_recv()
        target[q, :, :, :, lanes] = last[c].astype(full)

    def small_steps():
        source = small_ref
        for index, partner in enumerate(partners):
            copy = copies.send(source, small_in.at[index], partner)
            yield
            copy.wait_recv()
            small_in[index] = small_in[index] + source[...]
            source = small_in.at[index]
        small_out[...] = source[me]

    waiting = [small_steps()] + [steps(c) for c in range(len(chunks))]
    active = []
    while waiting or active:
        left_over = []
        for chain in active:
            try:
                next(chain)
                left_over.append(chain)
            except StopIteration:
                pass
        active = left_over
        for chain in waiting[:1] if active else waiting[:2]:
            next(chain)
            active.append(chain)
            waiting = waiting[1:]
    copies.finish()


def total(parts, small, chips, height, width):
    kinds, views, count = [], [], 0
    for part in parts:
        rows, columns = part.shape
        stack = rows // height
        kinds.append((stack, columns))
        views.append(part.reshape(2, 2, stack, 2, 2, rows // (16 * stack), columns))
        count += stack * (columns // width)
    piece = height // 16
    stages = chips.bit_length() - 1
    copies = count * (7 + stages + 1) + 3 + stages
    outs = [
        jax.ShapeDtypeStruct(view.shape[2:], full) for view in views
    ] + [jax.ShapeDtypeStruct(small.shape[1:], full)]
    vmem = pl.BlockSpec(memory_space=pltpu.VMEM)
    sums = pl.pallas_call(
        functools.partial(total_kernel, chips, width, tuple(kinds)),
        in_specs=[vmem] * (len(parts) + 1),
        out_specs=[vmem] * (len(parts) + 1),
        out_shape=outs,
        scratch_shapes=[
            pltpu.VMEM((count, 2, 2, 2, piece, width), low),
            pltpu.VMEM((count, 2, piece, width), low),
            pltpu.VMEM((count, 2, piece, width), low),
            pltpu.VMEM((count, 2, piece, width), low),
            pltpu.VMEM((count, piece, width), low),
            pltpu.VMEM((stages - 1, count, piece, width), low),
            pltpu.VMEM((count, 2, 2, piece, width), low),
            pltpu.VMEM((3 + stages,) + small.shape, full),
            pltpu.SemaphoreType.DMA((copies,)),
            pltpu.SemaphoreType.DMA((copies,)),
        ],
        compiler_params=pltpu.CompilerParams(
            collective_id=1, has_side_effects=True, vmem_limit_bytes=60 * 2**20
        ),
        name="total",
    )(*views, small)
    return [
        result.reshape(-1, part.shape[1]) for result, part in zip(sums, parts)
    ], sums[-1].reshape(-1)


def shards(
    groups,
    copies,
    tokens,
    segments,
    cotangent,
    qkv_weight,
    qkv_bias,
    out_weight,
    out_bias,
    up_weight,
    up_bias,
    down_weight,
    down_bias,
    first_gain,
    first_shift,
    second_gain,
    second_shift,
    query_gain,
    key_gain,
):
    vectors = [
        qkv_bias,
        out_bias,
        up_bias,
        down_bias,
        first_gain,
        first_shift,
        second_gain,
        second_shift,
        query_gain,
        key_gain,
    ]
    count, width = tokens.shape
    column = segments.reshape(count, 1)
    valid = (segments >= 0)[:, None]

    small = jnp.concatenate(vectors).reshape(1, -1)
    gather = functools.partial(lax.all_gather, axis_name="fsdp", axis=0, tiled=True)
    kernels = groups == 4 and copies >= 8
    if kernels:
        qkv_w, out_w, small = fetch(qkv_weight, out_weight, small)
    else:
        qkv_w, out_w, small = gather(qkv_weight), gather(out_weight), gather(small)
    whole, start = [], 0
    for vector in vectors:
        size = vector.shape[0]
        whole.append(small[:, start : start + size].reshape(-1).astype(full))
        start += size
    (qkv_b, out_b, up_b, down_b, gain_1, shift_1, gain_2, shift_2, gain_q, gain_k) = whole
    pair_q = jnp.tile(gain_q, 2).reshape(1, 128)
    pair_k = jnp.tile(gain_k, 2).reshape(1, 128)
    normed = layer_norm(tokens.astype(full), gain_1, shift_1).astype(low)
    mixed = (plain(normed, qkv_w) + qkv_b).astype(low)
    attended, log_total, *fetched = attend(
        mixed, column, pair_q, pair_k, up_weight if kernels else None, 2
    )
    up_w = fetched[0] if kernels else gather(up_weight)
    inputs = tokens.astype(full)
    residual = inputs + plain(attended, out_w) + out_b
    second, second_back = jax.vjp(layer_norm, residual, gain_2, shift_2)
    second = second.astype(low)
    active, slope, *fetched = expand(second, up_w, up_b, down_weight if kernels else None, 3)
    down_w = fetched[0] if kernels else gather(down_weight)

    grad_low = jnp.where(valid, cotangent, jnp.zeros_like(cotangent))
    grad_output = grad_low.astype(full)
    down_b_grad = jnp.sum(grad_output, axis=0)
    down_grad = left_product(active, grad_low).astype(low)
    grad_hidden = (right_product(grad_low, down_w) * slope.astype(full)).astype(low)
    up_b_grad = jnp.sum(grad_hidden.astype(full), axis=0)
    output = jnp.where(valid, residual + plain(active, down_w) + down_b, 0.0).astype(low)
    up_grad = left_product(second, grad_hidden).astype(low)
    grad_norm_2, gain_2_grad, shift_2_grad = second_back(right_product(grad_hidden, up_w))
    grad_residual = grad_output + grad_norm_2
    branch = grad_residual.astype(low)
    out_b_grad = jnp.sum(branch.astype(full), axis=0)
    out_grad = left_product(attended, branch).astype(low)
    grad_attended = right_product(branch, out_w).astype(low)
    part, pair_gains = attend_back(
        mixed,
        column,
        pair_q,
        pair_k,
        attended,
        log_total,
        grad_attended,
        0,
        width // 128,
    )
    qkv_grad = jnp.concatenate([left_product(normed, part[i]).astype(low) for i in range(3)], 1)
    gain_sums = jnp.sum(pair_gains, axis=0).reshape(2, 2, -1).sum(axis=1)
    qkv_b_grad = jnp.sum(part.astype(full), axis=1).reshape(-1)
    grad_input, sums_1 = input_grad(tokens, gain_1.reshape(1, -1), grad_residual, [part], qkv_w)
    vectors = [
        qkv_b_grad,
        out_b_grad,
        up_b_grad,
        down_b_grad,
        sums_1[0],
        sums_1[1],
        gain_2_grad,
        shift_2_grad,
        gain_sums[0],
        gain_sums[1],
    ]
    rows = jnp.concatenate([vector.reshape(groups, -1) for vector in vectors], axis=1)
    grads = [down_grad, up_grad, out_grad, qkv_grad]
    if kernels:
        grads, sums = total(grads, rows.reshape(groups, 1, -1), copies // 2, width, width)
    else:
        scatter = functools.partial(
            lax.psum_scatter, axis_name="fsdp", scatter_dimension=0, tiled=True
        )
        grads = [lax.psum(scatter(grad), ("z", "core")).astype(full) for grad in grads]
        sums = lax.psum(scatter(rows), ("z", "core")).reshape(-1)
    final, start = [], 0
    for vector in vectors:
        size = vector.shape[0] // groups
        final.append(sums[start : start + size])
        start += size
    return (
        output,
        grad_input,
        grads[3],
        final[0],
        grads[2],
        final[1],
        grads[1],
        final[2],
        grads[0],
        final[3],
        *final[4:],
    )


def solution(mesh):
    copies, groups = mesh.shape["dp"], mesh.shape["fsdp"]
    devices = mesh.devices.reshape(copies // 2, 2, groups)
    mesh = jax.sharding.Mesh(devices, ("z", "core", "fsdp"))
    rows = P(("z", "core", "fsdp"), None)
    matrix = P("fsdp", None)
    vector = P("fsdp")
    params = (matrix, vector) * 4 + (vector,) * 6
    return jax.shard_map(
        functools.partial(shards, groups, copies),
        mesh=mesh,
        in_specs=(rows, P(("z", "core", "fsdp")), rows) + params,
        out_specs=(rows, rows) + params,
        check_vma=False,
    )
```

```python
import functools

import jax
import jax.numpy as jnp
from jax import lax
from jax.experimental import pallas as pl
from jax.experimental.pallas import tpu as pltpu
from jax.sharding import PartitionSpec as P

norm_eps = 1e-06
low = jnp.bfloat16
full = jnp.float32


def layer_norm(value, gain, shift):
    centred = value - jnp.mean(value, axis=-1, keepdims=True)
    scaled = centred * lax.rsqrt(jnp.mean(centred * centred, axis=-1, keepdims=True) + norm_eps)
    return scaled * gain + shift


def exact_gelu(value):
    return jax.nn.gelu(value, approximate=False)


def left_product(left, right):
    return lax.dot_general(
        left, right, (((0,), (0,)), ((), ())), preferred_element_type=jnp.float32
    )


def right_product(left, right):
    return lax.dot_general(
        left, right, (((1,), (1,)), ((), ())), preferred_element_type=jnp.float32
    )


def plain(left, right):
    return jnp.dot(left, right, preferred_element_type=jnp.float32)


def lane_index(shape):
    return lax.broadcasted_iota(jnp.int32, shape, len(shape) - 1)


def same_head(scale):
    row = lax.broadcasted_iota(jnp.int32, (128, 128), 0) // 64
    column = lax.broadcasted_iota(jnp.int32, (128, 128), 1) // 64
    return jnp.where(row == column, scale, 0.0).astype(low)


def head_norm(raw, mean_map):
    value = raw.astype(full)
    centred = value - plain(raw, mean_map)
    scale = lax.rsqrt(plain((centred * centred).astype(low), mean_map) + norm_eps)
    return centred * scale, scale


def half_mask(head, lanes):
    return (lanes < 64) if head == 0 else (lanes >= 64)


def query_codes(segments, lanes):
    spot = lanes % 64
    match = jnp.where(spot == segments + 1, 128.0, 0.0)
    return jnp.where(spot == 17, -128.0, match)


def key_codes(segments, lanes):
    spot = lanes % 64
    match = jnp.where(spot == segments + 1, 1.0, 0.0)
    return jnp.where((spot >= 17) & (spot < 20), 1.0, match)


def spans(count):
    cut = count * 9 // 16
    return ((0, cut), (cut, count))


def attend_pair(queries, keys, values, segments, gain_q, gain_k, store):
    count = queries.shape[0]
    lanes = lane_index((count, 128))
    mean_map = same_head(1.0 / 64)
    q_unit, _ = head_norm(queries, mean_map)
    k_unit, _ = head_norm(keys, mean_map)
    q_low = q_unit * (gain_q * 0.125)
    k_low = k_unit * gain_k
    q_code = query_codes(segments, lanes)
    k_code = key_codes(segments, lanes)
    q_heads = [jnp.where(half_mask(h, lanes), q_low, q_code).astype(low) for h in (0, 1)]
    k_heads = [jnp.where(half_mask(h, lanes), k_low, k_code).astype(low) for h in (0, 1)]
    v_heads = [
        jnp.where(half_mask(h, lanes), values.astype(full), 1.0).astype(low) for h in (0, 1)
    ]
    for first, last in spans(count):
        tile = (last - first) // 2
        for start in range(first, last, tile):
            parts = []
            for h in (0, 1):
                scores = right_product(q_heads[h][start : start + tile], k_heads[h][first:last])
                parts.append(plain(jnp.exp(scores).astype(low), v_heads[h][first:last]))
            here = lane_index((tile, 128)) < 64
            raw = jnp.where(here, parts[0], parts[1])
            sums = jnp.where(here, parts[1], parts[0])
            total = pltpu.roll(sums, 64, 1)
            store(slice(start, start + tile), raw / total, jnp.log(sums))


def attend_kernel(fetching, mixed_ref, seg_ref, gq_ref, gk_ref, *refs):
    if fetching:
        own_ref, o_ref, total_ref, all_ref, send, recv, local = refs
        arrivals = fetch_steps(((own_ref, all_ref),), send, recv, local)
        next(arrivals)
    else:
        o_ref, total_ref = refs
    width = o_ref.shape[1]
    pairs = width // 128

    def one(i, carry):
        def columns(kind):
            return pl.ds(pl.multiple_of(kind * width + i * 128, 128), 128)

        def store(rows, value, log_total):
            o_ref[rows, columns(0)] = value.astype(low)
            total_ref[rows, columns(0)] = log_total

        attend_pair(
            mixed_ref[:, columns(0)],
            mixed_ref[:, columns(1)],
            mixed_ref[:, columns(2)],
            seg_ref[...],
            gq_ref[...],
            gk_ref[...],
            store,
        )
        return carry

    early, late = pairs // 2, pairs - 1
    lax.fori_loop(0, early, one, 0)
    if fetching:
        next(arrivals)
    lax.fori_loop(early, late, one, 0)
    if fetching:
        next(arrivals)
    lax.fori_loop(late, pairs, one, 0)
    if fetching:
        for _ in arrivals:
            pass


def attend_back_kernel(
    q_ref,
    k_ref,
    v_ref,
    seg_ref,
    gq_ref,
    gk_ref,
    o_ref,
    total_ref,
    do_ref,
    grad_ref,
    gain_ref,
    dq_scr,
):
    count = q_ref.shape[0]
    lanes = lane_index((count, 128))
    spot = lanes % 64
    mean_map = same_head(1.0 / 64)
    q_unit, q_scale = head_norm(q_ref[...], mean_map)
    k_unit, k_scale = head_norm(k_ref[...], mean_map)
    q_low = (q_unit * (gq_ref[...] * 0.125)).astype(low)
    k_low = (k_unit * gk_ref[...]).astype(low)
    segments = seg_ref[...]
    log_total = total_ref[...]
    log_high = log_total.astype(low).astype(full)
    q_code = jnp.where(
        spot == 18,
        -log_high,
        jnp.where(spot == 19, log_high - log_total, query_codes(segments, lanes)),
    ).astype(low)
    k_code = key_codes(segments, lanes).astype(low)
    grads = do_ref[...]
    product = (grads.astype(full) * o_ref[...].astype(full)).astype(low)
    row = lax.broadcasted_iota(jnp.int32, (128, 128), 0) // 64
    column = lax.broadcasted_iota(jnp.int32, (128, 128), 1) // 64
    delta = plain(product, jnp.where(row != column, 1.0, 0.0).astype(low))
    delta_high = delta.astype(low).astype(full)
    g_code = jnp.where(
        spot == 0, -delta_high, jnp.where(spot == 1, delta_high - delta, 0.0)
    ).astype(low)
    v_code = jnp.where(spot < 2, 1.0, 0.0).astype(low)
    values = v_ref[...]
    masks = [half_mask(h, lanes) for h in (0, 1)]
    q_heads = [jnp.where(masks[h], q_low, q_code) for h in (0, 1)]
    k_heads = [jnp.where(masks[h], k_low, k_code) for h in (0, 1)]
    v_heads = [jnp.where(masks[h], values, v_code) for h in (0, 1)]
    g_heads = [jnp.where(masks[h], grads, g_code) for h in (0, 1)]
    dk_parts = []

    def run(first, last, other_first, other_last, tile):
        for start in range(first, last, tile):
            rows = slice(start, start + tile)
            others = slice(other_first, other_last)
            dv_parts, dk_parts, dq_parts = [], [], []
            for h in (0, 1):
                scores = right_product(k_heads[h][rows], q_heads[h][others])
                weights = jnp.exp(scores)
                change = right_product(v_heads[h][rows], g_heads[h][others])
                sloped = (weights * change).astype(low)
                dv_parts.append(plain(weights.astype(low), grads[others]))
                dk_parts.append(plain(sloped, q_low[others]))
                dq_parts.append(left_product(sloped, k_low[rows]))
            here = lane_index((tile, 128)) < 64
            there = lane_index((other_last - other_first, 128)) < 64
            grad_ref[2, rows] = jnp.where(here, dv_parts[0], dv_parts[1]).astype(low)
            dk = jnp.where(here, dk_parts[0], dk_parts[1])
            dk_scr_store(rows, dk)
            dq = jnp.where(there, dq_parts[0], dq_parts[1])
            if start == first:
                dq_scr[0, others] = dq
            else:
                dq_scr[0, others] += dq

    def dk_scr_store(rows, value):
        dq_scr[1, rows] = value

    for first, last in spans(count):
        run(first, last, first, last, (last - first) // 2)

    def norm_back(slot, factor, unit, scale, gain):
        slope = dq_scr[slot] * factor
        inner = slope * gain
        shared = inner * unit
        result = scale * (
            inner
            - plain(inner.astype(low), mean_map)
            - unit * plain(shared.astype(low), mean_map)
        )
        grad_ref[slot] = result.astype(low)
        gain_ref[0, slot : slot + 1] = jnp.sum(slope * unit, axis=0, keepdims=True)

    norm_back(0, 0.125, q_unit, q_scale, gq_ref[...])
    norm_back(1, 1.0, k_unit, k_scale, gk_ref[...])


def attend_specs(count, width, first=0):
    pairs = width // 128
    column = lambda offset: pl.BlockSpec((count, 128), lambda i: (0, i + first + offset))
    fixed = lambda shape: pl.BlockSpec(shape, lambda i: (0, 0))
    shared = [
        column(0),
        column(pairs),
        column(2 * pairs),
        fixed((count, 1)),
        fixed((1, 128)),
        fixed((1, 128)),
    ]
    return pairs, column, shared


VMEM = pl.BlockSpec(memory_space=pltpu.VMEM)


def attend(mixed, segments, gain_q, gain_k, weight, identity):
    count = mixed.shape[0]
    width = mixed.shape[1] // 3
    fetching = weight is not None
    extra = fetch_parts((weight,)) if fetching else ((), [], [])
    result = list(pl.pallas_call(
        functools.partial(attend_kernel, fetching),
        in_specs=[VMEM] * (4 + len(extra[0])),
        out_specs=[VMEM] * (2 + len(extra[1])),
        out_shape=[
            jax.ShapeDtypeStruct((count, width), low),
            jax.ShapeDtypeStruct((count, width), full),
        ]
        + extra[1],
        scratch_shapes=extra[2],
        compiler_params=sender(identity if fetching else None),
        cost_estimate=pl.CostEstimate(
            flops=16 * count * count * width,
            bytes_accessed=count * width * 12,
            transcendentals=count * count * width // 64,
        ),
        name="attend",
    )(mixed, segments, gain_q, gain_k, *extra[0]))
    if fetching:
        result[2] = result[2].reshape(-1, weight.shape[1])
    return result


def attend_back(mixed, segments, gain_q, gain_k, attended, log_total, grad, first, pairs):
    count = mixed.shape[0]
    width = mixed.shape[1] // 3
    _, column, shared = attend_specs(count, width, first)
    return pl.pallas_call(
        attend_back_kernel,
        grid=(pairs,),
        in_specs=shared + [column(0), column(0), column(0)],
        out_specs=[
            pl.BlockSpec((3, count, 128), lambda i: (0, 0, i)),
            pl.BlockSpec((1, 2, 128), lambda i: (i, 0, 0)),
        ],
        scratch_shapes=[pltpu.VMEM((2, count, 128), full)],
        out_shape=[
            jax.ShapeDtypeStruct((3, count, pairs * 128), low),
            jax.ShapeDtypeStruct((pairs, 2, 128), full),
        ],
        compiler_params=pltpu.CompilerParams(vmem_limit_bytes=50 * 2**20),
        cost_estimate=pl.CostEstimate(
            flops=40 * count * count * pairs * 128,
            bytes_accessed=count * pairs * 128 * 18,
            transcendentals=count * count * pairs * 2,
        ),
        name="attend_back",
    )(mixed, mixed, mixed, segments, gain_q, gain_k, attended, log_total, grad)


def input_grad_kernel(tokens_ref, gain_ref, above_ref, *refs):
    parts, (weight_ref, out_ref, sums_ref) = refs[:-3], refs[-3:]
    width = tokens_ref.shape[1]
    size = width // len(parts)
    slope = 0.0
    for p, part_ref in enumerate(parts):
        for kind in range(3):
            start = kind * width + p * size
            slope += right_product(part_ref[kind], weight_ref[:, start : start + size])
    value = tokens_ref[...].astype(full)
    centred = value - jnp.mean(value, axis=-1, keepdims=True)
    scale = lax.rsqrt(jnp.mean(centred * centred, axis=-1, keepdims=True) + norm_eps)
    unit = centred * scale
    inner = slope * gain_ref[...]
    shared = slope * unit
    back = scale * (
        inner
        - jnp.mean(inner, axis=-1, keepdims=True)
        - unit * jnp.mean(inner * unit, axis=-1, keepdims=True)
    )
    out_ref[...] = (above_ref[...] + back).astype(out_ref.dtype)
    sums = jnp.concatenate(
        [jnp.sum(shared, axis=0, keepdims=True), jnp.sum(slope, axis=0, keepdims=True)]
    )
    first = pl.program_id(0) == 0

    @pl.when(first)
    def _():
        sums_ref[...] = sums

    @pl.when(jnp.logical_not(first))
    def _():
        sums_ref[...] += sums


def input_grad(tokens, gain, above, parts, weight):
    count, width = tokens.shape
    tile = min(256, count)
    rows = pl.BlockSpec((tile, width), lambda i: (i, 0))
    whole = lambda array: pl.BlockSpec(array.shape, lambda i: (0, 0))
    return pl.pallas_call(
        input_grad_kernel,
        grid=(count // tile,),
        in_specs=[rows, whole(gain), rows]
        + [pl.BlockSpec((3, tile, part.shape[2]), lambda i: (0, i, 0)) for part in parts]
        + [whole(weight)],
        out_specs=[rows, pl.BlockSpec((2, width), lambda i: (0, 0))],
        out_shape=[
            jax.ShapeDtypeStruct((count, width), low),
            jax.ShapeDtypeStruct((2, width), full),
        ],
        compiler_params=pltpu.CompilerParams(vmem_limit_bytes=50 * 2**20),
        cost_estimate=pl.CostEstimate(
            flops=6 * count * width * width,
            bytes_accessed=count * width * 14 + 6 * width * width,
            transcendentals=0,
        ),
        name="input_grad",
    )(tokens, gain, above, *parts, weight)


def gelu_terms(value):
    size = jnp.abs(value)
    t = 1.0 / (1.0 + 0.3275911 * 0.70710678118 * size)
    expo = jnp.exp(-0.5 * value * value)
    series = 0.254829592 + t * (
        -0.284496736 + t * (1.421413741 + t * (-1.453152027 + t * 1.061405429))
    )
    below = 0.5 * t * series * expo
    share = jnp.where(value >= 0.0, 1.0 - below, below)
    return value * share, share + value * expo * 0.3989422804


def expand_kernel(fetching, rows_ref, weight_ref, shift_ref, *refs):
    if fetching:
        own_ref, active_ref, slope_ref, all_ref, send, recv, local = refs
        arrivals = fetch_steps(((own_ref, all_ref),), send, recv, local)
        next(arrivals)
    else:
        active_ref, slope_ref = refs
    columns = weight_ref.shape[1]
    count = rows_ref.shape[0]
    tile, height = 256, min(128, count)

    def one(i, carry):
        spot = pl.ds(pl.multiple_of(i * height, height), height)
        rows = rows_ref[spot, :]
        for start in range(0, columns, tile):
            span = slice(start, start + tile)
            hidden = plain(rows, weight_ref[:, span]) + shift_ref[:, span]
            active, slope = gelu_terms(hidden)
            active_ref[spot, span] = active.astype(low)
            slope_ref[spot, span] = slope.astype(low)
        return carry

    tiles = count // height
    early, late = tiles // 2, tiles - 1
    lax.fori_loop(0, early, one, 0)
    if fetching:
        next(arrivals)
    lax.fori_loop(early, late, one, 0)
    if fetching:
        next(arrivals)
    lax.fori_loop(late, tiles, one, 0)
    if fetching:
        for _ in arrivals:
            pass


def expand(rows, weight, shift, other, identity):
    count, width = rows.shape
    columns = weight.shape[1]
    fetching = other is not None
    extra = fetch_parts((other,)) if fetching else ((), [], [])
    result = list(pl.pallas_call(
        functools.partial(expand_kernel, fetching),
        in_specs=[VMEM] * (3 + len(extra[0])),
        out_specs=[VMEM] * (2 + len(extra[1])),
        out_shape=[jax.ShapeDtypeStruct((count, columns), low)] * 2 + extra[1],
        scratch_shapes=extra[2],
        compiler_params=sender(identity if fetching else None),
        cost_estimate=pl.CostEstimate(
            flops=2 * count * width * columns,
            bytes_accessed=2 * width * columns + 4 * count * columns,
            transcendentals=2 * count * columns,
        ),
        name="expand",
    )(rows, weight, shift.reshape(1, -1), *extra[0]))
    if fetching:
        result[2] = result[2].reshape(-1, other.shape[1])
    return result


def place(axis, bit):
    return lax.rem(lax.div(lax.axis_index(axis), 1 << bit), 2)


def across(axis, bit):
    index = lax.axis_index(axis)
    return {axis: index + (1 - 2 * place(axis, bit)) * (1 << bit)}


def greet(partners):
    barrier = pltpu.get_barrier_semaphore()
    for partner in partners:
        pl.semaphore_signal(
            barrier, inc=1, device_id=partner, device_id_type=pl.DeviceIdType.MESH
        )
    pl.semaphore_wait(barrier, len(partners))


class Copies:
    def __init__(self, send_sems, recv_sems):
        self.send_sems, self.recv_sems = send_sems, recv_sems
        self.all = []

    def send(self, source, target, partner):
        index = len(self.all)
        copy = pltpu.make_async_remote_copy(
            src_ref=source,
            dst_ref=target,
            send_sem=self.send_sems.at[index],
            recv_sem=self.recv_sems.at[index],
            device_id=partner,
            device_id_type=pl.DeviceIdType.MESH,
        )
        copy.start()
        self.all.append(copy)
        return copy

    def finish(self):
        for copy in self.all:
            copy.wait_send()


def sender(identity):
    if identity is None:
        return pltpu.CompilerParams(vmem_limit_bytes=50 * 2**20)
    return pltpu.CompilerParams(
        collective_id=identity, has_side_effects=True, vmem_limit_bytes=50 * 2**20
    )


def fetch_parts(weights):
    parts = []
    for weight in weights:
        rows, columns = weight.shape
        parts.append(weight.reshape(2, 2, rows // 4, columns))
    count = 3 + 9 * len(parts)
    shapes = [jax.ShapeDtypeStruct((4,) + part.shape, part.dtype) for part in parts]
    sems = [
        pltpu.SemaphoreType.DMA((count,)),
        pltpu.SemaphoreType.DMA((count,)),
        pltpu.SemaphoreType.DMA((len(parts) + 1,)),
    ]
    return parts, shapes, sems


def fetch_steps(whole, send, recv, local, small=None):
    core, x, y = place("core", 0), place("fsdp", 0), place("fsdp", 1)
    me = lax.axis_index("fsdp")
    to_core, to_x, to_y = across("core", 0), across("fsdp", 0), across("fsdp", 1)
    to_far = {"fsdp": 3 - me}
    partners = [to_core, to_x, to_y]
    greet(partners if small is None else partners + [to_far])
    copies = Copies(send, recv)
    arrivals = []
    if small is not None:
        for partner in (to_x, to_y, to_far):
            arrivals.append(copies.send(small[0], small[1].at[me], partner))
    from_x_row, from_y_row, far_row = 2 * y + 1 - x, 2 * (1 - y) + x, 3 - me
    ahead, behind = [], []
    for own, target in whole:
        ahead.append(
            (
                copies.send(own.at[core, 0], target.at[me, core, 0], to_x),
                copies.send(own.at[core, 1], target.at[me, core, 1], to_y),
            )
        )
    for own, target in whole:
        behind.append(
            (
                copies.send(own.at[core, 1], target.at[me, core, 1], to_x),
                copies.send(own.at[core, 0], target.at[me, core, 0], to_y),
            )
        )
    own_copies = [
        pltpu.make_async_copy(own, target.at[me], local.at[i])
        for i, (own, target) in enumerate(whole + (() if small is None else (small,)))
    ]
    for copy in own_copies:
        copy.start()
    yield
    far = []
    for (own, target), (by_x, by_y) in zip(whole, ahead):
        by_x.wait_recv()
        quarter = target.at[from_x_row, core, 0]
        low_far = copies.send(quarter, quarter, to_y)
        by_y.wait_recv()
        quarter = target.at[from_y_row, core, 1]
        far.append((low_far, copies.send(quarter, quarter, to_x)))
    yield
    for (own, target), (by_x, by_y) in zip(whole, behind):
        by_x.wait_recv()
        half = target.at[from_x_row, core]
        arrivals.append(copies.send(half, half, to_core))
        by_y.wait_recv()
        half = target.at[from_y_row, core]
        arrivals.append(copies.send(half, half, to_core))
    yield
    for (own, target), (low_far, high_far) in zip(whole, far):
        low_far.wait_recv()
        high_far.wait_recv()
        half = target.at[far_row, core]
        arrivals.append(copies.send(half, half, to_core))
    for copy in arrivals:
        copy.wait_recv()
    for copy in own_copies:
        copy.wait()
    copies.finish()


def fetch_kernel(qkv_ref, out_ref, small_ref, qkv_all, out_all, small_all, send, recv, local):
    whole = ((qkv_ref, qkv_all), (out_ref, out_all))
    for _ in fetch_steps(whole, send, recv, local, (small_ref, small_all)):
        pass


def fetch(qkv_weight, out_weight, small):
    parts, shapes, sems = fetch_parts((qkv_weight, out_weight))
    qkv_w, out_w, vectors = pl.pallas_call(
        fetch_kernel,
        in_specs=[VMEM] * 3,
        out_specs=[VMEM] * 3,
        out_shape=shapes + [jax.ShapeDtypeStruct((4,) + small.shape, small.dtype)],
        scratch_shapes=sems,
        compiler_params=sender(0),
        name="fetch",
    )(*parts, small)
    return (
        qkv_w.reshape(-1, qkv_weight.shape[1]),
        out_w.reshape(-1, out_weight.shape[1]),
        vectors.reshape(4, -1),
    )


def total_kernel(chips, width, kinds, *refs):
    count = len(kinds)
    ins, small_ref = refs[:count], refs[count]
    outs, small_out = refs[count + 1 : 2 * count + 1], refs[2 * count + 1]
    first, left, right, second, third, fourth, last, small_in, send, recv = refs[2 * count + 2 :]
    core, x, y, chip = place("core", 0), place("fsdp", 0), place("fsdp", 1), place("z", 0)
    me = lax.axis_index("fsdp")
    to_core, to_x, to_y = across("core", 0), across("fsdp", 0), across("fsdp", 1)
    to_z = [across("z", bit) for bit in range(chips.bit_length() - 1)]
    partners = [to_core, to_x, to_y] + to_z
    greet(partners)
    copies = Copies(send, recv)

    chunks = []
    for index, kind in enumerate(kinds):
        stack, columns = kind
        for q in range(stack):
            for p in range(columns // width):
                span = slice(p * width, (p + 1) * width)
                chunks.append((ins[index], outs[index], q, span))

    shared = []
    for c, (source, _, q, span) in enumerate(chunks):
        lanes = pl.ds(span.start, width)
        mine = source.at[:, :, q, 1 - core, :, :, lanes]
        shared.append(copies.send(mine, first.at[c], to_core))

    def steps(c):
        source, target, q, span = chunks[c]
        lanes = pl.ds(span.start, width)
        shared[c].wait_recv()
        for row in range(2):
            first[c, row] = first[c, row] + source[row, :, q, core, :, :, lanes]
        by_x = copies.send(first.at[c, :, 1 - x, 0], left.at[c], to_x)
        by_y = copies.send(first.at[c, 1 - y, :, 1], right.at[c], to_y)
        yield
        yield
        by_x.wait_recv()
        left[c] = left[c] + first[c, :, x, 0]
        by_y.wait_recv()
        right[c] = right[c] + first[c, y, :, 1]
        by_y = copies.send(left.at[c, 1 - y], second.at[c, 0], to_y)
        by_x = copies.send(right.at[c, 1 - x], second.at[c, 1], to_x)
        yield
        by_y.wait_recv()
        second[c, 0] = second[c, 0] + left[c, y]
        by_x.wait_recv()
        second[c, 1] = second[c, 1] + right[c, x]
        copy = copies.send(second.at[c, 1 - chip], third.at[c], to_z[0])
        yield
        copy.wait_recv()
        third[c] = third[c] + second[c, chip]
        summed = third
        for bit, partner in enumerate(to_z[1:]):
            buffer = fourth.at[bit]
            copy = copies.send(summed.at[c], buffer.at[c], partner)
            yield
            copy.wait_recv()
            buffer[c] = buffer[c] + summed[c]
            summed = buffer
        last[c, core, chip] = summed[c]
        copy = copies.send(summed.at[c], last.at[c, core, chip], to_z[0])
        yield
        copy.wait_recv()
        half = last.at[c, core]
        copy = copies.send(half, half, to_core)
        yield
        copy.wait_recv()
        target[q, :, :, :, lanes] = last[c].astype(full)

    def small_steps():
        source = small_ref
        for index, partner in enumerate(partners):
            copy = copies.send(source, small_in.at[index], partner)
            yield
            copy.wait_recv()
            small_in[index] = small_in[index] + source[...]
            source = small_in.at[index]
        small_out[...] = source[me]

    waiting = [small_steps()] + [steps(c) for c in range(len(chunks))]
    active = []
    while waiting or active:
        left_over = []
        for chain in active:
            try:
                next(chain)
                left_over.append(chain)
            except StopIteration:
                pass
        active = left_over
        for chain in waiting[:1] if active else waiting[:2]:
            next(chain)
            active.append(chain)
            waiting = waiting[1:]
    copies.finish()


def total(parts, small, chips, height, width):
    kinds, views, count = [], [], 0
    for part in parts:
        rows, columns = part.shape
        stack = rows // height
        kinds.append((stack, columns))
        views.append(part.reshape(2, 2, stack, 2, 2, rows // (16 * stack), columns))
        count += stack * (columns // width)
    piece = height // 16
    stages = chips.bit_length() - 1
    copies = count * (7 + stages + 1) + 3 + stages
    outs = [
        jax.ShapeDtypeStruct(view.shape[2:], full) for view in views
    ] + [jax.ShapeDtypeStruct(small.shape[1:], full)]
    vmem = pl.BlockSpec(memory_space=pltpu.VMEM)
    sums = pl.pallas_call(
        functools.partial(total_kernel, chips, width, tuple(kinds)),
        in_specs=[vmem] * (len(parts) + 1),
        out_specs=[vmem] * (len(parts) + 1),
        out_shape=outs,
        scratch_shapes=[
            pltpu.VMEM((count, 2, 2, 2, piece, width), low),
            pltpu.VMEM((count, 2, piece, width), low),
            pltpu.VMEM((count, 2, piece, width), low),
            pltpu.VMEM((count, 2, piece, width), low),
            pltpu.VMEM((count, piece, width), low),
            pltpu.VMEM((stages - 1, count, piece, width), low),
            pltpu.VMEM((count, 2, 2, piece, width), low),
            pltpu.VMEM((3 + stages,) + small.shape, full),
            pltpu.SemaphoreType.DMA((copies,)),
            pltpu.SemaphoreType.DMA((copies,)),
        ],
        compiler_params=pltpu.CompilerParams(
            collective_id=1, has_side_effects=True, vmem_limit_bytes=60 * 2**20
        ),
        name="total",
    )(*views, small)
    return [
        result.reshape(-1, part.shape[1]) for result, part in zip(sums, parts)
    ], sums[-1].reshape(-1)


def shards(
    groups,
    copies,
    tokens,
    segments,
    cotangent,
    qkv_weight,
    qkv_bias,
    out_weight,
    out_bias,
    up_weight,
    up_bias,
    down_weight,
    down_bias,
    first_gain,
    first_shift,
    second_gain,
    second_shift,
    query_gain,
    key_gain,
):
    vectors = [
        qkv_bias,
        out_bias,
        up_bias,
        down_bias,
        first_gain,
        first_shift,
        second_gain,
        second_shift,
        query_gain,
        key_gain,
    ]
    count, width = tokens.shape
    column = segments.reshape(count, 1)
    valid = (segments >= 0)[:, None]

    small = jnp.concatenate(vectors).reshape(1, -1)
    gather = functools.partial(lax.all_gather, axis_name="fsdp", axis=0, tiled=True)
    kernels = groups == 4 and copies >= 8
    if kernels:
        qkv_w, out_w, small = fetch(qkv_weight, out_weight, small)
    else:
        qkv_w, out_w, small = gather(qkv_weight), gather(out_weight), gather(small)
    whole, start = [], 0
    for vector in vectors:
        size = vector.shape[0]
        whole.append(small[:, start : start + size].reshape(-1).astype(full))
        start += size
    (qkv_b, out_b, up_b, down_b, gain_1, shift_1, gain_2, shift_2, gain_q, gain_k) = whole
    pair_q = jnp.tile(gain_q, 2).reshape(1, 128)
    pair_k = jnp.tile(gain_k, 2).reshape(1, 128)
    normed = layer_norm(tokens.astype(full), gain_1, shift_1).astype(low)
    mixed = (plain(normed, qkv_w) + qkv_b).astype(low)
    attended, log_total, *fetched = attend(
        mixed, column, pair_q, pair_k, up_weight if kernels else None, 2
    )
    up_w = fetched[0] if kernels else gather(up_weight)
    inputs = tokens.astype(full)
    residual = inputs + plain(attended, out_w) + out_b
    second, second_back = jax.vjp(layer_norm, residual, gain_2, shift_2)
    second = second.astype(low)
    active, slope, *fetched = expand(second, up_w, up_b, down_weight if kernels else None, 3)
    down_w = fetched[0] if kernels else gather(down_weight)

    grad_low = jnp.where(valid, cotangent, jnp.zeros_like(cotangent))
    grad_output = grad_low.astype(full)
    down_b_grad = jnp.sum(grad_output, axis=0)
    down_grad = left_product(active, grad_low).astype(low)
    grad_hidden = (right_product(grad_low, down_w) * slope.astype(full)).astype(low)
    up_b_grad = jnp.sum(grad_hidden.astype(full), axis=0)
    output = jnp.where(valid, residual + plain(active, down_w) + down_b, 0.0).astype(low)
    up_grad = left_product(second, grad_hidden).astype(low)
    grad_norm_2, gain_2_grad, shift_2_grad = second_back(right_product(grad_hidden, up_w))
    grad_residual = grad_output + grad_norm_2
    branch = grad_residual.astype(low)
    out_b_grad = jnp.sum(branch.astype(full), axis=0)
    out_grad = left_product(attended, branch).astype(low)
    grad_attended = right_product(branch, out_w).astype(low)
    part, pair_gains = attend_back(
        mixed,
        column,
        pair_q,
        pair_k,
        attended,
        log_total,
        grad_attended,
        0,
        width // 128,
    )
    qkv_grad = jnp.concatenate([left_product(normed, part[i]).astype(low) for i in range(3)], 1)
    gain_sums = jnp.sum(pair_gains, axis=0).reshape(2, 2, -1).sum(axis=1)
    qkv_b_grad = jnp.sum(part.astype(full), axis=1).reshape(-1)
    grad_input, sums_1 = input_grad(tokens, gain_1.reshape(1, -1), grad_residual, [part], qkv_w)
    vectors = [
        qkv_b_grad,
        out_b_grad,
        up_b_grad,
        down_b_grad,
        sums_1[0],
        sums_1[1],
        gain_2_grad,
        shift_2_grad,
        gain_sums[0],
        gain_sums[1],
    ]
    rows = jnp.concatenate([vector.reshape(groups, -1) for vector in vectors], axis=1)
    grads = [down_grad, up_grad, out_grad, qkv_grad]
    if kernels:
        grads, sums = total(grads, rows.reshape(groups, 1, -1), copies // 2, width, width)
    else:
        scatter = functools.partial(
            lax.psum_scatter, axis_name="fsdp", scatter_dimension=0, tiled=True
        )
        grads = [lax.psum(scatter(grad), ("z", "core")).astype(full) for grad in grads]
        sums = lax.psum(scatter(rows), ("z", "core")).reshape(-1)
    final, start = [], 0
    for vector in vectors:
        size = vector.shape[0] // groups
        final.append(sums[start : start + size])
        start += size
    return (
        output,
        grad_input,
        grads[3],
        final[0],
        grads[2],
        final[1],
        grads[1],
        final[2],
        grads[0],
        final[3],
        *final[4:],
    )


def solution(mesh):
    copies, groups = mesh.shape["dp"], mesh.shape["fsdp"]
    devices = mesh.devices.reshape(copies // 2, 2, groups)
    mesh = jax.sharding.Mesh(devices, ("z", "core", "fsdp"))
    rows = P(("z", "core", "fsdp"), None)
    matrix = P("fsdp", None)
    vector = P("fsdp")
    params = (matrix, vector) * 4 + (vector,) * 6
    return jax.shard_map(
        functools.partial(shards, groups, copies),
        mesh=mesh,
        in_specs=(rows, P(("z", "core", "fsdp")), rows) + params,
        out_specs=(rows, rows) + params,
        check_vma=False,
    )
```

```python
import functools

import jax
import jax.numpy as jnp
from jax import lax
from jax.experimental import pallas as pl
from jax.experimental.pallas import tpu as pltpu
from jax.sharding import PartitionSpec as P

norm_eps = 1e-06
low = jnp.bfloat16
full = jnp.float32


def layer_norm(value, gain, shift):
    centred = value - jnp.mean(value, axis=-1, keepdims=True)
    scaled = centred * lax.rsqrt(jnp.mean(centred * centred, axis=-1, keepdims=True) + norm_eps)
    return scaled * gain + shift


def exact_gelu(value):
    return jax.nn.gelu(value, approximate=False)


def left_product(left, right):
    return lax.dot_general(
        left, right, (((0,), (0,)), ((), ())), preferred_element_type=jnp.float32
    )


def right_product(left, right):
    return lax.dot_general(
        left, right, (((1,), (1,)), ((), ())), preferred_element_type=jnp.float32
    )


def plain(left, right):
    return jnp.dot(left, right, preferred_element_type=jnp.float32)


def lane_index(shape):
    return lax.broadcasted_iota(jnp.int32, shape, len(shape) - 1)


def same_head(scale):
    row = lax.broadcasted_iota(jnp.int32, (128, 128), 0) // 64
    column = lax.broadcasted_iota(jnp.int32, (128, 128), 1) // 64
    return jnp.where(row == column, scale, 0.0).astype(low)


def head_norm(raw, mean_map):
    value = raw.astype(full)
    centred = value - plain(raw, mean_map)
    scale = lax.rsqrt(plain((centred * centred).astype(low), mean_map) + norm_eps)
    return centred * scale, scale


def half_mask(head, lanes):
    return (lanes < 64) if head == 0 else (lanes >= 64)


def query_codes(segments, lanes):
    spot = lanes % 64
    match = jnp.where(spot == segments + 1, 128.0, 0.0)
    return jnp.where(spot == 17, -128.0, match)


def key_codes(segments, lanes):
    spot = lanes % 64
    match = jnp.where(spot == segments + 1, 1.0, 0.0)
    return jnp.where((spot >= 17) & (spot < 20), 1.0, match)


def spans(count):
    cut = count * 9 // 16
    return ((0, cut), (cut, count))


def attend_pair(queries, keys, values, segments, gain_q, gain_k, store):
    count = queries.shape[0]
    lanes = lane_index((count, 128))
    mean_map = same_head(1.0 / 64)
    q_unit, _ = head_norm(queries, mean_map)
    k_unit, _ = head_norm(keys, mean_map)
    q_low = q_unit * (gain_q * 0.125)
    k_low = k_unit * gain_k
    q_code = query_codes(segments, lanes)
    k_code = key_codes(segments, lanes)
    q_heads = [jnp.where(half_mask(h, lanes), q_low, q_code).astype(low) for h in (0, 1)]
    k_heads = [jnp.where(half_mask(h, lanes), k_low, k_code).astype(low) for h in (0, 1)]
    v_heads = [
        jnp.where(half_mask(h, lanes), values.astype(full), 1.0).astype(low) for h in (0, 1)
    ]
    for first, last in spans(count):
        tile = (last - first) // 2
        for start in range(first, last, tile):
            parts = []
            for h in (0, 1):
                scores = right_product(q_heads[h][start : start + tile], k_heads[h][first:last])
                parts.append(plain(jnp.exp(scores).astype(low), v_heads[h][first:last]))
            here = lane_index((tile, 128)) < 64
            raw = jnp.where(here, parts[0], parts[1])
            sums = jnp.where(here, parts[1], parts[0])
            total = pltpu.roll(sums, 64, 1)
            store(slice(start, start + tile), raw / total, jnp.log(sums))


def attend_kernel(fetching, mixed_ref, seg_ref, gq_ref, gk_ref, *refs):
    if fetching:
        own_ref, o_ref, total_ref, all_ref, send, recv, local = refs
        arrivals = fetch_steps(((own_ref, all_ref),), send, recv, local)
        next(arrivals)
    else:
        o_ref, total_ref = refs
    width = o_ref.shape[1]
    pairs = width // 128

    def one(i, carry):
        def columns(kind):
            return pl.ds(pl.multiple_of(kind * width + i * 128, 128), 128)

        def store(rows, value, log_total):
            o_ref[rows, columns(0)] = value.astype(low)
            total_ref[rows, columns(0)] = log_total

        attend_pair(
            mixed_ref[:, columns(0)],
            mixed_ref[:, columns(1)],
            mixed_ref[:, columns(2)],
            seg_ref[...],
            gq_ref[...],
            gk_ref[...],
            store,
        )
        return carry

    early, late = pairs // 2, pairs - 1
    lax.fori_loop(0, early, one, 0)
    if fetching:
        next(arrivals)
    lax.fori_loop(early, late, one, 0)
    if fetching:
        next(arrivals)
    lax.fori_loop(late, pairs, one, 0)
    if fetching:
        for _ in arrivals:
            pass


def attend_back_kernel(
    q_ref,
    k_ref,
    v_ref,
    seg_ref,
    gq_ref,
    gk_ref,
    o_ref,
    total_ref,
    do_ref,
    grad_ref,
    gain_ref,
    dq_scr,
):
    count = q_ref.shape[0]
    lanes = lane_index((count, 128))
    spot = lanes % 64
    mean_map = same_head(1.0 / 64)
    q_unit, q_scale = head_norm(q_ref[...], mean_map)
    k_unit, k_scale = head_norm(k_ref[...], mean_map)
    q_low = (q_unit * (gq_ref[...] * 0.125)).astype(low)
    k_low = (k_unit * gk_ref[...]).astype(low)
    segments = seg_ref[...]
    log_total = total_ref[...]
    log_high = log_total.astype(low).astype(full)
    q_code = jnp.where(
        spot == 18,
        -log_high,
        jnp.where(spot == 19, log_high - log_total, query_codes(segments, lanes)),
    ).astype(low)
    k_code = key_codes(segments, lanes).astype(low)
    grads = do_ref[...]
    product = (grads.astype(full) * o_ref[...].astype(full)).astype(low)
    row = lax.broadcasted_iota(jnp.int32, (128, 128), 0) // 64
    column = lax.broadcasted_iota(jnp.int32, (128, 128), 1) // 64
    delta = plain(product, jnp.where(row != column, 1.0, 0.0).astype(low))
    delta_high = delta.astype(low).astype(full)
    g_code = jnp.where(
        spot == 0, -delta_high, jnp.where(spot == 1, delta_high - delta, 0.0)
    ).astype(low)
    v_code = jnp.where(spot < 2, 1.0, 0.0).astype(low)
    values = v_ref[...]
    masks = [half_mask(h, lanes) for h in (0, 1)]
    q_heads = [jnp.where(masks[h], q_low, q_code) for h in (0, 1)]
    k_heads = [jnp.where(masks[h], k_low, k_code) for h in (0, 1)]
    v_heads = [jnp.where(masks[h], values, v_code) for h in (0, 1)]
    g_heads = [jnp.where(masks[h], grads, g_code) for h in (0, 1)]
    dk_parts = []

    def run(first, last, other_first, other_last, tile):
        for start in range(first, last, tile):
            rows = slice(start, start + tile)
            others = slice(other_first, other_last)
            dv_parts, dk_parts, dq_parts = [], [], []
            for h in (0, 1):
                scores = right_product(k_heads[h][rows], q_heads[h][others])
                weights = jnp.exp(scores)
                change = right_product(v_heads[h][rows], g_heads[h][others])
                sloped = (weights * change).astype(low)
                dv_parts.append(plain(weights.astype(low), grads[others]))
                dk_parts.append(plain(sloped, q_low[others]))
                dq_parts.append(left_product(sloped, k_low[rows]))
            here = lane_index((tile, 128)) < 64
            there = lane_index((other_last - other_first, 128)) < 64
            grad_ref[2, rows] = jnp.where(here, dv_parts[0], dv_parts[1]).astype(low)
            dk = jnp.where(here, dk_parts[0], dk_parts[1])
            dk_scr_store(rows, dk)
            dq = jnp.where(there, dq_parts[0], dq_parts[1])
            if start == first:
                dq_scr[0, others] = dq
            else:
                dq_scr[0, others] += dq

    def dk_scr_store(rows, value):
        dq_scr[1, rows] = value

    for first, last in spans(count):
        run(first, last, first, last, (last - first) // 2)

    def norm_back(slot, factor, unit, scale, gain):
        slope = dq_scr[slot] * factor
        inner = slope * gain
        shared = inner * unit
        result = scale * (
            inner
            - plain(inner.astype(low), mean_map)
            - unit * plain(shared.astype(low), mean_map)
        )
        grad_ref[slot] = result.astype(low)
        gain_ref[0, slot : slot + 1] = jnp.sum(slope * unit, axis=0, keepdims=True)

    norm_back(0, 0.125, q_unit, q_scale, gq_ref[...])
    norm_back(1, 1.0, k_unit, k_scale, gk_ref[...])


def attend_specs(count, width, first=0):
    pairs = width // 128
    column = lambda offset: pl.BlockSpec((count, 128), lambda i: (0, i + first + offset))
    fixed = lambda shape: pl.BlockSpec(shape, lambda i: (0, 0))
    shared = [
        column(0),
        column(pairs),
        column(2 * pairs),
        fixed((count, 1)),
        fixed((1, 128)),
        fixed((1, 128)),
    ]
    return pairs, column, shared


VMEM = pl.BlockSpec(memory_space=pltpu.VMEM)


def attend(mixed, segments, gain_q, gain_k, weight, identity):
    count = mixed.shape[0]
    width = mixed.shape[1] // 3
    fetching = weight is not None
    extra = fetch_parts((weight,)) if fetching else ((), [], [])
    result = list(pl.pallas_call(
        functools.partial(attend_kernel, fetching),
        in_specs=[VMEM] * (4 + len(extra[0])),
        out_specs=[VMEM] * (2 + len(extra[1])),
        out_shape=[
            jax.ShapeDtypeStruct((count, width), low),
            jax.ShapeDtypeStruct((count, width), full),
        ]
        + extra[1],
        scratch_shapes=extra[2],
        compiler_params=sender(identity if fetching else None),
        cost_estimate=pl.CostEstimate(
            flops=16 * count * count * width,
            bytes_accessed=count * width * 12,
            transcendentals=count * count * width // 64,
        ),
        name="attend",
    )(mixed, segments, gain_q, gain_k, *extra[0]))
    if fetching:
        result[2] = result[2].reshape(-1, weight.shape[1])
    return result


def attend_back(mixed, segments, gain_q, gain_k, attended, log_total, grad, first, pairs):
    count = mixed.shape[0]
    width = mixed.shape[1] // 3
    _, column, shared = attend_specs(count, width, first)
    return pl.pallas_call(
        attend_back_kernel,
        grid=(pairs,),
        in_specs=shared + [column(0), column(0), column(0)],
        out_specs=[
            pl.BlockSpec((3, count, 128), lambda i: (0, 0, i)),
            pl.BlockSpec((1, 2, 128), lambda i: (i, 0, 0)),
        ],
        scratch_shapes=[pltpu.VMEM((2, count, 128), full)],
        out_shape=[
            jax.ShapeDtypeStruct((3, count, pairs * 128), low),
            jax.ShapeDtypeStruct((pairs, 2, 128), full),
        ],
        compiler_params=pltpu.CompilerParams(vmem_limit_bytes=50 * 2**20),
        cost_estimate=pl.CostEstimate(
            flops=40 * count * count * pairs * 128,
            bytes_accessed=count * pairs * 128 * 18,
            transcendentals=count * count * pairs * 2,
        ),
        name="attend_back",
    )(mixed, mixed, mixed, segments, gain_q, gain_k, attended, log_total, grad)


def input_grad_kernel(tokens_ref, gain_ref, above_ref, *refs):
    parts, (weight_ref, out_ref, sums_ref) = refs[:-3], refs[-3:]
    width = tokens_ref.shape[1]
    size = width // len(parts)
    slope = 0.0
    for p, part_ref in enumerate(parts):
        for kind in range(3):
            start = kind * width + p * size
            slope += right_product(part_ref[kind], weight_ref[:, start : start + size])
    value = tokens_ref[...].astype(full)
    centred = value - jnp.mean(value, axis=-1, keepdims=True)
    scale = lax.rsqrt(jnp.mean(centred * centred, axis=-1, keepdims=True) + norm_eps)
    unit = centred * scale
    inner = slope * gain_ref[...]
    shared = slope * unit
    back = scale * (
        inner
        - jnp.mean(inner, axis=-1, keepdims=True)
        - unit * jnp.mean(inner * unit, axis=-1, keepdims=True)
    )
    out_ref[...] = (above_ref[...] + back).astype(out_ref.dtype)
    sums = jnp.concatenate(
        [jnp.sum(shared, axis=0, keepdims=True), jnp.sum(slope, axis=0, keepdims=True)]
    )
    first = pl.program_id(0) == 0

    @pl.when(first)
    def _():
        sums_ref[...] = sums

    @pl.when(jnp.logical_not(first))
    def _():
        sums_ref[...] += sums


def input_grad(tokens, gain, above, parts, weight):
    count, width = tokens.shape
    tile = min(256, count)
    rows = pl.BlockSpec((tile, width), lambda i: (i, 0))
    whole = lambda array: pl.BlockSpec(array.shape, lambda i: (0, 0))
    return pl.pallas_call(
        input_grad_kernel,
        grid=(count // tile,),
        in_specs=[rows, whole(gain), rows]
        + [pl.BlockSpec((3, tile, part.shape[2]), lambda i: (0, i, 0)) for part in parts]
        + [whole(weight)],
        out_specs=[rows, pl.BlockSpec((2, width), lambda i: (0, 0))],
        out_shape=[
            jax.ShapeDtypeStruct((count, width), low),
            jax.ShapeDtypeStruct((2, width), full),
        ],
        compiler_params=pltpu.CompilerParams(vmem_limit_bytes=50 * 2**20),
        cost_estimate=pl.CostEstimate(
            flops=6 * count * width * width,
            bytes_accessed=count * width * 14 + 6 * width * width,
            transcendentals=0,
        ),
        name="input_grad",
    )(tokens, gain, above, *parts, weight)


def gelu_terms(value):
    size = jnp.abs(value)
    t = 1.0 / (1.0 + 0.3275911 * 0.70710678118 * size)
    expo = jnp.exp(-0.5 * value * value)
    series = 0.254829592 + t * (
        -0.284496736 + t * (1.421413741 + t * (-1.453152027 + t * 1.061405429))
    )
    below = 0.5 * t * series * expo
    share = jnp.where(value >= 0.0, 1.0 - below, below)
    return value * share, share + value * expo * 0.3989422804


def expand_kernel(fetching, rows_ref, weight_ref, shift_ref, *refs):
    if fetching:
        own_ref, active_ref, slope_ref, all_ref, send, recv, local = refs
        arrivals = fetch_steps(((own_ref, all_ref),), send, recv, local)
        next(arrivals)
    else:
        active_ref, slope_ref = refs
    columns = weight_ref.shape[1]
    count = rows_ref.shape[0]
    tile, height = 256, min(128, count)

    def one(i, carry):
        spot = pl.ds(pl.multiple_of(i * height, height), height)
        rows = rows_ref[spot, :]
        for start in range(0, columns, tile):
            span = slice(start, start + tile)
            hidden = plain(rows, weight_ref[:, span]) + shift_ref[:, span]
            active, slope = gelu_terms(hidden)
            active_ref[spot, span] = active.astype(low)
            slope_ref[spot, span] = slope.astype(low)
        return carry

    tiles = count // height
    early, late = tiles // 2, tiles - 1
    lax.fori_loop(0, early, one, 0)
    if fetching:
        next(arrivals)
    lax.fori_loop(early, late, one, 0)
    if fetching:
        next(arrivals)
    lax.fori_loop(late, tiles, one, 0)
    if fetching:
        for _ in arrivals:
            pass


def expand(rows, weight, shift, other, identity):
    count, width = rows.shape
    columns = weight.shape[1]
    fetching = other is not None
    extra = fetch_parts((other,)) if fetching else ((), [], [])
    result = list(pl.pallas_call(
        functools.partial(expand_kernel, fetching),
        in_specs=[VMEM] * (3 + len(extra[0])),
        out_specs=[VMEM] * (2 + len(extra[1])),
        out_shape=[jax.ShapeDtypeStruct((count, columns), low)] * 2 + extra[1],
        scratch_shapes=extra[2],
        compiler_params=sender(identity if fetching else None),
        cost_estimate=pl.CostEstimate(
            flops=2 * count * width * columns,
            bytes_accessed=2 * width * columns + 4 * count * columns,
            transcendentals=2 * count * columns,
        ),
        name="expand",
    )(rows, weight, shift.reshape(1, -1), *extra[0]))
    if fetching:
        result[2] = result[2].reshape(-1, other.shape[1])
    return result


def weight_grad_kernel(rows_ref, part_ref, out_ref, sums_ref, turned):
    @pl.when(pl.program_id(0) == 0)
    def _():
        turned[...] = rows_ref[...].T

    part = part_ref[0]
    out_ref[...] = plain(turned[...], part).astype(low)
    sums_ref[0] = jnp.sum(part.astype(full), axis=0, keepdims=True)


def weight_grad(rows, parts):
    count, width = rows.shape
    kinds, _, columns = parts.shape
    return pl.pallas_call(
        weight_grad_kernel,
        grid=(kinds,),
        in_specs=[
            pl.BlockSpec((count, width), lambda i: (0, 0)),
            pl.BlockSpec((1, count, columns), lambda i: (i, 0, 0)),
        ],
        out_specs=[
            pl.BlockSpec((width, columns), lambda i: (0, i)),
            pl.BlockSpec((1, 1, columns), lambda i: (i, 0, 0)),
        ],
        out_shape=[
            jax.ShapeDtypeStruct((width, kinds * columns), low),
            jax.ShapeDtypeStruct((kinds, 1, columns), full),
        ],
        scratch_shapes=[pltpu.VMEM((width, count), low)],
        compiler_params=pltpu.CompilerParams(vmem_limit_bytes=40 * 2**20),
        cost_estimate=pl.CostEstimate(
            flops=2 * count * width * kinds * columns,
            bytes_accessed=2 * (count + width) * (kinds + 1) * columns,
            transcendentals=0,
        ),
        name="weight_grad",
    )(rows, parts)


def place(axis, bit):
    return lax.rem(lax.div(lax.axis_index(axis), 1 << bit), 2)


def across(axis, bit):
    index = lax.axis_index(axis)
    return {axis: index + (1 - 2 * place(axis, bit)) * (1 << bit)}


def greet(partners):
    barrier = pltpu.get_barrier_semaphore()
    for partner in partners:
        pl.semaphore_signal(
            barrier, inc=1, device_id=partner, device_id_type=pl.DeviceIdType.MESH
        )
    pl.semaphore_wait(barrier, len(partners))


class Copies:
    def __init__(self, send_sems, recv_sems):
        self.send_sems, self.recv_sems = send_sems, recv_sems
        self.all = []

    def send(self, source, target, partner):
        index = len(self.all)
        copy = pltpu.make_async_remote_copy(
            src_ref=source,
            dst_ref=target,
            send_sem=self.send_sems.at[index],
            recv_sem=self.recv_sems.at[index],
            device_id=partner,
            device_id_type=pl.DeviceIdType.MESH,
        )
        copy.start()
        self.all.append(copy)
        return copy

    def finish(self):
        for copy in self.all:
            copy.wait_send()


def sender(identity):
    if identity is None:
        return pltpu.CompilerParams(vmem_limit_bytes=50 * 2**20)
    return pltpu.CompilerParams(
        collective_id=identity, has_side_effects=True, vmem_limit_bytes=50 * 2**20
    )


def fetch_parts(weights):
    parts = []
    for weight in weights:
        rows, columns = weight.shape
        parts.append(weight.reshape(2, 2, rows // 4, columns))
    count = 3 + 9 * len(parts)
    shapes = [jax.ShapeDtypeStruct((4,) + part.shape, part.dtype) for part in parts]
    sems = [
        pltpu.SemaphoreType.DMA((count,)),
        pltpu.SemaphoreType.DMA((count,)),
        pltpu.SemaphoreType.DMA((len(parts) + 1,)),
    ]
    return parts, shapes, sems


def fetch_steps(whole, send, recv, local, small=None):
    core, x, y = place("core", 0), place("fsdp", 0), place("fsdp", 1)
    me = lax.axis_index("fsdp")
    to_core, to_x, to_y = across("core", 0), across("fsdp", 0), across("fsdp", 1)
    to_far = {"fsdp": 3 - me}
    partners = [to_core, to_x, to_y]
    greet(partners if small is None else partners + [to_far])
    copies = Copies(send, recv)
    arrivals = []
    if small is not None:
        for partner in (to_x, to_y, to_far):
            arrivals.append(copies.send(small[0], small[1].at[me], partner))
    from_x_row, from_y_row, far_row = 2 * y + 1 - x, 2 * (1 - y) + x, 3 - me
    ahead, behind = [], []
    for own, target in whole:
        ahead.append(
            (
                copies.send(own.at[core, 0], target.at[me, core, 0], to_x),
                copies.send(own.at[core, 1], target.at[me, core, 1], to_y),
            )
        )
    for own, target in whole:
        behind.append(
            (
                copies.send(own.at[core, 1], target.at[me, core, 1], to_x),
                copies.send(own.at[core, 0], target.at[me, core, 0], to_y),
            )
        )
    own_copies = [
        pltpu.make_async_copy(own, target.at[me], local.at[i])
        for i, (own, target) in enumerate(whole + (() if small is None else (small,)))
    ]
    for copy in own_copies:
        copy.start()
    yield
    far = []
    for (own, target), (by_x, by_y) in zip(whole, ahead):
        by_x.wait_recv()
        quarter = target.at[from_x_row, core, 0]
        low_far = copies.send(quarter, quarter, to_y)
        by_y.wait_recv()
        quarter = target.at[from_y_row, core, 1]
        far.append((low_far, copies.send(quarter, quarter, to_x)))
    yield
    for (own, target), (by_x, by_y) in zip(whole, behind):
        by_x.wait_recv()
        half = target.at[from_x_row, core]
        arrivals.append(copies.send(half, half, to_core))
        by_y.wait_recv()
        half = target.at[from_y_row, core]
        arrivals.append(copies.send(half, half, to_core))
    yield
    for (own, target), (low_far, high_far) in zip(whole, far):
        low_far.wait_recv()
        high_far.wait_recv()
        half = target.at[far_row, core]
        arrivals.append(copies.send(half, half, to_core))
    for copy in arrivals:
        copy.wait_recv()
    for copy in own_copies:
        copy.wait()
    copies.finish()


def fetch_kernel(qkv_ref, out_ref, small_ref, qkv_all, out_all, small_all, send, recv, local):
    whole = ((qkv_ref, qkv_all), (out_ref, out_all))
    for _ in fetch_steps(whole, send, recv, local, (small_ref, small_all)):
        pass


def fetch(qkv_weight, out_weight, small):
    parts, shapes, sems = fetch_parts((qkv_weight, out_weight))
    qkv_w, out_w, vectors = pl.pallas_call(
        fetch_kernel,
        in_specs=[VMEM] * 3,
        out_specs=[VMEM] * 3,
        out_shape=shapes + [jax.ShapeDtypeStruct((4,) + small.shape, small.dtype)],
        scratch_shapes=sems,
        compiler_params=sender(0),
        name="fetch",
    )(*parts, small)
    return (
        qkv_w.reshape(-1, qkv_weight.shape[1]),
        out_w.reshape(-1, out_weight.shape[1]),
        vectors.reshape(4, -1),
    )


def total_kernel(chips, width, kinds, *refs):
    count = len(kinds)
    ins, small_ref = refs[:count], refs[count]
    outs, small_out = refs[count + 1 : 2 * count + 1], refs[2 * count + 1]
    first, left, right, second, third, fourth, last, small_in, send, recv = refs[2 * count + 2 :]
    core, x, y, chip = place("core", 0), place("fsdp", 0), place("fsdp", 1), place("z", 0)
    me = lax.axis_index("fsdp")
    to_core, to_x, to_y = across("core", 0), across("fsdp", 0), across("fsdp", 1)
    to_z = [across("z", bit) for bit in range(chips.bit_length() - 1)]
    partners = [to_core, to_x, to_y] + to_z
    greet(partners)
    copies = Copies(send, recv)

    chunks = []
    for index, kind in enumerate(kinds):
        stack, columns = kind
        for q in range(stack):
            for p in range(columns // width):
                span = slice(p * width, (p + 1) * width)
                chunks.append((ins[index], outs[index], q, span))

    shared = []
    for c, (source, _, q, span) in enumerate(chunks):
        lanes = pl.ds(span.start, width)
        mine = source.at[:, :, q, 1 - core, :, :, lanes]
        shared.append(copies.send(mine, first.at[c], to_core))

    def steps(c):
        source, target, q, span = chunks[c]
        lanes = pl.ds(span.start, width)
        shared[c].wait_recv()
        for row in range(2):
            first[c, row] = first[c, row] + source[row, :, q, core, :, :, lanes]
        by_x = copies.send(first.at[c, :, 1 - x, 0], left.at[c], to_x)
        by_y = copies.send(first.at[c, 1 - y, :, 1], right.at[c], to_y)
        yield
        yield
        by_x.wait_recv()
        left[c] = left[c] + first[c, :, x, 0]
        by_y.wait_recv()
        right[c] = right[c] + first[c, y, :, 1]
        by_y = copies.send(left.at[c, 1 - y], second.at[c, 0], to_y)
        by_x = copies.send(right.at[c, 1 - x], second.at[c, 1], to_x)
        yield
        by_y.wait_recv()
        second[c, 0] = second[c, 0] + left[c, y]
        by_x.wait_recv()
        second[c, 1] = second[c, 1] + right[c, x]
        copy = copies.send(second.at[c, 1 - chip], third.at[c], to_z[0])
        yield
        copy.wait_recv()
        third[c] = third[c] + second[c, chip]
        summed = third
        for bit, partner in enumerate(to_z[1:]):
            buffer = fourth.at[bit]
            copy = copies.send(summed.at[c], buffer.at[c], partner)
            yield
            copy.wait_recv()
            buffer[c] = buffer[c] + summed[c]
            summed = buffer
        last[c, core, chip] = summed[c]
        copy = copies.send(summed.at[c], last.at[c, core, chip], to_z[0])
        yield
        copy.wait_recv()
        half = last.at[c, core]
        copy = copies.send(half, half, to_core)
        yield
        copy.wait_recv()
        target[q, :, :, :, lanes] = last[c].astype(full)

    def small_steps():
        source = small_ref
        for index, partner in enumerate(partners):
            copy = copies.send(source, small_in.at[index], partner)
            yield
            copy.wait_recv()
            small_in[index] = small_in[index] + source[...]
            source = small_in.at[index]
        small_out[...] = source[me]

    waiting = [small_steps()] + [steps(c) for c in range(len(chunks))]
    active = []
    while waiting or active:
        left_over = []
        for chain in active:
            try:
                next(chain)
                left_over.append(chain)
            except StopIteration:
                pass
        active = left_over
        for chain in waiting[:1] if active else waiting[:2]:
            next(chain)
            active.append(chain)
            waiting = waiting[1:]
    copies.finish()


def total(parts, small, chips, height, width):
    kinds, views, count = [], [], 0
    for part in parts:
        rows, columns = part.shape
        stack = rows // height
        kinds.append((stack, columns))
        views.append(part.reshape(2, 2, stack, 2, 2, rows // (16 * stack), columns))
        count += stack * (columns // width)
    piece = height // 16
    stages = chips.bit_length() - 1
    copies = count * (7 + stages + 1) + 3 + stages
    outs = [
        jax.ShapeDtypeStruct(view.shape[2:], full) for view in views
    ] + [jax.ShapeDtypeStruct(small.shape[1:], full)]
    vmem = pl.BlockSpec(memory_space=pltpu.VMEM)
    sums = pl.pallas_call(
        functools.partial(total_kernel, chips, width, tuple(kinds)),
        in_specs=[vmem] * (len(parts) + 1),
        out_specs=[vmem] * (len(parts) + 1),
        out_shape=outs,
        scratch_shapes=[
            pltpu.VMEM((count, 2, 2, 2, piece, width), low),
            pltpu.VMEM((count, 2, piece, width), low),
            pltpu.VMEM((count, 2, piece, width), low),
            pltpu.VMEM((count, 2, piece, width), low),
            pltpu.VMEM((count, piece, width), low),
            pltpu.VMEM((stages - 1, count, piece, width), low),
            pltpu.VMEM((count, 2, 2, piece, width), low),
            pltpu.VMEM((3 + stages,) + small.shape, full),
            pltpu.SemaphoreType.DMA((copies,)),
            pltpu.SemaphoreType.DMA((copies,)),
        ],
        compiler_params=pltpu.CompilerParams(
            collective_id=1, has_side_effects=True, vmem_limit_bytes=60 * 2**20
        ),
        name="total",
    )(*views, small)
    return [
        result.reshape(-1, part.shape[1]) for result, part in zip(sums, parts)
    ], sums[-1].reshape(-1)


def shards(
    groups,
    copies,
    tokens,
    segments,
    cotangent,
    qkv_weight,
    qkv_bias,
    out_weight,
    out_bias,
    up_weight,
    up_bias,
    down_weight,
    down_bias,
    first_gain,
    first_shift,
    second_gain,
    second_shift,
    query_gain,
    key_gain,
):
    vectors = [
        qkv_bias,
        out_bias,
        up_bias,
        down_bias,
        first_gain,
        first_shift,
        second_gain,
        second_shift,
        query_gain,
        key_gain,
    ]
    count, width = tokens.shape
    column = segments.reshape(count, 1)
    valid = (segments >= 0)[:, None]

    small = jnp.concatenate(vectors).reshape(1, -1)
    gather = functools.partial(lax.all_gather, axis_name="fsdp", axis=0, tiled=True)
    kernels = groups == 4 and copies >= 8
    if kernels:
        qkv_w, out_w, small = fetch(qkv_weight, out_weight, small)
    else:
        qkv_w, out_w, small = gather(qkv_weight), gather(out_weight), gather(small)
    whole, start = [], 0
    for vector in vectors:
        size = vector.shape[0]
        whole.append(small[:, start : start + size].reshape(-1).astype(full))
        start += size
    (qkv_b, out_b, up_b, down_b, gain_1, shift_1, gain_2, shift_2, gain_q, gain_k) = whole
    pair_q = jnp.tile(gain_q, 2).reshape(1, 128)
    pair_k = jnp.tile(gain_k, 2).reshape(1, 128)
    normed = layer_norm(tokens.astype(full), gain_1, shift_1).astype(low)
    mixed = (plain(normed, qkv_w) + qkv_b).astype(low)
    attended, log_total, *fetched = attend(
        mixed, column, pair_q, pair_k, up_weight if kernels else None, 2
    )
    up_w = fetched[0] if kernels else gather(up_weight)
    inputs = tokens.astype(full)
    residual = inputs + plain(attended, out_w) + out_b
    second, second_back = jax.vjp(layer_norm, residual, gain_2, shift_2)
    second = second.astype(low)
    active, slope, *fetched = expand(second, up_w, up_b, down_weight if kernels else None, 3)
    down_w = fetched[0] if kernels else gather(down_weight)

    grad_low = jnp.where(valid, cotangent, jnp.zeros_like(cotangent))
    grad_output = grad_low.astype(full)
    down_b_grad = jnp.sum(grad_output, axis=0)
    down_grad = left_product(active, grad_low).astype(low)
    grad_hidden = (right_product(grad_low, down_w) * slope.astype(full)).astype(low)
    up_b_grad = jnp.sum(grad_hidden.astype(full), axis=0)
    output = jnp.where(valid, residual + plain(active, down_w) + down_b, 0.0).astype(low)
    up_grad = left_product(second, grad_hidden).astype(low)
    grad_norm_2, gain_2_grad, shift_2_grad = second_back(right_product(grad_hidden, up_w))
    grad_residual = grad_output + grad_norm_2
    branch = grad_residual.astype(low)
    out_b_grad = jnp.sum(branch.astype(full), axis=0)
    out_grad = left_product(attended, branch).astype(low)
    grad_attended = right_product(branch, out_w).astype(low)
    part, pair_gains = attend_back(
        mixed,
        column,
        pair_q,
        pair_k,
        attended,
        log_total,
        grad_attended,
        0,
        width // 128,
    )
    qkv_grad, qkv_b_grad = weight_grad(normed, part)
    gain_sums = jnp.sum(pair_gains, axis=0).reshape(2, 2, -1).sum(axis=1)
    grad_input, sums_1 = input_grad(tokens, gain_1.reshape(1, -1), grad_residual, [part], qkv_w)
    vectors = [
        qkv_b_grad.reshape(-1),
        out_b_grad,
        up_b_grad,
        down_b_grad,
        sums_1[0],
        sums_1[1],
        gain_2_grad,
        shift_2_grad,
        gain_sums[0],
        gain_sums[1],
    ]
    rows = jnp.concatenate([vector.reshape(groups, -1) for vector in vectors], axis=1)
    grads = [down_grad, up_grad, out_grad, qkv_grad]
    if kernels:
        grads, sums = total(grads, rows.reshape(groups, 1, -1), copies // 2, width, width)
    else:
        scatter = functools.partial(
            lax.psum_scatter, axis_name="fsdp", scatter_dimension=0, tiled=True
        )
        grads = [lax.psum(scatter(grad), ("z", "core")).astype(full) for grad in grads]
        sums = lax.psum(scatter(rows), ("z", "core")).reshape(-1)
    final, start = [], 0
    for vector in vectors:
        size = vector.shape[0] // groups
        final.append(sums[start : start + size])
        start += size
    return (
        output,
        grad_input,
        grads[3],
        final[0],
        grads[2],
        final[1],
        grads[1],
        final[2],
        grads[0],
        final[3],
        *final[4:],
    )


def solution(mesh):
    copies, groups = mesh.shape["dp"], mesh.shape["fsdp"]
    devices = mesh.devices.reshape(copies // 2, 2, groups)
    mesh = jax.sharding.Mesh(devices, ("z", "core", "fsdp"))
    rows = P(("z", "core", "fsdp"), None)
    matrix = P("fsdp", None)
    vector = P("fsdp")
    params = (matrix, vector) * 4 + (vector,) * 6
    return jax.shard_map(
        functools.partial(shards, groups, copies),
        mesh=mesh,
        in_specs=(rows, P(("z", "core", "fsdp")), rows) + params,
        out_specs=(rows, rows) + params,
        check_vma=False,
    )
```

```python
import functools

import jax
import jax.numpy as jnp
from jax import lax
from jax.experimental import pallas as pl
from jax.experimental.pallas import tpu as pltpu
from jax.sharding import PartitionSpec as P

norm_eps = 1e-06
low = jnp.bfloat16
full = jnp.float32


def layer_norm(value, gain, shift):
    centred = value - jnp.mean(value, axis=-1, keepdims=True)
    scaled = centred * lax.rsqrt(jnp.mean(centred * centred, axis=-1, keepdims=True) + norm_eps)
    return scaled * gain + shift


def exact_gelu(value):
    return jax.nn.gelu(value, approximate=False)


def left_product(left, right):
    return lax.dot_general(
        left, right, (((0,), (0,)), ((), ())), preferred_element_type=jnp.float32
    )


def right_product(left, right):
    return lax.dot_general(
        left, right, (((1,), (1,)), ((), ())), preferred_element_type=jnp.float32
    )


def plain(left, right):
    return jnp.dot(left, right, preferred_element_type=jnp.float32)


def lane_index(shape):
    return lax.broadcasted_iota(jnp.int32, shape, len(shape) - 1)


def same_head(scale):
    row = lax.broadcasted_iota(jnp.int32, (128, 128), 0) // 64
    column = lax.broadcasted_iota(jnp.int32, (128, 128), 1) // 64
    return jnp.where(row == column, scale, 0.0).astype(low)


def head_norm(raw, mean_map):
    value = raw.astype(full)
    centred = value - plain(raw, mean_map)
    scale = lax.rsqrt(plain((centred * centred).astype(low), mean_map) + norm_eps)
    return centred * scale, scale


def half_mask(head, lanes):
    return (lanes < 64) if head == 0 else (lanes >= 64)


def query_codes(segments, lanes):
    spot = lanes % 64
    match = jnp.where(spot == segments + 1, 128.0, 0.0)
    return jnp.where(spot == 17, -128.0, match)


def key_codes(segments, lanes):
    spot = lanes % 64
    match = jnp.where(spot == segments + 1, 1.0, 0.0)
    return jnp.where((spot >= 17) & (spot < 20), 1.0, match)


def spans(count):
    cut = count * 9 // 16
    return ((0, cut), (cut, count))


def attend_pair(queries, keys, values, segments, gain_q, gain_k, store):
    count = queries.shape[0]
    lanes = lane_index((count, 128))
    mean_map = same_head(1.0 / 64)
    q_unit, _ = head_norm(queries, mean_map)
    k_unit, _ = head_norm(keys, mean_map)
    q_low = q_unit * (gain_q * 0.125)
    k_low = k_unit * gain_k
    q_code = query_codes(segments, lanes)
    k_code = key_codes(segments, lanes)
    q_heads = [jnp.where(half_mask(h, lanes), q_low, q_code).astype(low) for h in (0, 1)]
    k_heads = [jnp.where(half_mask(h, lanes), k_low, k_code).astype(low) for h in (0, 1)]
    v_heads = [
        jnp.where(half_mask(h, lanes), values.astype(full), 1.0).astype(low) for h in (0, 1)
    ]
    for first, last in spans(count):
        tile = (last - first) // 2
        for start in range(first, last, tile):
            parts = []
            for h in (0, 1):
                scores = right_product(q_heads[h][start : start + tile], k_heads[h][first:last])
                parts.append(plain(jnp.exp(scores).astype(low), v_heads[h][first:last]))
            here = lane_index((tile, 128)) < 64
            raw = jnp.where(here, parts[0], parts[1])
            sums = jnp.where(here, parts[1], parts[0])
            total = pltpu.roll(sums, 64, 1)
            store(slice(start, start + tile), raw / total, jnp.log(sums))


def forward_kernel(
    fetching,
    mixed_ref,
    seg_ref,
    gq_ref,
    gk_ref,
    tokens_ref,
    proj_ref,
    proj_shift_ref,
    gain_ref,
    shift_ref,
    up_shift_ref,
    *refs,
):
    if fetching:
        own_up, own_down = refs[:2]
        o_ref, total_ref, residual_ref, second_ref, active_ref, slope_ref = refs[2:8]
        up_ref, down_ref, send, recv, local = refs[8:]
        arrivals = fetch_sequence((own_up, up_ref), (own_down, down_ref), send, recv, local)
    else:
        up_ref = refs[0]
        o_ref, total_ref, residual_ref, second_ref, active_ref, slope_ref = refs[1:]
        arrivals = iter(())
    count, width = o_ref.shape
    pairs = width // 128
    columns = up_shift_ref.shape[1]
    tile, height = 256, min(128, count)
    tiles = count // height

    def one(i, carry):
        def lanes(kind):
            return pl.ds(pl.multiple_of(kind * width + i * 128, 128), 128)

        def store(rows, value, log_total):
            o_ref[rows, lanes(0)] = value.astype(low)
            total_ref[rows, lanes(0)] = log_total

        attend_pair(
            mixed_ref[:, lanes(0)],
            mixed_ref[:, lanes(1)],
            mixed_ref[:, lanes(2)],
            seg_ref[...],
            gq_ref[...],
            gk_ref[...],
            store,
        )
        return carry

    def spot_of(i):
        return pl.ds(pl.multiple_of(i * height, height), height)

    def project(i, carry):
        spot = spot_of(i)
        value = (
            tokens_ref[spot, :].astype(full)
            + plain(o_ref[spot, :], proj_ref[...])
            + proj_shift_ref[...]
        )
        residual_ref[spot, :] = value
        second_ref[spot, :] = layer_norm(value, gain_ref[...], shift_ref[...]).astype(low)
        return carry

    def widen(i, carry):
        spot = spot_of(i)
        rows = second_ref[spot, :]
        for start in range(0, columns, tile):
            span = slice(start, start + tile)
            weight = up_ref[..., span].reshape(width, tile)
            hidden = plain(rows, weight) + up_shift_ref[:, span]
            active, slope = gelu_terms(hidden)
            active_ref[spot, span] = active.astype(low)
            slope_ref[spot, span] = slope.astype(low)
        return carry

    next(arrivals, None)
    lax.fori_loop(0, pairs // 2, one, 0)
    next(arrivals, None)
    lax.fori_loop(pairs // 2, pairs - 1, one, 0)
    next(arrivals, None)
    lax.fori_loop(pairs - 1, pairs, one, 0)
    next(arrivals, None)
    lax.fori_loop(0, tiles, project, 0)
    next(arrivals, None)
    lax.fori_loop(0, tiles // 2, widen, 0)
    next(arrivals, None)
    lax.fori_loop(tiles // 2, tiles - 2, widen, 0)
    next(arrivals, None)
    lax.fori_loop(tiles - 2, tiles, widen, 0)
    for _ in arrivals:
        pass


def attend_back_kernel(
    q_ref,
    k_ref,
    v_ref,
    seg_ref,
    gq_ref,
    gk_ref,
    o_ref,
    total_ref,
    do_ref,
    grad_ref,
    gain_ref,
    dq_scr,
):
    count = q_ref.shape[0]
    lanes = lane_index((count, 128))
    spot = lanes % 64
    mean_map = same_head(1.0 / 64)
    q_unit, q_scale = head_norm(q_ref[...], mean_map)
    k_unit, k_scale = head_norm(k_ref[...], mean_map)
    q_low = (q_unit * (gq_ref[...] * 0.125)).astype(low)
    k_low = (k_unit * gk_ref[...]).astype(low)
    segments = seg_ref[...]
    log_total = total_ref[...]
    log_high = log_total.astype(low).astype(full)
    q_code = jnp.where(
        spot == 18,
        -log_high,
        jnp.where(spot == 19, log_high - log_total, query_codes(segments, lanes)),
    ).astype(low)
    k_code = key_codes(segments, lanes).astype(low)
    grads = do_ref[...]
    product = (grads.astype(full) * o_ref[...].astype(full)).astype(low)
    row = lax.broadcasted_iota(jnp.int32, (128, 128), 0) // 64
    column = lax.broadcasted_iota(jnp.int32, (128, 128), 1) // 64
    delta = plain(product, jnp.where(row != column, 1.0, 0.0).astype(low))
    delta_high = delta.astype(low).astype(full)
    g_code = jnp.where(
        spot == 0, -delta_high, jnp.where(spot == 1, delta_high - delta, 0.0)
    ).astype(low)
    v_code = jnp.where(spot < 2, 1.0, 0.0).astype(low)
    values = v_ref[...]
    masks = [half_mask(h, lanes) for h in (0, 1)]
    q_heads = [jnp.where(masks[h], q_low, q_code) for h in (0, 1)]
    k_heads = [jnp.where(masks[h], k_low, k_code) for h in (0, 1)]
    v_heads = [jnp.where(masks[h], values, v_code) for h in (0, 1)]
    g_heads = [jnp.where(masks[h], grads, g_code) for h in (0, 1)]
    dk_parts = []

    def run(first, last, other_first, other_last, tile):
        for start in range(first, last, tile):
            rows = slice(start, start + tile)
            others = slice(other_first, other_last)
            dv_parts, dk_parts, dq_parts = [], [], []
            for h in (0, 1):
                scores = right_product(k_heads[h][rows], q_heads[h][others])
                weights = jnp.exp(scores)
                change = right_product(v_heads[h][rows], g_heads[h][others])
                sloped = (weights * change).astype(low)
                dv_parts.append(plain(weights.astype(low), grads[others]))
                dk_parts.append(plain(sloped, q_low[others]))
                dq_parts.append(left_product(sloped, k_low[rows]))
            here = lane_index((tile, 128)) < 64
            there = lane_index((other_last - other_first, 128)) < 64
            grad_ref[2, rows] = jnp.where(here, dv_parts[0], dv_parts[1]).astype(low)
            dk = jnp.where(here, dk_parts[0], dk_parts[1])
            dk_scr_store(rows, dk)
            dq = jnp.where(there, dq_parts[0], dq_parts[1])
            if start == first:
                dq_scr[0, others] = dq
            else:
                dq_scr[0, others] += dq

    def dk_scr_store(rows, value):
        dq_scr[1, rows] = value

    for first, last in spans(count):
        run(first, last, first, last, (last - first) // 2)

    def norm_back(slot, factor, unit, scale, gain):
        slope = dq_scr[slot] * factor
        inner = slope * gain
        shared = inner * unit
        result = scale * (
            inner
            - plain(inner.astype(low), mean_map)
            - unit * plain(shared.astype(low), mean_map)
        )
        grad_ref[slot] = result.astype(low)
        gain_ref[0, slot : slot + 1] = jnp.sum(slope * unit, axis=0, keepdims=True)

    norm_back(0, 0.125, q_unit, q_scale, gq_ref[...])
    norm_back(1, 1.0, k_unit, k_scale, gk_ref[...])


def attend_specs(count, width, first=0):
    pairs = width // 128
    column = lambda offset: pl.BlockSpec((count, 128), lambda i: (0, i + first + offset))
    fixed = lambda shape: pl.BlockSpec(shape, lambda i: (0, 0))
    shared = [
        column(0),
        column(pairs),
        column(2 * pairs),
        fixed((count, 1)),
        fixed((1, 128)),
        fixed((1, 128)),
    ]
    return pairs, column, shared


VMEM = pl.BlockSpec(memory_space=pltpu.VMEM)


def forward(mixed, vectors, tokens, proj, weights, fetching):
    segments, gain_q, gain_k, proj_shift, gain, shift, up_shift = vectors
    count, width = tokens.shape
    columns = up_shift.shape[0]
    flat = [proj_shift, gain, shift, up_shift]
    flat = [vector.reshape(1, -1) for vector in flat]
    extra = fetch_parts(weights) if fetching else (list(weights[:1]), [], [])
    shapes = [(width, low), (width, full), (width, full), (width, low), (columns, low)]
    shapes.append((columns, low))
    outs = [jax.ShapeDtypeStruct((count, size), kind) for size, kind in shapes] + extra[1]
    operands = [mixed, segments, gain_q, gain_k, tokens, proj, *flat, *extra[0]]
    result = list(
        pl.pallas_call(
            functools.partial(forward_kernel, fetching),
            in_specs=[VMEM] * len(operands),
            out_specs=[VMEM] * len(outs),
            out_shape=outs,
            scratch_shapes=extra[2],
            compiler_params=sender(2 if fetching else None),
            name="forward",
        )(*operands)
    )
    for i, weight in enumerate(weights if fetching else ()):
        result[6 + i] = result[6 + i].reshape(-1, weight.shape[1])
    return result


def attend_back(mixed, segments, gain_q, gain_k, attended, log_total, grad, first, pairs):
    count = mixed.shape[0]
    width = mixed.shape[1] // 3
    _, column, shared = attend_specs(count, width, first)
    return pl.pallas_call(
        attend_back_kernel,
        grid=(pairs,),
        in_specs=shared + [column(0), column(0), column(0)],
        out_specs=[
            pl.BlockSpec((3, count, 128), lambda i: (0, 0, i)),
            pl.BlockSpec((1, 2, 128), lambda i: (i, 0, 0)),
        ],
        scratch_shapes=[pltpu.VMEM((2, count, 128), full)],
        out_shape=[
            jax.ShapeDtypeStruct((3, count, pairs * 128), low),
            jax.ShapeDtypeStruct((pairs, 2, 128), full),
        ],
        compiler_params=pltpu.CompilerParams(vmem_limit_bytes=50 * 2**20),
        cost_estimate=pl.CostEstimate(
            flops=40 * count * count * pairs * 128,
            bytes_accessed=count * pairs * 128 * 18,
            transcendentals=count * count * pairs * 2,
        ),
        name="attend_back",
    )(mixed, mixed, mixed, segments, gain_q, gain_k, attended, log_total, grad)


def input_grad_kernel(tokens_ref, gain_ref, above_ref, *refs):
    parts, (weight_ref, out_ref, sums_ref) = refs[:-3], refs[-3:]
    width = tokens_ref.shape[1]
    size = width // len(parts)
    slope = 0.0
    for p, part_ref in enumerate(parts):
        for kind in range(3):
            start = kind * width + p * size
            slope += right_product(part_ref[kind], weight_ref[:, start : start + size])
    value = tokens_ref[...].astype(full)
    centred = value - jnp.mean(value, axis=-1, keepdims=True)
    scale = lax.rsqrt(jnp.mean(centred * centred, axis=-1, keepdims=True) + norm_eps)
    unit = centred * scale
    inner = slope * gain_ref[...]
    shared = slope * unit
    back = scale * (
        inner
        - jnp.mean(inner, axis=-1, keepdims=True)
        - unit * jnp.mean(inner * unit, axis=-1, keepdims=True)
    )
    out_ref[...] = (above_ref[...] + back).astype(out_ref.dtype)
    sums = jnp.concatenate(
        [jnp.sum(shared, axis=0, keepdims=True), jnp.sum(slope, axis=0, keepdims=True)]
    )
    first = pl.program_id(0) == 0

    @pl.when(first)
    def _():
        sums_ref[...] = sums

    @pl.when(jnp.logical_not(first))
    def _():
        sums_ref[...] += sums


def input_grad(tokens, gain, above, parts, weight):
    count, width = tokens.shape
    tile = min(256, count)
    rows = pl.BlockSpec((tile, width), lambda i: (i, 0))
    whole = lambda array: pl.BlockSpec(array.shape, lambda i: (0, 0))
    return pl.pallas_call(
        input_grad_kernel,
        grid=(count // tile,),
        in_specs=[rows, whole(gain), rows]
        + [pl.BlockSpec((3, tile, part.shape[2]), lambda i: (0, i, 0)) for part in parts]
        + [whole(weight)],
        out_specs=[rows, pl.BlockSpec((2, width), lambda i: (0, 0))],
        out_shape=[
            jax.ShapeDtypeStruct((count, width), low),
            jax.ShapeDtypeStruct((2, width), full),
        ],
        compiler_params=pltpu.CompilerParams(vmem_limit_bytes=50 * 2**20),
        cost_estimate=pl.CostEstimate(
            flops=6 * count * width * width,
            bytes_accessed=count * width * 14 + 6 * width * width,
            transcendentals=0,
        ),
        name="input_grad",
    )(tokens, gain, above, *parts, weight)


def gelu_terms(value):
    size = jnp.abs(value)
    t = 1.0 / (1.0 + 0.3275911 * 0.70710678118 * size)
    expo = jnp.exp(-0.5 * value * value)
    series = 0.254829592 + t * (
        -0.284496736 + t * (1.421413741 + t * (-1.453152027 + t * 1.061405429))
    )
    below = 0.5 * t * series * expo
    share = jnp.where(value >= 0.0, 1.0 - below, below)
    return value * share, share + value * expo * 0.3989422804


def weight_grad_kernel(rows_ref, part_ref, out_ref, sums_ref, turned):
    @pl.when(pl.program_id(0) == 0)
    def _():
        turned[...] = rows_ref[...].T

    part = part_ref[0]
    out_ref[...] = plain(turned[...], part).astype(low)
    sums_ref[0] = jnp.sum(part.astype(full), axis=0, keepdims=True)


def weight_grad(rows, parts):
    count, width = rows.shape
    kinds, _, columns = parts.shape
    return pl.pallas_call(
        weight_grad_kernel,
        grid=(kinds,),
        in_specs=[
            pl.BlockSpec((count, width), lambda i: (0, 0)),
            pl.BlockSpec((1, count, columns), lambda i: (i, 0, 0)),
        ],
        out_specs=[
            pl.BlockSpec((width, columns), lambda i: (0, i)),
            pl.BlockSpec((1, 1, columns), lambda i: (i, 0, 0)),
        ],
        out_shape=[
            jax.ShapeDtypeStruct((width, kinds * columns), low),
            jax.ShapeDtypeStruct((kinds, 1, columns), full),
        ],
        scratch_shapes=[pltpu.VMEM((width, count), low)],
        compiler_params=pltpu.CompilerParams(vmem_limit_bytes=40 * 2**20),
        cost_estimate=pl.CostEstimate(
            flops=2 * count * width * kinds * columns,
            bytes_accessed=2 * (count + width) * (kinds + 1) * columns,
            transcendentals=0,
        ),
        name="weight_grad",
    )(rows, parts)


def place(axis, bit):
    return lax.rem(lax.div(lax.axis_index(axis), 1 << bit), 2)


def across(axis, bit):
    index = lax.axis_index(axis)
    return {axis: index + (1 - 2 * place(axis, bit)) * (1 << bit)}


def greet(partners):
    barrier = pltpu.get_barrier_semaphore()
    for partner in partners:
        pl.semaphore_signal(
            barrier, inc=1, device_id=partner, device_id_type=pl.DeviceIdType.MESH
        )
    pl.semaphore_wait(barrier, len(partners))


class Copies:
    def __init__(self, send_sems, recv_sems):
        self.send_sems, self.recv_sems = send_sems, recv_sems
        self.all = []

    def send(self, source, target, partner):
        index = len(self.all)
        copy = pltpu.make_async_remote_copy(
            src_ref=source,
            dst_ref=target,
            send_sem=self.send_sems.at[index],
            recv_sem=self.recv_sems.at[index],
            device_id=partner,
            device_id_type=pl.DeviceIdType.MESH,
        )
        copy.start()
        self.all.append(copy)
        return copy

    def finish(self):
        for copy in self.all:
            copy.wait_send()


def sender(identity):
    if identity is None:
        return pltpu.CompilerParams(vmem_limit_bytes=50 * 2**20)
    return pltpu.CompilerParams(
        collective_id=identity, has_side_effects=True, vmem_limit_bytes=50 * 2**20
    )


def fetch_parts(weights):
    parts = []
    for weight in weights:
        rows, columns = weight.shape
        parts.append(weight.reshape(2, 2, rows // 4, columns))
    count = 3 + 9 * len(parts)
    shapes = [jax.ShapeDtypeStruct((4,) + part.shape, part.dtype) for part in parts]
    sems = [
        pltpu.SemaphoreType.DMA((count,)),
        pltpu.SemaphoreType.DMA((count,)),
        pltpu.SemaphoreType.DMA((len(parts) + 1,)),
    ]
    return parts, shapes, sems


def fetch_steps(whole, send, recv, local, small=None):
    core, x, y = place("core", 0), place("fsdp", 0), place("fsdp", 1)
    me = lax.axis_index("fsdp")
    to_core, to_x, to_y = across("core", 0), across("fsdp", 0), across("fsdp", 1)
    to_far = {"fsdp": 3 - me}
    partners = [to_core, to_x, to_y]
    greet(partners if small is None else partners + [to_far])
    copies = Copies(send, recv)
    arrivals = []
    if small is not None:
        for partner in (to_x, to_y, to_far):
            arrivals.append(copies.send(small[0], small[1].at[me], partner))
    from_x_row, from_y_row, far_row = 2 * y + 1 - x, 2 * (1 - y) + x, 3 - me
    ahead, behind = [], []
    for own, target in whole:
        ahead.append(
            (
                copies.send(own.at[core, 0], target.at[me, core, 0], to_x),
                copies.send(own.at[core, 1], target.at[me, core, 1], to_y),
            )
        )
    for own, target in whole:
        behind.append(
            (
                copies.send(own.at[core, 1], target.at[me, core, 1], to_x),
                copies.send(own.at[core, 0], target.at[me, core, 0], to_y),
            )
        )
    own_copies = [
        pltpu.make_async_copy(own, target.at[me], local.at[i])
        for i, (own, target) in enumerate(whole + (() if small is None else (small,)))
    ]
    for copy in own_copies:
        copy.start()
    yield
    far = []
    for (own, target), (by_x, by_y) in zip(whole, ahead):
        by_x.wait_recv()
        quarter = target.at[from_x_row, core, 0]
        low_far = copies.send(quarter, quarter, to_y)
        by_y.wait_recv()
        quarter = target.at[from_y_row, core, 1]
        far.append((low_far, copies.send(quarter, quarter, to_x)))
    yield
    for (own, target), (by_x, by_y) in zip(whole, behind):
        by_x.wait_recv()
        half = target.at[from_x_row, core]
        arrivals.append(copies.send(half, half, to_core))
        by_y.wait_recv()
        half = target.at[from_y_row, core]
        arrivals.append(copies.send(half, half, to_core))
    yield
    for (own, target), (low_far, high_far) in zip(whole, far):
        low_far.wait_recv()
        high_far.wait_recv()
        half = target.at[far_row, core]
        arrivals.append(copies.send(half, half, to_core))
    for copy in arrivals:
        copy.wait_recv()
    for copy in own_copies:
        copy.wait()
    copies.finish()


def fetch_sequence(first, second, send, recv, local):
    core, x, y = place("core", 0), place("fsdp", 0), place("fsdp", 1)
    me = lax.axis_index("fsdp")
    to_core, to_x, to_y = across("core", 0), across("fsdp", 0), across("fsdp", 1)
    greet([to_core, to_x, to_y])
    copies = Copies(send, recv)
    from_x_row, from_y_row, far_row = 2 * y + 1 - x, 2 * (1 - y) + x, 3 - me

    def near(own, target):
        def one(quarter, partner):
            return copies.send(own.at[core, quarter], target.at[me, core, quarter], partner)

        return one(0, to_x), one(1, to_y), one(1, to_x), one(0, to_y)

    def forward_far(target, sent):
        sent[0].wait_recv()
        quarter = target.at[from_x_row, core, 0]
        low_far = copies.send(quarter, quarter, to_y)
        sent[1].wait_recv()
        quarter = target.at[from_y_row, core, 1]
        return low_far, copies.send(quarter, quarter, to_x)

    def share_near(target, sent):
        result = []
        for copy, row in ((sent[2], from_x_row), (sent[3], from_y_row)):
            copy.wait_recv()
            half = target.at[row, core]
            result.append(copies.send(half, half, to_core))
        return result

    def share_far(target, far):
        for copy in far:
            copy.wait_recv()
        half = target.at[far_row, core]
        return [copies.send(half, half, to_core)]

    sent = near(*first)
    own_copies = [
        pltpu.make_async_copy(own, target.at[me], local.at[i])
        for i, (own, target) in enumerate((first, second))
    ]
    for copy in own_copies:
        copy.start()
    yield
    far = forward_far(first[1], sent)
    later = near(*second)
    yield
    arrivals = share_near(first[1], sent)
    yield
    arrivals += share_far(first[1], far)
    yield
    for copy in arrivals + own_copies[:1]:
        if copy is own_copies[0]:
            copy.wait()
        else:
            copy.wait_recv()
    yield
    far = forward_far(second[1], later)
    yield
    arrivals = share_near(second[1], later)
    yield
    arrivals += share_far(second[1], far)
    for copy in arrivals:
        copy.wait_recv()
    own_copies[1].wait()
    copies.finish()


def fetch_kernel(qkv_ref, out_ref, small_ref, qkv_all, out_all, small_all, send, recv, local):
    whole = ((qkv_ref, qkv_all), (out_ref, out_all))
    for _ in fetch_steps(whole, send, recv, local, (small_ref, small_all)):
        pass


def fetch(qkv_weight, out_weight, small):
    parts, shapes, sems = fetch_parts((qkv_weight, out_weight))
    qkv_w, out_w, vectors = pl.pallas_call(
        fetch_kernel,
        in_specs=[VMEM] * 3,
        out_specs=[VMEM] * 3,
        out_shape=shapes + [jax.ShapeDtypeStruct((4,) + small.shape, small.dtype)],
        scratch_shapes=sems,
        compiler_params=sender(0),
        name="fetch",
    )(*parts, small)
    return (
        qkv_w.reshape(-1, qkv_weight.shape[1]),
        out_w.reshape(-1, out_weight.shape[1]),
        vectors.reshape(4, -1),
    )


def total_kernel(chips, width, kinds, *refs):
    count = len(kinds)
    ins, small_ref = refs[:count], refs[count]
    outs, small_out = refs[count + 1 : 2 * count + 1], refs[2 * count + 1]
    first, left, right, second, third, fourth, last, small_in, send, recv = refs[2 * count + 2 :]
    core, x, y, chip = place("core", 0), place("fsdp", 0), place("fsdp", 1), place("z", 0)
    me = lax.axis_index("fsdp")
    to_core, to_x, to_y = across("core", 0), across("fsdp", 0), across("fsdp", 1)
    to_z = [across("z", bit) for bit in range(chips.bit_length() - 1)]
    partners = [to_core, to_x, to_y] + to_z
    greet(partners)
    copies = Copies(send, recv)

    chunks = []
    for index, kind in enumerate(kinds):
        stack, columns = kind
        for q in range(stack):
            for p in range(columns // width):
                span = slice(p * width, (p + 1) * width)
                chunks.append((ins[index], outs[index], q, span))

    shared = []
    for c, (source, _, q, span) in enumerate(chunks):
        lanes = pl.ds(span.start, width)
        mine = source.at[:, :, q, 1 - core, :, :, lanes]
        shared.append(copies.send(mine, first.at[c], to_core))

    def steps(c):
        source, target, q, span = chunks[c]
        lanes = pl.ds(span.start, width)
        shared[c].wait_recv()
        for row in range(2):
            first[c, row] = first[c, row] + source[row, :, q, core, :, :, lanes]
        by_x = copies.send(first.at[c, :, 1 - x, 0], left.at[c], to_x)
        by_y = copies.send(first.at[c, 1 - y, :, 1], right.at[c], to_y)
        yield
        yield
        by_x.wait_recv()
        left[c] = left[c] + first[c, :, x, 0]
        by_y.wait_recv()
        right[c] = right[c] + first[c, y, :, 1]
        by_y = copies.send(left.at[c, 1 - y], second.at[c, 0], to_y)
        by_x = copies.send(right.at[c, 1 - x], second.at[c, 1], to_x)
        yield
        by_y.wait_recv()
        second[c, 0] = second[c, 0] + left[c, y]
        by_x.wait_recv()
        second[c, 1] = second[c, 1] + right[c, x]
        copy = copies.send(second.at[c, 1 - chip], third.at[c], to_z[0])
        yield
        copy.wait_recv()
        third[c] = third[c] + second[c, chip]
        summed = third
        for bit, partner in enumerate(to_z[1:]):
            buffer = fourth.at[bit]
            copy = copies.send(summed.at[c], buffer.at[c], partner)
            yield
            copy.wait_recv()
            buffer[c] = buffer[c] + summed[c]
            summed = buffer
        last[c, core, chip] = summed[c]
        copy = copies.send(summed.at[c], last.at[c, core, chip], to_z[0])
        yield
        copy.wait_recv()
        half = last.at[c, core]
        copy = copies.send(half, half, to_core)
        yield
        copy.wait_recv()
        target[q, :, :, :, lanes] = last[c].astype(full)

    def small_steps():
        source = small_ref
        for index, partner in enumerate(partners):
            copy = copies.send(source, small_in.at[index], partner)
            yield
            copy.wait_recv()
            small_in[index] = small_in[index] + source[...]
            source = small_in.at[index]
        small_out[...] = source[me]

    waiting = [small_steps()] + [steps(c) for c in range(len(chunks))]
    active = []
    while waiting or active:
        left_over = []
        for chain in active:
            try:
                next(chain)
                left_over.append(chain)
            except StopIteration:
                pass
        active = left_over
        for chain in waiting[:1] if active else waiting[:2]:
            next(chain)
            active.append(chain)
            waiting = waiting[1:]
    copies.finish()


def total(parts, small, chips, height, width):
    kinds, views, count = [], [], 0
    for part in parts:
        rows, columns = part.shape
        stack = rows // height
        kinds.append((stack, columns))
        views.append(part.reshape(2, 2, stack, 2, 2, rows // (16 * stack), columns))
        count += stack * (columns // width)
    piece = height // 16
    stages = chips.bit_length() - 1
    copies = count * (7 + stages + 1) + 3 + stages
    outs = [
        jax.ShapeDtypeStruct(view.shape[2:], full) for view in views
    ] + [jax.ShapeDtypeStruct(small.shape[1:], full)]
    vmem = pl.BlockSpec(memory_space=pltpu.VMEM)
    sums = pl.pallas_call(
        functools.partial(total_kernel, chips, width, tuple(kinds)),
        in_specs=[vmem] * (len(parts) + 1),
        out_specs=[vmem] * (len(parts) + 1),
        out_shape=outs,
        scratch_shapes=[
            pltpu.VMEM((count, 2, 2, 2, piece, width), low),
            pltpu.VMEM((count, 2, piece, width), low),
            pltpu.VMEM((count, 2, piece, width), low),
            pltpu.VMEM((count, 2, piece, width), low),
            pltpu.VMEM((count, piece, width), low),
            pltpu.VMEM((stages - 1, count, piece, width), low),
            pltpu.VMEM((count, 2, 2, piece, width), low),
            pltpu.VMEM((3 + stages,) + small.shape, full),
            pltpu.SemaphoreType.DMA((copies,)),
            pltpu.SemaphoreType.DMA((copies,)),
        ],
        compiler_params=pltpu.CompilerParams(
            collective_id=1, has_side_effects=True, vmem_limit_bytes=60 * 2**20
        ),
        name="total",
    )(*views, small)
    return [
        result.reshape(-1, part.shape[1]) for result, part in zip(sums, parts)
    ], sums[-1].reshape(-1)


def shards(
    groups,
    copies,
    tokens,
    segments,
    cotangent,
    qkv_weight,
    qkv_bias,
    out_weight,
    out_bias,
    up_weight,
    up_bias,
    down_weight,
    down_bias,
    first_gain,
    first_shift,
    second_gain,
    second_shift,
    query_gain,
    key_gain,
):
    vectors = [
        qkv_bias,
        out_bias,
        up_bias,
        down_bias,
        first_gain,
        first_shift,
        second_gain,
        second_shift,
        query_gain,
        key_gain,
    ]
    count, width = tokens.shape
    column = segments.reshape(count, 1)
    valid = (segments >= 0)[:, None]

    small = jnp.concatenate(vectors).reshape(1, -1)
    gather = functools.partial(lax.all_gather, axis_name="fsdp", axis=0, tiled=True)
    kernels = groups == 4 and copies >= 8
    if kernels:
        qkv_w, out_w, small = fetch(qkv_weight, out_weight, small)
    else:
        qkv_w, out_w, small = gather(qkv_weight), gather(out_weight), gather(small)
    whole, start = [], 0
    for vector in vectors:
        size = vector.shape[0]
        whole.append(small[:, start : start + size].reshape(-1).astype(full))
        start += size
    (qkv_b, out_b, up_b, down_b, gain_1, shift_1, gain_2, shift_2, gain_q, gain_k) = whole
    pair_q = jnp.tile(gain_q, 2).reshape(1, 128)
    pair_k = jnp.tile(gain_k, 2).reshape(1, 128)
    normed = layer_norm(tokens.astype(full), gain_1, shift_1).astype(low)
    mixed = (plain(normed, qkv_w) + qkv_b).astype(low)
    if kernels:
        weights = (up_weight, down_weight)
    else:
        weights = (gather(up_weight), gather(down_weight))
    vectors = (column, pair_q, pair_k, out_b, gain_2, shift_2, up_b)
    attended, log_total, residual, second, active, slope, *fetched = forward(
        mixed, vectors, tokens, out_w, weights, kernels
    )
    up_w, down_w = fetched if kernels else weights
    _, second_back = jax.vjp(layer_norm, residual, gain_2, shift_2)

    grad_low = jnp.where(valid, cotangent, jnp.zeros_like(cotangent))
    grad_output = grad_low.astype(full)
    down_b_grad = jnp.sum(grad_output, axis=0)
    down_grad = left_product(active, grad_low).astype(low)
    grad_hidden = (right_product(grad_low, down_w) * slope.astype(full)).astype(low)
    up_b_grad = jnp.sum(grad_hidden.astype(full), axis=0)
    output = jnp.where(valid, residual + plain(active, down_w) + down_b, 0.0).astype(low)
    up_grad = left_product(second, grad_hidden).astype(low)
    grad_norm_2, gain_2_grad, shift_2_grad = second_back(right_product(grad_hidden, up_w))
    grad_residual = grad_output + grad_norm_2
    branch = grad_residual.astype(low)
    out_b_grad = jnp.sum(branch.astype(full), axis=0)
    out_grad = left_product(attended, branch).astype(low)
    grad_attended = right_product(branch, out_w).astype(low)
    part, pair_gains = attend_back(
        mixed,
        column,
        pair_q,
        pair_k,
        attended,
        log_total,
        grad_attended,
        0,
        width // 128,
    )
    qkv_grad, qkv_b_grad = weight_grad(normed, part)
    gain_sums = jnp.sum(pair_gains, axis=0).reshape(2, 2, -1).sum(axis=1)
    grad_input, sums_1 = input_grad(tokens, gain_1.reshape(1, -1), grad_residual, [part], qkv_w)
    vectors = [
        qkv_b_grad.reshape(-1),
        out_b_grad,
        up_b_grad,
        down_b_grad,
        sums_1[0],
        sums_1[1],
        gain_2_grad,
        shift_2_grad,
        gain_sums[0],
        gain_sums[1],
    ]
    rows = jnp.concatenate([vector.reshape(groups, -1) for vector in vectors], axis=1)
    grads = [down_grad, up_grad, out_grad, qkv_grad]
    if kernels:
        grads, sums = total(grads, rows.reshape(groups, 1, -1), copies // 2, width, width)
    else:
        scatter = functools.partial(
            lax.psum_scatter, axis_name="fsdp", scatter_dimension=0, tiled=True
        )
        grads = [lax.psum(scatter(grad), ("z", "core")).astype(full) for grad in grads]
        sums = lax.psum(scatter(rows), ("z", "core")).reshape(-1)
    final, start = [], 0
    for vector in vectors:
        size = vector.shape[0] // groups
        final.append(sums[start : start + size])
        start += size
    return (
        output,
        grad_input,
        grads[3],
        final[0],
        grads[2],
        final[1],
        grads[1],
        final[2],
        grads[0],
        final[3],
        *final[4:],
    )


def solution(mesh):
    copies, groups = mesh.shape["dp"], mesh.shape["fsdp"]
    devices = mesh.devices.reshape(copies // 2, 2, groups)
    mesh = jax.sharding.Mesh(devices, ("z", "core", "fsdp"))
    rows = P(("z", "core", "fsdp"), None)
    matrix = P("fsdp", None)
    vector = P("fsdp")
    params = (matrix, vector) * 4 + (vector,) * 6
    return jax.shard_map(
        functools.partial(shards, groups, copies),
        mesh=mesh,
        in_specs=(rows, P(("z", "core", "fsdp")), rows) + params,
        out_specs=(rows, rows) + params,
        check_vma=False,
    )
```
